32 devices in a mesh: gx: 4 (over z), gy: 8 (over y, x, core).
Axes of the slice: x: 2, y: 2, z: 4, core: 2. Of those that a mesh axis runs over, the one named last changes fastest.
Arguments:
- forcing: float32 [16, 128, 512], P(None, 'gy', 'gx'), may hold values from -6 to 6
- pressure_in: float32 [16, 128, 512], P(None, 'gy', 'gx'), may hold values from -6 to 6
- x_coupling: float32 [16, 128, 512], P(None, 'gy', 'gx'), may hold values from 0.5 to 2000
- y_coupling: float32 [16, 128, 512], P(None, 'gy', 'gx'), may hold values from 0.5 to 2000
- z_coupling: float32 [16, 128, 512], P(None, 'gy', 'gx'), may hold values from 0.05 to 0.5
- damping: float32 [16, 128, 512], P(None, 'gy', 'gx'), may hold values from 0.2 to 2
Outputs:
- pressure: float32 [16, 128, 512], P(None, 'gy', 'gx')
- coarse_residual: float32 [8, 64, 256], P(None, 'gy', 'gx')
- coarse_correction: float32 [8, 64, 256], P(None, 'gy')
The draws below stay inside these ranges and needn't reach their ends.
All inputs are finite; a program needn't handle non-finite values.
Results may differ from the reference program's by a relative error of at most 0.0001.
Values sent between devices are 32-bit elements; how exact they have to be, the bound alone decides.
A program may use at most 128 MiB of HBM per device.

```python
import math
import jax
import jax.numpy as jnp
from jax import lax

NZ = 16
COARSE = 3
NX = 512
NY = 128


def coupling_draw(key, shape, flag_shape):
    base_key, flag_key = jax.random.split(key)
    base = jnp.exp(jax.random.uniform(base_key, shape, jnp.float32, math.log(0.5), math.log(2.0)))
    base = jnp.clip(base, 0.5, 2.0)
    strong = jax.random.uniform(flag_key, flag_shape, jnp.float32) < 0.5
    return base * jnp.where(strong, 1000.0, 1.0)


def draw_x_coupling(key, part):
    return coupling_draw(jax.random.fold_in(key, 11), (NZ, NY, NX), (NZ, NY, 1))


def draw_y_coupling(key, part):
    return coupling_draw(jax.random.fold_in(key, 23), (NZ, NY, NX), (NZ, 1, NX))


def block_scale(key, extent, pieces, smallest, top_value):
    loudness = 1.0
    for position, blocks in pieces:
        steps = jax.random.uniform(jax.random.fold_in(jax.random.fold_in(key, 6), position), (blocks,), jnp.float32, smallest / len(pieces), top_value / len(pieces))
        loudness = loudness * jnp.repeat(jnp.exp(steps), extent[position] // blocks).reshape((-1,) + (1,) * (len(extent) - 1 - position))
    return loudness


def gaussian(key, extent, scale, limit, cuts=(), kind=jnp.bfloat16):
    values = scale * jax.random.normal(key, extent, jnp.float32)
    if cuts:
        values = values * block_scale(key, extent, cuts, -0.22, 0.18)
    return jnp.clip(values, -limit, limit).astype(kind)


def setup_inputs(seed: int = 0) -> dict:
    key_of = jax.random.split(jax.random.key(seed), 7)
    forcing = gaussian(key_of[0], (NZ, NY, NX), 1.0, 6.0, ((1, 8), (2, 4)), jnp.float32)
    pressure_in = gaussian(key_of[1], (NZ, NY, NX), 1.0, 6.0, ((1, 8), (2, 4)), jnp.float32)
    x_coupling = draw_x_coupling(jax.random.fold_in(key_of[6], 71), 0)
    y_coupling = draw_y_coupling(jax.random.fold_in(key_of[6], 71), 0)
    z_coupling = jnp.clip(jnp.exp(math.log(0.5) - 2.3025851 * jax.random.uniform(key_of[4], (NZ, NY, NX), jnp.float32) ** block_scale(key_of[4], (NZ, NY, NX), ((1, 8), (2, 4)), -0.2, 0.2)), 0.05, 0.5)
    damping = jnp.clip(jnp.exp(math.log(2.0) - 2.3025851 * jax.random.uniform(key_of[5], (NZ, NY, NX), jnp.float32) ** block_scale(key_of[5], (NZ, NY, NX), ((1, 8), (2, 4)), -0.2, 0.2)), 0.2, 2.0)
    return {"forcing": forcing, "pressure_in": pressure_in, "x_coupling": x_coupling, "y_coupling": y_coupling, "z_coupling": z_coupling, "damping": damping}


RELAX = 0.8


def shifted(values, offset, axis_dim, filler):
    length = values.shape[axis_dim]
    if offset > 0:
        border = jnp.full_like(lax.slice_in_dim(values, 0, offset, axis=axis_dim), filler)
        return jnp.concatenate([border, lax.slice_in_dim(values, 0, length - offset, axis=axis_dim)], axis=axis_dim)
    amount = -offset
    border = jnp.full_like(lax.slice_in_dim(values, 0, amount, axis=axis_dim), filler)
    return jnp.concatenate([lax.slice_in_dim(values, amount, length, axis=axis_dim), border], axis=axis_dim)


def line_solve(low_band, diagonal, up_band, right_side, axis_dim):
    length = right_side.shape[axis_dim]
    stride = 1
    while stride < length:
        before = shifted(diagonal, stride, axis_dim, 1.0)
        after = shifted(diagonal, -stride, axis_dim, 1.0)
        weight_low = -low_band / before
        weight_up = -up_band / after
        new_diag = diagonal + weight_low * shifted(up_band, stride, axis_dim, 0.0) + weight_up * shifted(low_band, -stride, axis_dim, 0.0)
        new_right = right_side + weight_low * shifted(right_side, stride, axis_dim, 0.0) + weight_up * shifted(right_side, -stride, axis_dim, 0.0)
        low_band = weight_low * shifted(low_band, stride, axis_dim, 0.0)
        up_band = weight_up * shifted(up_band, -stride, axis_dim, 0.0)
        diagonal = new_diag
        right_side = new_right
        stride = stride * 2
    return right_side / diagonal


def top_masked(coupling):
    levels = coupling.shape[0]
    keep = (jnp.arange(levels) < levels - 1)[:, None, None]
    return jnp.where(keep, coupling, jnp.zeros_like(coupling))


def vertical(field, z_low, z_top):
    return z_low * shifted(field, 1, 0, 0.0) + z_top * shifted(field, -1, 0, 0.0)


def restrict(field):
    levels, rows, columns = field.shape
    blocks = field.reshape(levels // 2, 2, rows // 2, 2, columns // 2, 2)
    return jnp.sum(blocks, axis=(1, 3, 5)) * 0.125


def reference(forcing, pressure_in, x_coupling, y_coupling, z_coupling, damping):
    z_top = top_masked(z_coupling)
    z_low = shifted(z_top, 1, 0, 0.0)
    x_left = shifted(x_coupling, 1, 2, 0.0)
    y_left = shifted(y_coupling, 1, 1, 0.0)
    diagonal = x_left + x_coupling + y_left + y_coupling + z_low + z_top + damping
    field = pressure_in
    for repeat in range(2):
        source = forcing + y_left * shifted(field, 1, 1, 0.0) + y_coupling * shifted(field, -1, 1, 0.0) + vertical(field, z_low, z_top)
        field = line_solve(-x_left, diagonal, -x_coupling, source, 2)
        source = forcing + x_left * shifted(field, 1, 2, 0.0) + x_coupling * shifted(field, -1, 2, 0.0) + vertical(field, z_low, z_top)
        field = line_solve(-y_left, diagonal, -y_coupling, source, 1)
    applied = diagonal * field - x_left * shifted(field, 1, 2, 0.0) - x_coupling * shifted(field, -1, 2, 0.0) - y_left * shifted(field, 1, 1, 0.0) - y_coupling * shifted(field, -1, 1, 0.0) - vertical(field, z_low, z_top)
    coarse_residual = restrict(forcing - applied)
    coarse_x = restrict(x_coupling)
    coarse_y = restrict(y_coupling)
    coarse_z = restrict(z_coupling)
    coarse_damp = restrict(damping)
    cz_top = top_masked(coarse_z)
    cz_low = shifted(cz_top, 1, 0, 0.0)
    cx_left = shifted(coarse_x, 1, 2, 0.0)
    cy_left = shifted(coarse_y, 1, 1, 0.0)
    coarse_diag = cx_left + coarse_x + cy_left + coarse_y + cz_low + cz_top + coarse_damp
    correction = RELAX * coarse_residual / coarse_diag
    for repeat in range(COARSE - 1):
        applied_coarse = coarse_diag * correction - cx_left * shifted(correction, 1, 2, 0.0) - coarse_x * shifted(correction, -1, 2, 0.0) - cy_left * shifted(correction, 1, 1, 0.0) - coarse_y * shifted(correction, -1, 1, 0.0) - vertical(correction, cz_low, cz_top)
        correction = correction + RELAX * (coarse_residual - applied_coarse) / coarse_diag
    return (field, coarse_residual, correction)
```

```python
import functools

import jax
import jax.numpy as jnp
from jax import lax
from jax.experimental import pallas as pl
from jax.experimental.pallas import tpu as pltpu
from jax.sharding import PartitionSpec as P

COARSE = 3
RELAX = 0.8
CH = 16
CH2 = 4
MESH = pl.DeviceIdType.MESH


def up(v, s, fill):
    return jnp.concatenate([jnp.full_like(v[:s], fill), v[:-s]], axis=0)


def down(v, s, fill):
    return jnp.concatenate([v[s:], jnp.full_like(v[:s], fill)], axis=0)


def strides_of(length):
    out, s = [], 1
    while s < length:
        out.append(s)
        s *= 2
    return out


class Comm:
    def __init__(self, send_sems):
        self.sems, self.used, self.pending = send_sems, 0, []

    def send(self, src, dst, recv, dev, cond=None):
        copy = pltpu.make_async_remote_copy(
            src_ref=src, dst_ref=dst, send_sem=self.sems.at[self.used], recv_sem=recv,
            device_id=dev, device_id_type=MESH,
        )
        self.used += 1
        self.pending.append((copy, cond))
        if cond is None:
            copy.start()
        else:
            pl.when(cond)(copy.start)

    def finish(self):
        for copy, cond in self.pending:
            if cond is None:
                copy.wait_send()
            else:
                pl.when(cond)(copy.wait_send)


def await_recv(src, dst, sems, recv, dev, cond=None):
    copy = pltpu.make_async_remote_copy(
        src_ref=src, dst_ref=dst, send_sem=sems.at[0], recv_sem=recv, device_id=dev, device_id_type=MESH
    )
    if cond is None:
        copy.wait_recv()
    else:
        pl.when(cond)(copy.wait_recv)


def interface_factor(n, me, ls, le, rs, re, own, tau, sig, bet, tau2, sig2, dlt, kk):
    beta = jnp.zeros_like(ls[0])
    for d in range(n):
        bet[d] = beta
        w = 1.0 / (1.0 - ls[d] * beta)
        t = le[d] * w
        tau[d] = t
        s = t * beta
        sig[d] = s
        beta = re[d] + s * rs[d]
    delta = jnp.zeros_like(ls[0])
    for d in reversed(range(n)):
        dlt[d] = delta
        w = 1.0 / (1.0 - re[d] * delta)
        t = rs[d] * w
        tau2[d] = t
        s = t * delta
        sig2[d] = s
        delta = ls[d] + s * le[d]
    ls_m, le_m, rs_m, re_m = own
    beta, delta = bet[me], dlt[me]
    a, b = 1.0 - beta * ls_m, 1.0 - delta * re_m
    o1, o2 = beta * rs_m, delta * le_m
    inv = 1.0 / (a * b - o1 * o2)
    kk[0], kk[1], kk[2], kk[3] = b * inv, o1 * inv, a * inv, o2 * inv
    kk[4], kk[5] = beta, delta


def interface_solve(n, me, h_left, h_right, gs, ge, tau, tau2, kk):
    alpha = jnp.zeros_like(gs)
    for d in range(n - 1):
        alpha = jnp.where(d < me, h_left(d) + tau[d] * alpha, alpha)
    gamma = jnp.zeros_like(gs)
    for d in reversed(range(1, n)):
        gamma = jnp.where(d > me, h_right(d) + tau2[d] * gamma, gamma)
    p = alpha + kk[4] * gs
    q = gamma + kk[5] * ge
    return kk[0] * p + kk[1] * q, kk[2] * q + kk[3] * p


def kernel(nx, ny, f_hbm, p_hbm, x_hbm, y_hbm, z_hbm, d_hbm, op_ref, or_ref, oc_ref,
           xl_s, xc_s, yl_s, yc_s, zl_s, zt_s, fo_s, p_s, ri_s, g_s, q_s, zds_s,
           lx_s, rx_s, wx_s, ly_s, ry_s, wy_s,
           sx0, sy0, hx, hyd, hyu, xb, sxb, ycb, syc, yb, shy,
           xtau, xsig, xbet, xtau2, xsig2, xdlt, xkk,
           ytau, ysig, ybet, ytau2, ysig2, ydlt, ykk,
           pair_s, cown, cbuf, rown, rbuf, fown, fbuf, flip,
           ssem, s0, sx, syco, sy, sc, sr, sf, ins, sin):
    Y, Z, X = xc_s.shape
    CY, CZ = Y // 2, Z // 2
    gx, gy = lax.axis_index("gx"), lax.axis_index("gy")
    has_w, has_e = gx > 0, gx < nx - 1
    has_n, has_s = gy > 0, gy < ny - 1
    west, east = jnp.maximum(gx - 1, 0), jnp.minimum(gx + 1, nx - 1)
    north, south = jnp.maximum(gy - 1, 0), jnp.minimum(gy + 1, ny - 1)
    x_peers = [lax.rem(gx + o, nx) for o in range(1, nx)]
    y_peers = [lax.rem(gy + o, ny) for o in range(1, ny)]

    loads = []
    for m, ref in enumerate((x_hbm, y_hbm, p_hbm, z_hbm, d_hbm, f_hbm)):
        loads.append(pltpu.make_async_copy(ref, ins.at[m], sin.at[m]))
        loads[m].start()
    x_ref, y_ref, p_ref, z_ref, d_ref, f_ref = [ins.at[m] for m in range(6)]

    barrier = pltpu.get_barrier_semaphore()

    def greet(dev):
        pl.semaphore_signal(barrier, inc=1, device_id=dev, device_id_type=MESH)

    for i in x_peers:
        greet((i, gy))
    for j in y_peers:
        greet((gx, j))

    corners = [
        (jnp.logical_and(h, v), (i, j)) for h, i in ((has_w, west), (has_e, east)) for v, j in ((has_n, north), (has_s, south))
    ]
    for cond, dev in corners:
        pl.when(cond)(functools.partial(greet, dev))

    lane = lax.broadcasted_iota(jnp.int32, (Z, X), 1)
    level = lax.broadcasted_iota(jnp.int32, (Z, X), 0)
    lane3 = lax.broadcasted_iota(jnp.int32, (1, 1, X), 2)

    def rows(ref, j):
        return ref[pl.ds(j, Z, stride=Y), :]

    packed = jnp.zeros((Z, X), jnp.float32)
    for m in range(3):
        loads[m].wait()
    for j in range(Y):
        v = rows(x_ref, j)
        xc_s[j] = v
        packed = jnp.where(lane == j, v[:, X - 1:], packed)
        yc_s[j] = rows(y_ref, j)
        p_s[j] = rows(p_ref, j)
    for m in range(3, 6):
        loads[m].wait()
    for j in range(Y):
        zv = jnp.where(level < Z - 1, rows(z_ref, j), 0.0)
        zt_s[j] = zv
        zl_s[j] = pltpu.roll(zv, 1, 0)
        fo_s[j] = rows(f_ref, j)
    sx0[...] = packed
    sy0[0] = yc_s[Y - 1]
    sy0[1] = p_s[Y - 1]
    sy0[2] = p_s[0]

    @pl.when(jnp.logical_not(has_w))
    def _():
        hx[...] = jnp.zeros_like(hx)
        cbuf[0] = jnp.zeros_like(cbuf[0])
        rbuf[0] = jnp.zeros_like(rbuf[0])

    @pl.when(jnp.logical_not(has_e))
    def _():
        cbuf[2] = jnp.zeros_like(cbuf[2])
        rbuf[2] = jnp.zeros_like(rbuf[2])

    @pl.when(jnp.logical_not(has_n))
    def _():
        hyd[...] = jnp.zeros_like(hyd)
        for d in range(3):
            cbuf[d, :, 0:3] = jnp.zeros_like(cbuf[d, :, 0:3])
            rbuf[d, 0:2] = jnp.zeros_like(rbuf[d, 0:2])

    @pl.when(jnp.logical_not(has_s))
    def _():
        hyu[...] = jnp.zeros_like(hyu)
        for d in range(3):
            cbuf[d, :, 3 + CY:] = jnp.zeros_like(cbuf[d, :, 3 + CY:])
            rbuf[d, 2 + CY:] = jnp.zeros_like(rbuf[d, 2 + CY:])

    n_corners = sum(cond.astype(jnp.int32) for cond, _ in corners)
    pl.semaphore_wait(barrier, (nx - 1) + (ny - 1) + n_corners)

    comm = Comm(ssem)
    comm.send(sx0, hx, s0.at[0], (east, gy), has_e)
    comm.send(sy0.at[0:2], hyd, s0.at[1], (gx, south), has_s)
    comm.send(sy0.at[2:3], hyu, s0.at[2], (gx, north), has_n)

    half = X // 2
    off = half // 2
    ii = lax.broadcasted_iota(jnp.int32, (X, X), 0)
    mm = lax.broadcasted_iota(jnp.int32, (X, X), 1)

    def selection(step, start):
        target = lax.rem((ii + (step + 2)) // 2 - 1 + start + X, X)
        return jnp.where(mm == target, 0.125, 0.0)

    def pairs(field):
        v = field.reshape(CY, 2, Z, X)
        pair_s[...] = (v[:, 0] + v[:, 1]).reshape(CY * Z, X)
        return pair_s[pl.ds(0, CY * CZ, stride=2), :] + pair_s[pl.ds(1, CY * CZ, stride=2), :]

    def mxu(a, b):
        return jnp.dot(a, b, precision=lax.Precision.HIGHEST, preferred_element_type=jnp.float32)

    here, there = selection(0, off), selection(0, half + off)
    sel2 = jnp.concatenate([here, there], axis=0)
    zfull = jnp.stack([rows(z_ref, j) for j in range(Y)])
    damp = jnp.stack([rows(d_ref, j) for j in range(Y)])
    for m, (u, v) in enumerate(((xc_s[...], yc_s[...]), (zfull, damp))):
        both_pairs = jnp.concatenate([pairs(u), pairs(v)], axis=1)
        cown[m] = mxu(both_pairs, sel2).reshape(CY, CZ, X)

    await_recv(sx0, hx, ssem, s0.at[0], (east, gy), has_w)
    await_recv(sy0.at[0:2], hyd, ssem, s0.at[1], (gx, south), has_n)
    await_recv(sy0.at[2:3], hyu, ssem, s0.at[2], (gx, north), has_s)

    xc, yc = xc_s[...], yc_s[...]
    border = jnp.stack([jnp.broadcast_to(hx[:, j:j + 1], (Z, X)) for j in range(Y)])
    xl = jnp.where(lane3 == 0, border, pltpu.roll(xc, 1, 2))
    xl_s[...] = xl
    yl = jnp.concatenate([hyd[0:1], yc[:-1]], axis=0)
    yl_s[...] = yl
    zd = zl_s[...] + zt_s[...] + damp
    xs, ys = xl + xc, yl + yc
    ri = 1.0 / (xs + ys + zd)
    ri_s[...] = ri

    a, c, e = yl * ri, yc * ri, (xs + zd) * ri
    for n, s in enumerate(strides_of(Y)):
        a2, c2 = a * up(a, s, 1.0), c * down(c, s, 1.0)
        e2 = e + a * up(e, s, 0.0) + c * down(e, s, 0.0)
        inv = 1.0 / (a2 + c2 + e2)
        wy_s[n, 0], wy_s[n, 1], wy_s[n, 2] = inv, a * inv, c * inv
        a, c, e = a2 * inv, c2 * inv, e2 * inv
    ly_s[...], ry_s[...] = a, c
    syc[0], syc[1], syc[2], syc[3] = a[0], a[Y - 1], c[0], c[Y - 1]
    ycb[gy] = syc[...]
    for j in y_peers:
        comm.send(syc, ycb.at[gy], syco.at[gy], (gx, j))

    def y_local(r):
        for n, s in enumerate(strides_of(Y)):
            r = wy_s[n, 0] * r + wy_s[n, 1] * up(r, s, 0.0) + wy_s[n, 2] * down(r, s, 0.0)
        return r

    def z_terms(v):
        return zl_s[...] * pltpu.roll(v, 1, 1) + zt_s[...] * pltpu.roll(v, Z - 1, 1)

    def x_source(v, above, below):
        lower = jnp.concatenate([above[None], v[:-1]], axis=0)
        upper = jnp.concatenate([v[1:], below[None]], axis=0)
        return (fo_s[...] + yl_s[...] * lower + yc_s[...] * upper + z_terms(v)) * ri_s[...]

    def pack_edges(into, at, v, start):
        for j in range(v.shape[0]):
            into = jnp.where(lane == start + at + j, v[j][:, 0:1], into)
            into = jnp.where(lane == start + at + Y + j, v[j][:, X - 1:], into)
        return into

    ones = jnp.ones((1, 1, X), jnp.float32)
    packed = jnp.zeros((Z, X), jnp.float32)
    zds_s[...] = (yl + yc + zd) * ri
    g_s[...] = x_source(p_s[...], hyd[1], hyu[0])
    for lo in range(0, Y, CH):
        part = slice(lo, lo + CH)
        a, c = xl_s[part] * ri_s[part], xc_s[part] * ri_s[part]
        e, r = zds_s[part], g_s[part]
        for n, s in enumerate(strides_of(X)):
            low, high = lane3 >= s, lane3 < X - s
            a_in, c_in = jnp.where(low, a, 0.0), jnp.where(high, c, 0.0)
            a2 = a * jnp.where(low, pltpu.roll(a, s, 2), ones)
            c2 = c * jnp.where(high, pltpu.roll(c, X - s, 2), ones)
            e2 = e + a_in * pltpu.roll(e, s, 2) + c_in * pltpu.roll(e, X - s, 2)
            inv = 1.0 / (a2 + c2 + e2)
            wa, wc = a_in * inv, c_in * inv
            wx_s[n, 0, part], wx_s[n, 1, part], wx_s[n, 2, part] = inv, wa, wc
            r = inv * r + wa * pltpu.roll(r, s, 2) + wc * pltpu.roll(r, X - s, 2)
            a, c, e = a2 * inv, c2 * inv, e2 * inv
        g_s[part], lx_s[part], rx_s[part] = r, a, c
        for q, v in enumerate((r, a, c)):
            packed = pack_edges(packed, lo, v, 2 * q * Y)

    def x_exchange(m, packed):
        sxb[m] = packed
        xb[m, gx] = packed
        for i in x_peers:
            comm.send(sxb.at[m], xb.at[m, gx], sx.at[m, gx], (i, gy))

    x_exchange(0, packed)

    def halo_exchange(src, dst, sems, top, lead, starting):
        def part(ref, lo, n):
            return ref.at[(slice(None),) * lead + (pl.ds(lo, n),)]

        def rows_of(slot):
            return dst.at[slot]

        for slot, i, ok, back in ((0, west, has_w, 2), (1, gx, None, 1), (2, east, has_e, 0)):
            both_ok = (lambda c: c) if ok is None else (lambda c, ok=ok: jnp.logical_and(c, ok))
            if starting:
                if ok is not None:
                    comm.send(src, part(rows_of(back), top, CY), sems.at[0, back], (i, gy), ok)
                comm.send(part(src, CY - top, top), part(rows_of(back), 0, top), sems.at[1, back], (i, south), both_ok(has_s))
                comm.send(part(src, 0, 2), part(rows_of(back), top + CY, 2), sems.at[2, back], (i, north), both_ok(has_n))
            else:
                if ok is not None:
                    await_recv(src, part(rows_of(slot), top, CY), ssem, sems.at[0, slot], (i, gy), ok)
                await_recv(part(src, CY - top, top), part(rows_of(slot), 0, top), ssem, sems.at[1, slot], (i, south), both_ok(has_n))
                await_recv(part(src, 0, 2), part(rows_of(slot), top + CY, 2), ssem, sems.at[2, slot], (i, north), both_ok(has_s))

    for m in range(2):
        cbuf[1, m, 3:3 + CY] = cown[m]
    halo_exchange(cown, cbuf, sc, 3, 1, True)

    for j in y_peers:
        await_recv(syc, ycb.at[j], ssem, syco.at[j], (gx, j))
    interface_factor(
        ny, gy, *[[ycb[d, m] for d in range(ny)] for m in range(4)], [syc[m] for m in range(4)],
        ytau, ysig, ybet, ytau2, ysig2, ydlt, ykk,
    )

    def slot(v, m):
        return v if m == 0 else pltpu.roll(v, X - m * Y, 1)

    def x_collect(m):
        for i in x_peers:
            await_recv(sxb.at[m], xb.at[m, i], ssem, sx.at[m, i], (i, gy))
        if m == 0:
            coefs = [[slot(xb[0, d], 2 + q) for d in range(nx)] for q in range(4)]
            own = [slot(sxb[0], 2 + q) for q in range(4)]
            interface_factor(nx, gx, *coefs, own, xtau, xsig, xbet, xtau2, xsig2, xdlt, xkk)
        gs = [xb[m, d] for d in range(nx)]
        ge = [slot(v, 1) for v in gs]
        return interface_solve(
            nx, gx, lambda d: ge[d] + xsig[d] * gs[d], lambda d: gs[d] + xsig2[d] * ge[d],
            sxb[m], slot(sxb[m], 1), xtau, xtau2, xkk,
        )

    def spread(v):
        return jnp.stack([jnp.broadcast_to(v[:, j:j + 1], (Z, X)) for j in range(Y)])

    def y_half(m):
        left, right = x_collect(m)
        left, right = spread(left), spread(right)
        v = g_s[...] + lx_s[...] * left + rx_s[...] * right
        q_s[...] = v
        before = jnp.where(lane3 == 0, left, pltpu.roll(v, 1, 2))
        after = jnp.where(lane3 == X - 1, right, pltpu.roll(v, X - 1, 2))
        r = (fo_s[...] + xl_s[...] * before + xc_s[...] * after + z_terms(v)) * ri_s[...]
        r = y_local(r)
        g_s[...] = r
        gs, ge = r[0], r[Y - 1]
        shy[m, 0] = ge + ysig[gy] * gs
        shy[m, 1] = gs + ysig2[gy] * ge
        yb[m, gy] = shy[m, 0]
        for j in y_peers:
            side = jnp.where(j > gy, 0, 1)
            comm.send(shy.at[m, side], yb.at[m, gy], sy.at[m, gy], (gx, j))
        for j in y_peers:
            await_recv(shy.at[m, 0], yb.at[m, j], ssem, sy.at[m, j], (gx, j))
        above, below = interface_solve(
            ny, gy, lambda d: yb[m, d], lambda d: yb[m, d], g_s[0], g_s[Y - 1], ytau, ytau2, ykk
        )
        return g_s[...] + ly_s[...] * above[None] + ry_s[...] * below[None], above, below

    v, above, below = y_half(0)
    g_s[...] = x_source(v, above, below)
    packed = jnp.zeros((Z, X), jnp.float32)
    for lo in range(0, Y, CH2):
        part = slice(lo, lo + CH2)
        r = g_s[part]
        for n, s in enumerate(strides_of(X)):
            r = wx_s[n, 0, part] * r + wx_s[n, 1, part] * pltpu.roll(r, s, 2) + wx_s[n, 2, part] * pltpu.roll(r, X - s, 2)
        g_s[part] = r
        packed = pack_edges(packed, lo, r, 0)
    x_exchange(1, packed)
    v, above, below = y_half(1)

    change = v - q_s[...]
    stacked = jnp.concatenate(
        [pairs(xc_s[...] * change), pairs(xl_s[...] * change), pairs(z_terms(change))], axis=1
    )
    sel3 = jnp.concatenate([selection(1, off), selection(-1, off), here], axis=0)
    partial = mxu(stacked, sel3).reshape(CY, CZ, X)
    rown[...] = partial
    rbuf[1, 2:2 + CY] = partial
    halo_exchange(rown, rbuf, sr, 2, 0, True)
    for j in range(Y):
        op_ref[pl.ds(j, Z, stride=Y), :] = v[j]

    halo_exchange(cown, cbuf, sc, 3, 1, False)

    centre = jnp.logical_and(lane3 >= off, lane3 < off + half)
    wide = lane3

    def planes(m):
        w, o, e = cbuf[0, m], cbuf[1, m], cbuf[2, m]
        near = jnp.where(centre, o, pltpu.roll(jnp.where(lane3 >= half, w, e), half, 2))
        far = jnp.where(centre, pltpu.roll(o, half, 2), jnp.where(lane3 < half, w, e))
        return near, far

    cx, cy = planes(0)
    cz, cd = planes(1)
    czl = lax.broadcasted_iota(jnp.int32, (1, CZ, 1), 1)
    H = CY + 4
    row = lax.broadcasted_iota(jnp.int32, (H, 1, 1), 0)
    inside = jnp.logical_and(
        jnp.logical_or(row >= 2, has_n), jnp.logical_or(row < 2 + CY, has_s)
    )
    inside = jnp.logical_and(
        inside,
        jnp.logical_and(jnp.logical_or(lane3 >= off, has_w), jnp.logical_or(lane3 < off + half, has_e)),
    )
    cyl, cy = cy[:H], cy[1:]
    cx, cz, cd = cx[1:], cz[1:], cd[1:]
    cd = jnp.where(inside, cd, 1.0)
    ct = jnp.where(czl < CZ - 1, cz, 0.0)
    cl = pltpu.roll(ct, 1, 1)
    cxl = pltpu.roll(cx, 1, 2)
    diag = cxl + cx + cyl + cy + cl + ct + cd
    scale = RELAX / diag

    halo_exchange(rown, rbuf, sr, 2, 0, False)
    w, e = pltpu.roll(rbuf[0], half, 2), pltpu.roll(rbuf[2], half, 2)
    res = (
        rbuf[1]
        + jnp.where(jnp.logical_and(lane3 >= off - 2, lane3 <= off), w, 0.0)
        + jnp.where(jnp.logical_and(lane3 >= off + half - 1, lane3 <= off + half + 1), e, 0.0)
    )
    res = jnp.where(inside, res, 0.0)
    cor = scale * res
    for repeat in range(COARSE - 1):
        lo, n = 1 + repeat, H - 2 - 2 * repeat
        cut = slice(lo, lo + n)
        mid, above, below = cor[1:-1], cor[:-2], cor[2:]
        applied = (
            diag[cut] * mid
            - cxl[cut] * pltpu.roll(mid, 1, 2)
            - cx[cut] * pltpu.roll(mid, X - 1, 2)
            - cyl[cut] * above
            - cy[cut] * below
            - cl[cut] * pltpu.roll(mid, 1, 1)
            - ct[cut] * pltpu.roll(mid, CZ - 1, 1)
        )
        cor = jnp.where(inside[cut], mid + scale[cut] * (res[cut] - applied), 0.0)
    hj = CY // 2
    mine = jnp.where(lane3 < half, pltpu.roll(cor[:hj], X - off, 2), pltpu.roll(cor[hj:], off, 2))
    fown[...] = mine
    fbuf[gx] = mine
    for i in x_peers:
        comm.send(fown, fbuf.at[gx], sf.at[gx], (i, gy))
    own = pltpu.roll(res[2:2 + CY], X - off, 2)
    for j in range(CY):
        flip[pl.ds(j, CZ, stride=CY), :] = own[j]
    or_ref[...] = flip[0:CZ * CY, :half]
    for i in x_peers:
        await_recv(fown, fbuf.at[i], ssem, sf.at[i], (i, gy))
    for t in range(nx // 2):
        u, v = fbuf[2 * t], fbuf[2 * t + 1]
        top = jnp.where(lane3 < half, u, pltpu.roll(v, half, 2))
        low = jnp.where(lane3 < half, pltpu.roll(u, half, 2), v)
        base = (t + 1) * CZ * CY
        for j in range(CY):
            flip[pl.ds(base + j, CZ, stride=CY), :] = top[j] if j < hj else low[j - hj]
        oc_ref[:, t * X:(t + 1) * X] = flip[base:base + CZ * CY, :]
    comm.finish()


def put(*refs):
    sems = refs[6]
    give = [pltpu.make_async_copy(refs[m], refs[3 + m], sems.at[m]) for m in range(3)]
    for copy in give:
        copy.start()
    for copy in give:
        copy.wait()


def body(nx, ny, *args):
    Z, Y, X = args[0].shape
    CZ, CY = Z // 2, Y // 2
    flat = [v.reshape(Z * Y, X) for v in args]
    f32 = jnp.float32

    def vm(*shape):
        return pltpu.VMEM(shape, f32)

    block = (Y, Z, X)
    nsx, nsy = len(strides_of(X)), len(strides_of(Y))
    tables_x = [vm(nx, Z, X) for _ in range(6)] + [vm(6, Z, X)]
    tables_y = [vm(ny, Z, X) for _ in range(6)] + [vm(6, Z, X)]
    sends = 3 + (ny - 1) * 3 + (nx - 1) * 3 + 8 * 2
    dma = pltpu.SemaphoreType.DMA
    scratch = (
        [vm(*block) for _ in range(12)]
        + [vm(*block), vm(*block), vm(nsx, 3, *block), vm(*block), vm(*block), vm(nsy, 3, *block)]
        + [vm(Z, X), vm(3, Z, X), vm(Z, X), vm(2, Z, X), vm(1, Z, X)]
        + [vm(2, nx, Z, X), vm(2, Z, X), vm(ny, 4, Z, X), vm(4, Z, X), vm(2, ny, Z, X), vm(2, 2, Z, X)]
        + tables_x + tables_y
        + [vm(CY * Z, X), vm(2, CY, CZ, X), vm(3, 2, CY + 5, CZ, X), vm(CY, CZ, X), vm(3, CY + 4, CZ, X),
           vm(CY // 2, CZ, X), vm(nx, CY // 2, CZ, X), vm((nx // 2 + 1) * CZ * CY, X)]
        + [dma((sends,)), dma((3,)), dma((2, nx)), dma((ny,)), dma((2, ny)), dma((3, 3)), dma((3, 3)), dma((nx,))]
        + [vm(6, Z * Y, X), dma((6,))]
    )
    p, r, c = pl.pallas_call(
        functools.partial(kernel, nx, ny),
        out_shape=(
            vm(Z * Y, X),
            vm(CZ * CY, X // 2),
            vm(CZ * CY, nx * X // 2),
        ),
        in_specs=[pl.BlockSpec(memory_space=pltpu.HBM)] * 6,
        out_specs=[pl.BlockSpec(memory_space=pltpu.VMEM)] * 3,
        scratch_shapes=scratch,
        compiler_params=pltpu.CompilerParams(
            collective_id=0, has_side_effects=True, vmem_limit_bytes=60000000
        ),
    )(*flat)
    p, r, c = pl.pallas_call(
        put,
        out_shape=tuple(jax.ShapeDtypeStruct(v.shape, f32) for v in (p, r, c)),
        in_specs=[pl.BlockSpec(memory_space=pltpu.VMEM)] * 3,
        out_specs=[pl.BlockSpec(memory_space=pltpu.HBM)] * 3,
        scratch_shapes=[dma((3,))],
    )(*[pltpu.with_memory_space_constraint(v, pltpu.VMEM) for v in (p, r, c)])
    return p.reshape(Z, Y, X), r.reshape(CZ, CY, X // 2), c.reshape(CZ, CY, nx * X // 2)


def solution(mesh):
    nx, ny = mesh.shape["gx"], mesh.shape["gy"]
    split = P(None, "gy", "gx")
    return jax.shard_map(
        functools.partial(body, nx, ny),
        mesh=mesh,
        in_specs=(split,) * 6,
        out_specs=(split, split, P(None, "gy", None)),
        check_vma=False,
    )
```

```python
import functools

import jax
import jax.numpy as jnp
from jax import lax
from jax.experimental import pallas as pl
from jax.experimental.pallas import tpu as pltpu
from jax.sharding import PartitionSpec as P

COARSE = 3
RELAX = 0.8
CH = 4
LE, LS, RE, RS, GS, GE, XC = range(7)
SLOTS = 8
MESH = pl.DeviceIdType.MESH


def strides_of(length):
    out, s = [], 1
    while s < length:
        out.append(s)
        s *= 2
    return out


class Comm:
    def __init__(self, send_sems):
        self.sems, self.used, self.pending = send_sems, 0, []

    def send(self, src, dst, recv, dev, cond=None):
        copy = pltpu.make_async_remote_copy(
            src_ref=src, dst_ref=dst, send_sem=self.sems.at[self.used], recv_sem=recv,
            device_id=dev, device_id_type=MESH,
        )
        self.used += 1
        self.pending.append((copy, cond))
        if cond is None:
            copy.start()
        else:
            pl.when(cond)(copy.start)

    def finish(self):
        for copy, cond in self.pending:
            if cond is None:
                copy.wait_send()
            else:
                pl.when(cond)(copy.wait_send)


def await_recv(src, dst, sems, recv, dev, cond=None):
    copy = pltpu.make_async_remote_copy(
        src_ref=src, dst_ref=dst, send_sem=sems.at[0], recv_sem=recv, device_id=dev, device_id_type=MESH
    )
    if cond is None:
        copy.wait_recv()
    else:
        pl.when(cond)(copy.wait_recv)


def farthest_first(me, n):
    out = []
    for k in range(n - 1):
        down = jnp.where(n - 1 - k > me, n - 1 - k, n - 2 - k)
        up = jnp.where(k < me, k, k + 1)
        out.append(jnp.where(2 * me < n, down, up))
    return out


def flipped(me, n):
    if n & (n - 1):
        return [lax.rem(me + o, n) for o in range(1, n)]
    out = []
    for mask in range(n - 1, 0, -1):
        peer, bit = 0, 1
        while bit < n:
            value = lax.rem(me // bit, 2)
            peer = peer + bit * (1 - value if mask & bit else value)
            bit *= 2
        out.append(peer)
    return out


def interface_factor(n, me, ls, le, rs, re, own, tau, sig, bet, tau2, sig2, dlt, kk):
    beta = jnp.zeros_like(ls[0])
    for d in range(n):
        bet[d] = beta
        w = 1.0 / (1.0 - ls[d] * beta)
        t = le[d] * w
        tau[d] = t
        s = t * beta
        sig[d] = s
        beta = re[d] + s * rs[d]
    delta = jnp.zeros_like(ls[0])
    for d in reversed(range(n)):
        dlt[d] = delta
        w = 1.0 / (1.0 - re[d] * delta)
        t = rs[d] * w
        tau2[d] = t
        s = t * delta
        sig2[d] = s
        delta = ls[d] + s * le[d]
    ls_m, le_m, rs_m, re_m = own
    beta, delta = bet[me], dlt[me]
    a, b = 1.0 - beta * ls_m, 1.0 - delta * re_m
    o1, o2 = beta * rs_m, delta * le_m
    inv = 1.0 / (a * b - o1 * o2)
    kk[0], kk[1], kk[2], kk[3] = b * inv, o1 * inv, a * inv, o2 * inv
    kk[4], kk[5] = beta, delta


def interface_solve(n, me, h_left, h_right, gs, ge, tau, tau2, kk):
    alpha = jnp.zeros_like(gs)
    for d in range(n - 1):
        alpha = jnp.where(d < me, h_left(d) + tau[d] * alpha, alpha)
    gamma = jnp.zeros_like(gs)
    for d in reversed(range(1, n)):
        gamma = jnp.where(d > me, h_right(d) + tau2[d] * gamma, gamma)
    p = alpha + kk[4] * gs
    q = gamma + kk[5] * ge
    return kk[0] * p + kk[1] * q, kk[2] * q + kk[3] * p


def chain_factor(n, me, ls, le, rs, re, xc, own, rho, tau, sig, bet, tau2, sig2, scl, dlt, kk):
    one, zero = jnp.ones_like(ls[0]), jnp.zeros_like(ls[0])
    beta = zero
    for d in range(n):
        r = zero if d == 0 else xc[d - 1]
        b = one if d == 0 else 1.0 - r * (1.0 - beta)
        rho[d], bet[d] = r, b
        w = 1.0 / (1.0 - ls[d] * b)
        t = le[d] * w
        tau[d] = t * r
        s = t * b
        sig[d] = s
        beta = re[d] + s * rs[d]
    delta = zero
    for d in reversed(range(n)):
        dlt[d] = delta
        t = rs[d] / (1.0 - re[d] * delta)
        s = t * delta
        q = ls[d] + s * le[d]
        if d > 0:
            v = 1.0 / (1.0 - q + q * xc[d - 1])
            scl[d], tau2[d], sig2[d] = v, v * t, v * s
            delta = v * q * xc[d - 1]
        else:
            scl[d], tau2[d], sig2[d] = zero, zero, zero
    ls_m, le_m, rs_m, re_m = own
    beta, delta = bet[me], dlt[me]
    a, b = 1.0 - beta * ls_m, 1.0 - delta * re_m
    o1, o2 = beta * rs_m, delta * le_m
    inv = 1.0 / (a * b - o1 * o2)
    kk[0], kk[1], kk[2], kk[3] = b * inv, o1 * inv, a * inv, o2 * inv


def kernel(nx, ny, f_hbm, p_hbm, x_hbm, y_hbm, z_hbm, d_hbm, op_ref, or_ref, oc_ref,
           xl_s, xc_s, yl_s, yc_s, zl_s, zt_s, zd_s, fo_s, p_s, r_s, g_s, q_s,
           lx_s, rx_s, ix_s, wx_s, ly_s, ry_s, iy_s, wy_s,
           sx0, sy0, hx, hyd, hyu, xb, sxb, xb1, sx1, ycb, syc, yb, shy,
           xown, xrho, xtau, xsig, xbet, xtau2, xsig2, xscl, xdlt, xkk,
           ytau, ysig, ybet, ytau2, ysig2, ydlt, ykk, ysc,
           pair_s, cown, cbuf, rown, nbuf, ebuf, sedge, fown, fbuf, flip,
           ssem, s0, sx, syco, sy, sc, sr, sf, ins, sin):
    Y, Z, X = xc_s.shape
    CY, CZ = Y // 2, Z // 2
    f32 = jnp.float32
    gx, gy = lax.axis_index("gx"), lax.axis_index("gy")
    has_w, has_e = gx > 0, gx < nx - 1
    has_n, has_s = gy > 0, gy < ny - 1
    west, east = jnp.maximum(gx - 1, 0), jnp.minimum(gx + 1, nx - 1)
    north, south = jnp.maximum(gy - 1, 0), jnp.minimum(gy + 1, ny - 1)
    x_peers = farthest_first(gx, nx)
    y_peers = flipped(gy, ny)

    loads = []
    for m, ref in enumerate((x_hbm, y_hbm, p_hbm, z_hbm, d_hbm, f_hbm)):
        loads.append(pltpu.make_async_copy(ref, ins.at[m], sin.at[m]))
        loads[m].start()
    x_ref, y_ref, p_ref, z_ref, d_ref, f_ref = [ins.at[m] for m in range(6)]

    barrier = pltpu.get_barrier_semaphore()

    def greet(dev):
        pl.semaphore_signal(barrier, inc=1, device_id=dev, device_id_type=MESH)

    for i in x_peers:
        greet((i, gy))
    for j in y_peers:
        greet((gx, j))

    corners = [
        (jnp.logical_and(h, v), (i, j)) for h, i in ((has_w, west), (has_e, east)) for v, j in ((has_n, north), (has_s, south))
    ]
    for cond, dev in corners:
        pl.when(cond)(functools.partial(greet, dev))

    lane = lax.broadcasted_iota(jnp.int32, (Z, X), 1)
    level = lax.broadcasted_iota(jnp.int32, (Z, X), 0)
    lane3 = lax.broadcasted_iota(jnp.int32, (1, 1, X), 2)
    item, group = lane % SLOTS, lane // SLOTS

    def rows(ref, j):
        return ref[pl.ds(j, Z, stride=Y), :]

    for m in range(3):
        loads[m].wait()
    packed = jnp.zeros((Z, X), f32)
    for j in range(Y):
        v = rows(x_ref, j)
        xc_s[j] = v
        packed = jnp.where(lane == SLOTS * j + XC, v[:, X - 1:], packed)
    sx0[...] = packed
    sy0[0] = rows(y_ref, Y - 1)
    sy0[1] = rows(p_ref, Y - 1)
    sy0[2] = rows(p_ref, 0)

    n_corners = sum(cond.astype(jnp.int32) for cond, _ in corners)
    pl.semaphore_wait(barrier, (nx - 1) + (ny - 1) + n_corners)

    comm = Comm(ssem)
    comm.send(sy0.at[0:2], hyd, s0.at[1], (gx, south), has_s)
    comm.send(sy0.at[2:3], hyu, s0.at[2], (gx, north), has_n)
    comm.send(sx0, hx, s0.at[0], (east, gy), has_e)

    for j in range(Y):
        yc_s[j] = rows(y_ref, j)
        p_s[j] = rows(p_ref, j)
    for m in range(3, 6):
        loads[m].wait()
    for j in range(Y):
        zv = jnp.where(level < Z - 1, rows(z_ref, j), 0.0)
        zt_s[j] = zv
        zl = pltpu.roll(zv, 1, 0)
        zl_s[j] = zl
        zd_s[j] = zv + zl + rows(d_ref, j)
        fo_s[j] = rows(f_ref, j)

    first, last = lane3 == 0, lane3 == X - 1

    def x_factor(lo, hi, above):
        part = slice(lo, hi)
        c = xc_s[part]
        a = jnp.where(first, 1.0, pltpu.roll(c, 1, 2))
        e = above + yc_s[part] + zd_s[part]
        for n, s in enumerate(strides_of(X)):
            low, high = lane3 >= s, lane3 < X - s
            inv = 1.0 / (a + c + e)
            ai, ci = a * inv, c * inv
            am, cm = jnp.where(low, ai, 0.0), jnp.where(high, ci, 0.0)
            wx_s[n, 0, part], wx_s[n, 1, part] = cm, am
            a = a * jnp.where(low, pltpu.roll(ai, s, 2), 1.0)
            c = c * jnp.where(high, pltpu.roll(ci, X - s, 2), 1.0)
            e = e + pltpu.roll(cm * e, s, 2) + pltpu.roll(am * e, X - s, 2)
        inv = 1.0 / (a + c + e)
        ix_s[part], lx_s[part], rx_s[part] = inv, a * inv, c * inv

    def z_terms(v, part):
        return zl_s[part] * pltpu.roll(v, 1, 1) + zt_s[part] * pltpu.roll(v, Z - 1, 1)

    def x_source(lo, hi, lower, upper):
        part = slice(lo, hi)
        r_s[part] = fo_s[part] + yl_s[part] * lower + yc_s[part] * upper + z_terms(p_s[part], part)

    ends = jnp.logical_or(lane == 0, lane == X - 1)

    def edge_sums(j):
        r = r_s[j]
        return jnp.sum(lx_s[j] * r, axis=1, keepdims=True), jnp.sum(rx_s[j] * r, axis=1, keepdims=True)

    def pack_row(packed, j):
        gs, ge = edge_sums(j)
        v = jnp.where(ends, lx_s[j], pltpu.roll(rx_s[j], 2, 1))
        v = jnp.where(item < GS, pltpu.roll(v, SLOTS * j + 1, 1), jnp.where(item == GS, gs, ge))
        return jnp.where(group == j, v, packed)

    yl_s[1:Y] = yc_s[0:Y - 1]
    packed = jnp.zeros((Z, X), f32)
    for lo in range(0, Y, CH):
        hi = lo + CH
        at = max(lo, 1)
        x_factor(at, hi, yl_s[at:hi])
        at, to = max(lo, 1), min(hi, Y - 1)
        x_source(at, to, p_s[at - 1:to - 1], p_s[at + 1:to + 1])
        for j in range(at, to):
            packed = pack_row(packed, j)

    @pl.when(jnp.logical_not(has_w))
    def _():
        hx[...] = jnp.zeros_like(hx)
        cbuf[0] = jnp.zeros_like(cbuf[0])
        ebuf[0] = jnp.zeros_like(ebuf[0])

    @pl.when(jnp.logical_not(has_e))
    def _():
        cbuf[2] = jnp.zeros_like(cbuf[2])
        ebuf[1] = jnp.zeros_like(ebuf[1])

    @pl.when(jnp.logical_not(has_n))
    def _():
        hyd[...] = jnp.zeros_like(hyd)
        nbuf[0] = jnp.zeros_like(nbuf[0])
        for d in range(3):
            cbuf[d, :, 0:3] = jnp.zeros_like(cbuf[d, :, 0:3])
        for d in range(2):
            ebuf[d, 0] = jnp.zeros_like(ebuf[d, 0])

    @pl.when(jnp.logical_not(has_s))
    def _():
        hyu[...] = jnp.zeros_like(hyu)
        nbuf[1] = jnp.zeros_like(nbuf[1])
        for d in range(3):
            cbuf[d, :, 3 + CY:] = jnp.zeros_like(cbuf[d, :, 3 + CY:])
        for d in range(2):
            ebuf[d, 2] = jnp.zeros_like(ebuf[d, 2])

    await_recv(sx0, hx, ssem, s0.at[0], (east, gy), has_w)
    await_recv(sy0.at[0:2], hyd, ssem, s0.at[1], (gx, south), has_n)
    await_recv(sy0.at[2:3], hyu, ssem, s0.at[2], (gx, north), has_s)

    yl_s[0] = hyd[0]
    for j in range(Y):
        xl_s[j] = jnp.where(lane == 0, hx[:, SLOTS * j + XC:SLOTS * j + XC + 1], pltpu.roll(xc_s[j], 1, 1))

    ysteps = strides_of(Y)
    for lo in range(0, Z, 8):
        zs = slice(lo, lo + 8)
        a = [yl_s[j, zs] for j in range(Y)]
        c = [yc_s[j, zs] for j in range(Y)]
        e = [xl_s[j, zs] + xc_s[j, zs] + zd_s[j, zs] for j in range(Y)]
        for n, s in enumerate(ysteps):
            inv = [1.0 / (a[j] + c[j] + e[j]) for j in range(Y)]
            ai, ci = [a[j] * inv[j] for j in range(Y)], [c[j] * inv[j] for j in range(Y)]
            for j in range(Y):
                if j + s < Y:
                    wy_s[n, 0, j, zs] = ci[j]
                if j >= s:
                    wy_s[n, 1, j, zs] = ai[j]
            e2 = []
            for j in range(Y):
                v = e[j]
                if j >= s:
                    v = v + ci[j - s] * e[j - s]
                if j + s < Y:
                    v = v + ai[j + s] * e[j + s]
                e2.append(v)
            a = [a[j] * ai[j - s] if j >= s else a[j] for j in range(Y)]
            c = [c[j] * ci[j + s] if j + s < Y else c[j] for j in range(Y)]
            e = e2
        for j in range(Y):
            inv = 1.0 / (a[j] + c[j] + e[j])
            iy_s[j, zs], ly_s[j, zs], ry_s[j, zs] = inv, a[j] * inv, c[j] * inv

    k_top, k_end = jnp.sqrt(yl_s[0]), jnp.sqrt(yc_s[Y - 1])
    i_top = jnp.where(has_n, 1.0 / jnp.where(has_n, k_top, 1.0), 0.0)
    ysc[0], ysc[1] = i_top, 1.0 / k_end
    syc[0], syc[1], syc[2] = ly_s[0], ly_s[Y - 1] * k_end * i_top, ry_s[Y - 1]
    ycb[gy] = syc[...]
    for j in y_peers:
        comm.send(syc, ycb.at[gy], syco.at[gy], (gx, j))

    x_factor(0, 1, yl_s[0:1])
    x_source(0, 1, hyd[1:2], p_s[1:2])
    x_source(Y - 1, Y, p_s[Y - 2:Y - 1], hyu[0:1])
    for lo in range(0, Y, Y - 1):
        packed = pack_row(packed, lo)
    packed = jnp.where(item == XC, sx0[...], packed)
    sxb[...] = packed
    xb[gx] = packed
    for i in x_peers:
        comm.send(sxb, xb.at[gx], sx.at[0, gx], (i, gy))

    def x_local():
        for lo in range(0, Y, CH):
            part = slice(lo, lo + CH)
            r = r_s[part]
            for n, s in enumerate(strides_of(X)):
                r = r + pltpu.roll(wx_s[n, 0, part] * r, s, 2) + pltpu.roll(wx_s[n, 1, part] * r, X - s, 2)
            g_s[part] = r * ix_s[part]

    def y_local():
        for lo in range(0, Z, 8):
            zs = slice(lo, lo + 8)
            r = [r_s[j, zs] for j in range(Y)]
            for n, s in enumerate(ysteps):
                low = [wy_s[n, 0, j, zs] * r[j] if j + s < Y else None for j in range(Y)]
                high = [wy_s[n, 1, j, zs] * r[j] if j >= s else None for j in range(Y)]
                r2 = []
                for j in range(Y):
                    v = r[j]
                    if j >= s:
                        v = v + low[j - s]
                    if j + s < Y:
                        v = v + high[j + s]
                    r2.append(v)
                r = r2
            for j in range(Y):
                g_s[j, zs] = r[j] * iy_s[j, zs]

    x_local()

    half = X // 2
    off = half // 2
    ii = lax.broadcasted_iota(jnp.int32, (X, X), 0)
    mm = lax.broadcasted_iota(jnp.int32, (X, X), 1)

    def selection(step, start):
        target = lax.rem((ii + (step + 2)) // 2 - 1 + start + X, X)
        return jnp.where(mm == target, 0.125, 0.0)

    def pairs(field):
        v = field.reshape(CY, 2, Z, X)
        pair_s[...] = (v[:, 0] + v[:, 1]).reshape(CY * Z, X)
        return pair_s[pl.ds(0, CY * CZ, stride=2), :] + pair_s[pl.ds(1, CY * CZ, stride=2), :]

    def mxu(a, b):
        return jnp.dot(a, b, precision=lax.Precision.HIGHEST, preferred_element_type=f32)

    here, there = selection(0, off), selection(0, half + off)
    sel2 = jnp.concatenate([here, there], axis=0)
    zfull = jnp.stack([rows(z_ref, j) for j in range(Y)])
    damp = jnp.stack([rows(d_ref, j) for j in range(Y)])
    for m, (u, v) in enumerate(((xc_s[...], yc_s[...]), (zfull, damp))):
        both_pairs = jnp.concatenate([pairs(u), pairs(v)], axis=1)
        part = mxu(both_pairs, sel2).reshape(CY, CZ, X)
        cown[m] = part
        cbuf[1, m, 3:3 + CY] = part

    def coarse_parts(straight):
        def rows_of(slot, lo, n):
            return cbuf.at[slot, :, pl.ds(lo, n)]

        out = []
        for slot, i, ok, back in ((0, west, has_w, 2), (1, gx, None, 1), (2, east, has_e, 0)):
            both_ok = (lambda c: c) if ok is None else (lambda c, ok=ok: jnp.logical_and(c, ok))
            if straight:
                if ok is not None:
                    out.append((cown, 3, CY, 0, slot, back, (i, gy), ok, ok))
            else:
                out.append((cown.at[:, pl.ds(CY - 3, 3)], 0, 3, 1, slot, back, (i, south), both_ok(has_s), both_ok(has_n)))
                out.append((cown.at[:, pl.ds(0, 2)], 3 + CY, 2, 2, slot, back, (i, north), both_ok(has_n), both_ok(has_s)))
        return rows_of, out

    def coarse_send(straight):
        rows_of, parts = coarse_parts(straight)
        for src, lo, n, kind, slot, back, dev, ok, _ in parts:
            comm.send(src, rows_of(back, lo, n), sc.at[kind, back], dev, ok)

    def coarse_wait():
        for straight in (True, False):
            rows_of, parts = coarse_parts(straight)
            for src, lo, n, kind, slot, back, dev, _, ok in parts:
                await_recv(src, rows_of(slot, lo, n), ssem, sc.at[kind, slot], dev, ok)

    def slot(v, k):
        return v if k == 0 else pltpu.roll(v, X - k, 1)

    def expand(v):
        return jnp.concatenate([v, pltpu.roll(v, X - 1, 1)], axis=0)

    def x_solve(hl, hr, gs, ge):
        alpha = jnp.zeros((Z, X), f32)
        for d in range(nx - 1):
            alpha = jnp.where(d < gx, hl(d) + xtau[d] * alpha, alpha)
        gamma = jnp.zeros((Z, X), f32)
        for d in reversed(range(1, nx)):
            gamma = jnp.where(d > gx, hr(d) + xtau2[d] * gamma, gamma)
        p = xrho[gx] * alpha + xbet[gx] * gs
        q = gamma + xdlt[gx] * ge
        return xkk[0] * p + xkk[1] * q, xkk[2] * q + xkk[3] * p

    def x_first():
        for i in x_peers:
            await_recv(sxb, xb.at[i], ssem, sx.at[0, i], (i, gy))
        tiles = [xb[d] for d in range(nx)]
        cut = [[slot(t, k) for t in tiles] for k in range(SLOTS - 1)]
        own = [slot(sxb[...], k) for k in range(SLOTS - 1)]
        inv = [1.0 / v for v in cut[XC]]
        ge = [cut[GE][d] * inv[d] for d in range(nx)]
        gs = cut[GS]
        xown[0] = 1.0 / own[XC]
        chain_factor(nx, gx, cut[LS], cut[LE], cut[RS], cut[RE], cut[XC], [own[LS], own[LE], own[RS], own[RE]],
                     xrho, xtau, xsig, xbet, xtau2, xsig2, xscl, xdlt, xkk)
        return x_solve(
            lambda d: ge[d] + xsig[d] * gs[d], lambda d: xscl[d] * gs[d] + xsig2[d] * ge[d], own[GS], own[GE] * xown[0]
        )

    def x_second():
        packed = jnp.zeros((Z, X), f32)
        for j in range(Y):
            gs, ge = edge_sums(j)
            packed = jnp.where(group == j, jnp.where(item == 0, gs, ge), packed)
        gs, ge = packed, pltpu.roll(packed, X - 1, 1) * xown[0]
        for side, h in enumerate((ge + xsig[gx] * gs, xscl[gx] * gs + xsig2[gx] * ge)):
            sx1[side] = jnp.where(item[:CZ] == 0, h[:CZ], pltpu.roll(h[CZ:], 1, 1))
        for i in x_peers:
            comm.send(sx1.at[jnp.where(i > gx, 0, 1)], xb1.at[gx], sx.at[1, gx], (i, gy))
        x_local()
        coarse_send(False)
        for i in x_peers:
            await_recv(sx1.at[0], xb1.at[i], ssem, sx.at[1, i], (i, gy))
        return x_solve(lambda d: expand(xb1[d]), lambda d: expand(xb1[d]), gs, ge)

    def y_half(m, left, right):
        top, end = jnp.zeros((Z, X), f32), jnp.zeros((Z, X), f32)
        for j in range(Y):
            u = jnp.broadcast_to(left[:, SLOTS * j:SLOTS * j + 1], (Z, X))
            w = jnp.broadcast_to(right[:, SLOTS * j:SLOTS * j + 1], (Z, X))
            v = g_s[j] + lx_s[j] * u + rx_s[j] * w
            q_s[j] = v
            before = jnp.where(lane == 0, v, pltpu.roll(v, 1, 1))
            after = jnp.where(lane == X - 1, w, pltpu.roll(v, X - 1, 1))
            r = fo_s[j] + xl_s[j] * before + xc_s[j] * after + jnp.where(lane == 0, u - v, 0.0)
            r = r + zl_s[j] * pltpu.roll(v, 1, 0) + zt_s[j] * pltpu.roll(v, Z - 1, 0)
            r_s[j] = r
            top, end = top + ly_s[j] * r, end + ry_s[j] * r
        top, end = top * ysc[0], end * ysc[1]
        if m == 0:
            for j in y_peers:
                await_recv(syc, ycb.at[j], ssem, syco.at[j], (gx, j))
            ls, mid, re = [[ycb[d, k] for d in range(ny)] for k in range(3)]
            interface_factor(
                ny, gy, ls, mid, mid, re, [syc[0], syc[1], syc[1], syc[2]],
                ytau, ysig, ybet, ytau2, ysig2, ydlt, ykk,
            )
        shy[m, 0] = end + ysig[gy] * top
        shy[m, 1] = top + ysig2[gy] * end
        yb[m, gy] = shy[m, 0]
        for j in y_peers:
            side = jnp.where(j > gy, 0, 1)
            comm.send(shy.at[m, side], yb.at[m, gy], sy.at[m, gy], (gx, j))
        y_local()
        if m == 0:
            coarse_send(True)
        else:
            coarse_wait()
            coefs = planes()
        for j in y_peers:
            await_recv(shy.at[m, 0], yb.at[m, j], ssem, sy.at[m, j], (gx, j))
        above, below = interface_solve(ny, gy, lambda d: yb[m, d], lambda d: yb[m, d], top, end, ytau, ytau2, ykk)
        above, below = above * ysc[0], below * ysc[1]
        return above, below, (coefs if m else None)

    centre = jnp.logical_and(lane3 >= off, lane3 < off + half)
    H = CY + 4
    row = lax.broadcasted_iota(jnp.int32, (H, 1, 1), 0)
    inside = jnp.logical_and(
        jnp.logical_or(row >= 2, has_n), jnp.logical_or(row < 2 + CY, has_s)
    )
    inside = jnp.logical_and(
        inside,
        jnp.logical_and(jnp.logical_or(lane3 >= off, has_w), jnp.logical_or(lane3 < off + half, has_e)),
    )

    def planes():
        out = []
        for m in range(2):
            w, o, e = cbuf[0, m], cbuf[1, m], cbuf[2, m]
            out.append(jnp.where(centre, o, pltpu.roll(jnp.where(lane3 >= half, w, e), half, 2)))
            out.append(jnp.where(centre, pltpu.roll(o, half, 2), jnp.where(lane3 < half, w, e)))
        cx, cy, cz, cd = out
        czl = lax.broadcasted_iota(jnp.int32, (1, CZ, 1), 1)
        cyl, cy = cy[:H], cy[1:]
        cx, cz, cd = cx[1:], cz[1:], cd[1:]
        cd = jnp.where(inside, cd, 1.0)
        ct = jnp.where(czl < CZ - 1, cz, 0.0)
        cl = pltpu.roll(ct, 1, 1)
        cxl = pltpu.roll(cx, 1, 2)
        diag = cxl + cx + cyl + cy + cl + ct + cd
        return cx, cxl, cy, cyl, cl, ct, diag, RELAX / diag

    left, right = x_first()
    above, below, _ = y_half(0, left, right)
    p_s[...] = g_s[...] + ly_s[...] * above[None] + ry_s[...] * below[None]
    for lo in range(0, Y, CH):
        hi = lo + CH
        lower = jnp.concatenate([above[None], p_s[0:hi - 1]], axis=0) if lo == 0 else p_s[lo - 1:hi - 1]
        upper = jnp.concatenate([p_s[lo + 1:Y], below[None]], axis=0) if hi == Y else p_s[lo + 1:hi + 1]
        x_source(lo, hi, lower, upper)
    left, right = x_second()
    above, below, coefs = y_half(1, left, right)
    v = g_s[...] + ly_s[...] * above[None] + ry_s[...] * below[None]
    for j in range(Y):
        op_ref[pl.ds(j, Z, stride=Y), :] = v[j]

    whole = slice(0, Y)
    change = v - q_s[...]
    stacked = jnp.concatenate(
        [pairs(xc_s[...] * change), pairs(xl_s[...] * change), pairs(z_terms(change, whole))], axis=1
    )
    sel3 = jnp.concatenate([selection(1, off), selection(-1, off), here], axis=0)
    partial = mxu(stacked, sel3).reshape(CY, CZ, X)
    rown[0], rown[1] = partial[0:2], partial[CY - 2:]
    clane = lax.broadcasted_iota(jnp.int32, (CZ, X), 1)
    inner = clane % half
    edge = jnp.zeros((CZ, X), f32)
    for r in range(CY):
        edge = jnp.where(inner >= 4 * r, pltpu.roll(partial[r], half - off + 2 + 4 * r, 1), edge)
    sedge[...] = edge

    def residual_exchange(starting):
        for n, (dev, ok, back) in enumerate((((gx, south), has_s, 0), ((gx, north), has_n, 1))):
            if starting:
                comm.send(rown.at[1 - n], nbuf.at[back], sr.at[2, back], dev, ok)
            else:
                await_recv(rown.at[n], nbuf.at[n], ssem, sr.at[2, n], dev, (has_n, has_s)[n])
        for n, (i, ok) in enumerate(((west, has_w), (east, has_e))):
            for r, (j, okj) in enumerate(((north, has_n), (gy, None), (south, has_s))):
                cond = ok if okj is None else jnp.logical_and(ok, okj)
                if starting:
                    comm.send(sedge, ebuf.at[1 - n, 2 - r], sr.at[1 - n, 2 - r], (i, j), cond)
                else:
                    await_recv(sedge, ebuf.at[n, r], ssem, sr.at[n, r], (i, j), cond)

    residual_exchange(True)
    cx, cxl, cy, cyl, cl, ct, diag, scale = coefs
    residual_exchange(False)
    fringe = []
    for n in range(3):
        both = jnp.where(clane < half, ebuf[0, n], ebuf[1, n])
        for r in ((CY - 2, CY - 1), range(CY), (0, 1))[n]:
            fringe.append(pltpu.roll(both, (off - 2 - 4 * r) % X, 1))
    near = jnp.logical_or(
        jnp.logical_and(lane3 >= off - 2, lane3 <= off), jnp.logical_and(lane3 >= off + half - 1, lane3 <= off + half + 1)
    )
    res = jnp.concatenate([nbuf[0], partial, nbuf[1]], axis=0) + jnp.where(near, jnp.stack(fringe), 0.0)
    res = jnp.where(inside, res, 0.0)
    cor = scale * res
    for repeat in range(COARSE - 1):
        lo, n = 1 + repeat, H - 2 - 2 * repeat
        cut = slice(lo, lo + n)
        mid, over, under = cor[1:-1], cor[:-2], cor[2:]
        applied = (
            diag[cut] * mid
            - cxl[cut] * pltpu.roll(mid, 1, 2)
            - cx[cut] * pltpu.roll(mid, X - 1, 2)
            - cyl[cut] * over
            - cy[cut] * under
            - cl[cut] * pltpu.roll(mid, 1, 1)
            - ct[cut] * pltpu.roll(mid, CZ - 1, 1)
        )
        cor = jnp.where(inside[cut], mid + scale[cut] * (res[cut] - applied), 0.0)
    hj = CY // 2
    mine = jnp.where(lane3 < half, pltpu.roll(cor[:hj], X - off, 2), pltpu.roll(cor[hj:], off, 2))
    fown[...] = mine
    fbuf[gx] = mine
    for i in x_peers:
        comm.send(fown, fbuf.at[gx], sf.at[gx], (i, gy))
    own = pltpu.roll(res[2:2 + CY], X - off, 2)
    for j in range(CY):
        flip[pl.ds(j, CZ, stride=CY), :] = own[j]
    or_ref[...] = flip[0:CZ * CY, :half]
    for i in x_peers:
        await_recv(fown, fbuf.at[i], ssem, sf.at[i], (i, gy))
    for t in range(nx // 2):
        u, v = fbuf[2 * t], fbuf[2 * t + 1]
        top = jnp.where(lane3 < half, u, pltpu.roll(v, half, 2))
        low = jnp.where(lane3 < half, pltpu.roll(u, half, 2), v)
        base = (t + 1) * CZ * CY
        for j in range(CY):
            flip[pl.ds(base + j, CZ, stride=CY), :] = top[j] if j < hj else low[j - hj]
        oc_ref[:, t * X:(t + 1) * X] = flip[base:base + CZ * CY, :]
    comm.finish()


def put(*refs):
    sems = refs[6]
    give = [pltpu.make_async_copy(refs[m], refs[3 + m], sems.at[m]) for m in range(3)]
    for copy in give:
        copy.start()
    for copy in give:
        copy.wait()


def body(nx, ny, *args):
    Z, Y, X = args[0].shape
    CZ, CY = Z // 2, Y // 2
    flat = [v.reshape(Z * Y, X) for v in args]
    f32 = jnp.float32

    def vm(*shape):
        return pltpu.VMEM(shape, f32)

    block = (Y, Z, X)
    assert Y * SLOTS <= X and 4 * CY <= X // 2
    nsx, nsy = len(strides_of(X)), len(strides_of(Y))
    sends = 3 + (ny - 1) * 3 + (nx - 1) * 3 + 8 * 2
    dma = pltpu.SemaphoreType.DMA
    scratch = (
        [vm(*block) for _ in range(12)]
        + [vm(*block), vm(*block), vm(*block), vm(nsx, 2, *block), vm(*block), vm(*block), vm(*block), vm(nsy, 2, *block)]
        + [vm(Z, X), vm(3, Z, X), vm(Z, X), vm(2, Z, X), vm(1, Z, X)]
        + [vm(nx, Z, X), vm(Z, X), vm(nx, CZ, X), vm(2, CZ, X)]
        + [vm(ny, 3, Z, X), vm(3, Z, X), vm(2, ny, Z, X), vm(2, 2, Z, X)]
        + [vm(1, Z, X)] + [vm(nx, Z, X) for _ in range(8)] + [vm(4, Z, X)]
        + [vm(ny, Z, X) for _ in range(6)] + [vm(6, Z, X), vm(2, Z, X)]
        + [vm(CY * Z, X), vm(2, CY, CZ, X), vm(3, 2, CY + 5, CZ, X), vm(2, 2, CZ, X), vm(2, 2, CZ, X),
           vm(2, 3, CZ, X), vm(CZ, X), vm(CY // 2, CZ, X), vm(nx, CY // 2, CZ, X), vm((nx // 2 + 1) * CZ * CY, X)]
        + [dma((sends,)), dma((3,)), dma((2, nx)), dma((ny,)), dma((2, ny)), dma((3, 3)), dma((3, 3)), dma((nx,))]
        + [vm(6, Z * Y, X), dma((6,))]
    )
    p, r, c = pl.pallas_call(
        functools.partial(kernel, nx, ny),
        out_shape=(
            vm(Z * Y, X),
            vm(CZ * CY, X // 2),
            vm(CZ * CY, nx * X // 2),
        ),
        in_specs=[pl.BlockSpec(memory_space=pltpu.HBM)] * 6,
        out_specs=[pl.BlockSpec(memory_space=pltpu.VMEM)] * 3,
        scratch_shapes=scratch,
        compiler_params=pltpu.CompilerParams(
            collective_id=0, has_side_effects=True, vmem_limit_bytes=60000000
        ),
    )(*flat)
    p, r, c = pl.pallas_call(
        put,
        out_shape=tuple(jax.ShapeDtypeStruct(v.shape, f32) for v in (p, r, c)),
        in_specs=[pl.BlockSpec(memory_space=pltpu.VMEM)] * 3,
        out_specs=[pl.BlockSpec(memory_space=pltpu.HBM)] * 3,
        scratch_shapes=[dma((3,))],
    )(*[pltpu.with_memory_space_constraint(v, pltpu.VMEM) for v in (p, r, c)])
    return p.reshape(Z, Y, X), r.reshape(CZ, CY, X // 2), c.reshape(CZ, CY, nx * X // 2)


def solution(mesh):
    nx, ny = mesh.shape["gx"], mesh.shape["gy"]
    split = P(None, "gy", "gx")
    return jax.shard_map(
        functools.partial(body, nx, ny),
        mesh=mesh,
        in_specs=(split,) * 6,
        out_specs=(split, split, P(None, "gy", None)),
        check_vma=False,
    )
```

```python
import functools

import jax
import jax.numpy as jnp
from jax import lax
from jax.experimental import pallas as pl
from jax.experimental.pallas import tpu as pltpu
from jax.sharding import PartitionSpec as P

COARSE = 3
RELAX = 0.8
CH = 4
LE, LS, RE, RS, GS, GE, XC = range(7)
SLOTS = 8
MESH = pl.DeviceIdType.MESH


def strides_of(length):
    out, s = [], 1
    while s < length:
        out.append(s)
        s *= 2
    return out


class Comm:
    def __init__(self, send_sems):
        self.sems, self.used, self.pending = send_sems, 0, []

    def send(self, src, dst, recv, dev, cond=None):
        copy = pltpu.make_async_remote_copy(
            src_ref=src, dst_ref=dst, send_sem=self.sems.at[self.used], recv_sem=recv,
            device_id=dev, device_id_type=MESH,
        )
        self.used += 1
        self.pending.append((copy, cond))
        if cond is None:
            copy.start()
        else:
            pl.when(cond)(copy.start)

    def finish(self):
        for copy, cond in self.pending:
            if cond is None:
                copy.wait_send()
            else:
                pl.when(cond)(copy.wait_send)


def await_recv(src, dst, sems, recv, dev, cond=None):
    copy = pltpu.make_async_remote_copy(
        src_ref=src, dst_ref=dst, send_sem=sems.at[0], recv_sem=recv, device_id=dev, device_id_type=MESH
    )
    if cond is None:
        copy.wait_recv()
    else:
        pl.when(cond)(copy.wait_recv)


def farthest_first(me, n):
    out = []
    for k in range(n - 1):
        down = jnp.where(n - 1 - k > me, n - 1 - k, n - 2 - k)
        up = jnp.where(k < me, k, k + 1)
        out.append(jnp.where(2 * me < n, down, up))
    return out


def flipped(me, n):
    if n & (n - 1):
        return [lax.rem(me + o, n) for o in range(1, n)]
    out = []
    for mask in range(n - 1, 0, -1):
        peer, bit = 0, 1
        while bit < n:
            value = lax.rem(me // bit, 2)
            peer = peer + bit * (1 - value if mask & bit else value)
            bit *= 2
        out.append(peer)
    return out


def interface_factor(n, me, ls, le, rs, re, own, tau, sig, bet, tau2, sig2, dlt, kk):
    beta = jnp.zeros_like(ls[0])
    for d in range(n):
        bet[d] = beta
        w = 1.0 / (1.0 - ls[d] * beta)
        t = le[d] * w
        tau[d] = t
        s = t * beta
        sig[d] = s
        beta = re[d] + s * rs[d]
    delta = jnp.zeros_like(ls[0])
    for d in reversed(range(n)):
        dlt[d] = delta
        w = 1.0 / (1.0 - re[d] * delta)
        t = rs[d] * w
        tau2[d] = t
        s = t * delta
        sig2[d] = s
        delta = ls[d] + s * le[d]
    ls_m, le_m, rs_m, re_m = own
    beta, delta = bet[me], dlt[me]
    a, b = 1.0 - beta * ls_m, 1.0 - delta * re_m
    o1, o2 = beta * rs_m, delta * le_m
    inv = 1.0 / (a * b - o1 * o2)
    kk[0], kk[1], kk[2], kk[3] = b * inv, o1 * inv, a * inv, o2 * inv
    kk[4], kk[5] = beta, delta


def interface_solve(n, me, h_left, h_right, gs, ge, tau, tau2, kk):
    alpha = jnp.zeros_like(gs)
    for d in range(n - 1):
        alpha = jnp.where(d < me, h_left(d) + tau[d] * alpha, alpha)
    gamma = jnp.zeros_like(gs)
    for d in reversed(range(1, n)):
        gamma = jnp.where(d > me, h_right(d) + tau2[d] * gamma, gamma)
    p = alpha + kk[4] * gs
    q = gamma + kk[5] * ge
    return kk[0] * p + kk[1] * q, kk[2] * q + kk[3] * p


def chain_factor(n, me, ls, le, rs, re, xc, own, rho, tau, sig, bet, tau2, sig2, scl, dlt, kk):
    one, zero = jnp.ones_like(ls[0]), jnp.zeros_like(ls[0])
    beta = zero
    for d in range(n):
        r = zero if d == 0 else xc[d - 1]
        b = one if d == 0 else 1.0 - r * (1.0 - beta)
        rho[d], bet[d] = r, b
        w = 1.0 / (1.0 - ls[d] * b)
        t = le[d] * w
        tau[d] = t * r
        s = t * b
        sig[d] = s
        beta = re[d] + s * rs[d]
    delta = zero
    for d in reversed(range(n)):
        dlt[d] = delta
        t = rs[d] / (1.0 - re[d] * delta)
        s = t * delta
        q = ls[d] + s * le[d]
        if d > 0:
            v = 1.0 / (1.0 - q + q * xc[d - 1])
            scl[d], tau2[d], sig2[d] = v, v * t, v * s
            delta = v * q * xc[d - 1]
        else:
            scl[d], tau2[d], sig2[d] = zero, zero, zero
    ls_m, le_m, rs_m, re_m = own
    beta, delta = bet[me], dlt[me]
    a, b = 1.0 - beta * ls_m, 1.0 - delta * re_m
    o1, o2 = beta * rs_m, delta * le_m
    inv = 1.0 / (a * b - o1 * o2)
    kk[0], kk[1], kk[2], kk[3] = b * inv, o1 * inv, a * inv, o2 * inv


def kernel(nx, ny, f_hbm, p_hbm, x_hbm, y_hbm, z_hbm, d_hbm, op_ref, or_ref, oc_ref,
           xl_s, xc_s, yl_s, yc_s, zl_s, zt_s, zd_s, fo_s, p_s, r_s, g_s, q_s,
           lx_s, rx_s, ix_s, wx_s, ly_s, ry_s, iy_s, wy_s,
           sx0, sy0, hx, hyd, hyu, xb, sxb, xb1, sx1, ycb, syc, yb, shy,
           xown, xrho, xtau, xsig, xbet, xtau2, xsig2, xscl, xdlt, xkk,
           ytau, ysig, ybet, ytau2, ysig2, ydlt, ykk, ysc,
           pair_s, sel_s, cown, cbuf, wbuf, pbuf, sxt, xtr, ebuf, sedge, fown, fbuf, flip,
           ssem, s0, sx, syco, sy, sc, sr, sw, sf, ins, sin):
    Y, Z, X = xc_s.shape
    CY, CZ = Y // 2, Z // 2
    f32 = jnp.float32
    gx, gy = lax.axis_index("gx"), lax.axis_index("gy")
    has_w, has_e = gx > 0, gx < nx - 1
    has_n, has_s = gy > 0, gy < ny - 1
    west, east = jnp.maximum(gx - 1, 0), jnp.minimum(gx + 1, nx - 1)
    north, south = jnp.maximum(gy - 1, 0), jnp.minimum(gy + 1, ny - 1)
    x_peers = farthest_first(gx, nx)
    y_peers = flipped(gy, ny)

    loads = []
    for m, ref in enumerate((x_hbm, y_hbm, p_hbm, z_hbm, d_hbm, f_hbm)):
        loads.append(pltpu.make_async_copy(ref, ins.at[m], sin.at[m]))
        loads[m].start()
    x_ref, y_ref, p_ref, z_ref, d_ref, f_ref = [ins.at[m] for m in range(6)]

    barrier = pltpu.get_barrier_semaphore()

    def greet(dev):
        pl.semaphore_signal(barrier, inc=1, device_id=dev, device_id_type=MESH)

    for i in x_peers:
        greet((i, gy))
    for j in y_peers:
        greet((gx, j))

    corners = [
        (jnp.logical_and(h, v), (i, j)) for h, i in ((has_w, west), (has_e, east)) for v, j in ((has_n, north), (has_s, south))
    ]
    for cond, dev in corners:
        pl.when(cond)(functools.partial(greet, dev))

    lane = lax.broadcasted_iota(jnp.int32, (Z, X), 1)
    level = lax.broadcasted_iota(jnp.int32, (Z, X), 0)
    lane3 = lax.broadcasted_iota(jnp.int32, (1, 1, X), 2)
    item, group = lane % SLOTS, lane // SLOTS

    def rows(ref, j):
        return ref[pl.ds(j, Z, stride=Y), :]

    for m in range(3):
        loads[m].wait()
    packed = jnp.zeros((Z, X), f32)
    for j in range(Y):
        v = rows(x_ref, j)
        xc_s[j] = v
        packed = jnp.where(lane == SLOTS * j + XC, v[:, X - 1:], packed)
    sx0[...] = packed
    sy0[0] = rows(y_ref, Y - 1)
    sy0[1] = rows(p_ref, Y - 1)
    sy0[2] = rows(p_ref, 0)

    n_corners = sum(cond.astype(jnp.int32) for cond, _ in corners)
    pl.semaphore_wait(barrier, (nx - 1) + (ny - 1) + n_corners)

    comm = Comm(ssem)
    comm.send(sy0.at[0:2], hyd, s0.at[1], (gx, south), has_s)
    comm.send(sy0.at[2:3], hyu, s0.at[2], (gx, north), has_n)
    comm.send(sx0, hx, s0.at[0], (east, gy), has_e)

    for j in range(Y):
        yc_s[j] = rows(y_ref, j)
        p_s[j] = rows(p_ref, j)
    for m in range(3, 6):
        loads[m].wait()
    for j in range(Y):
        zv = jnp.where(level < Z - 1, rows(z_ref, j), 0.0)
        zt_s[j] = zv
        zl = pltpu.roll(zv, 1, 0)
        zl_s[j] = zl
        zd_s[j] = zv + zl + rows(d_ref, j)
        fo_s[j] = rows(f_ref, j)

    first, last = lane3 == 0, lane3 == X - 1

    def x_factor(lo, hi, above):
        part = slice(lo, hi)
        c = xc_s[part]
        a = jnp.where(first, 1.0, pltpu.roll(c, 1, 2))
        e = above + yc_s[part] + zd_s[part]
        for n, s in enumerate(strides_of(X)):
            low, high = lane3 >= s, lane3 < X - s
            inv = 1.0 / (a + c + e)
            ai, ci = a * inv, c * inv
            am, cm = jnp.where(low, ai, 0.0), jnp.where(high, ci, 0.0)
            wx_s[n, 0, part], wx_s[n, 1, part] = cm, am
            a = a * jnp.where(low, pltpu.roll(ai, s, 2), 1.0)
            c = c * jnp.where(high, pltpu.roll(ci, X - s, 2), 1.0)
            e = e + pltpu.roll(cm * e, s, 2) + pltpu.roll(am * e, X - s, 2)
        inv = 1.0 / (a + c + e)
        ix_s[part], lx_s[part], rx_s[part] = inv, a * inv, c * inv

    def z_terms(v, part):
        return zl_s[part] * pltpu.roll(v, 1, 1) + zt_s[part] * pltpu.roll(v, Z - 1, 1)

    def x_source(lo, hi, lower, upper):
        part = slice(lo, hi)
        r_s[part] = fo_s[part] + yl_s[part] * lower + yc_s[part] * upper + z_terms(p_s[part], part)

    ends = jnp.logical_or(lane == 0, lane == X - 1)

    def edge_sums(j):
        r = r_s[j]
        return jnp.sum(lx_s[j] * r, axis=1, keepdims=True), jnp.sum(rx_s[j] * r, axis=1, keepdims=True)

    def pack_row(packed, j):
        gs, ge = edge_sums(j)
        v = jnp.where(ends, lx_s[j], pltpu.roll(rx_s[j], 2, 1))
        v = jnp.where(item < GS, pltpu.roll(v, SLOTS * j + 1, 1), jnp.where(item == GS, gs, ge))
        return jnp.where(group == j, v, packed)

    yl_s[1:Y] = yc_s[0:Y - 1]
    packed = jnp.zeros((Z, X), f32)
    for lo in range(0, Y, CH):
        hi = lo + CH
        at = max(lo, 1)
        x_factor(at, hi, yl_s[at:hi])
        at, to = max(lo, 1), min(hi, Y - 1)
        x_source(at, to, p_s[at - 1:to - 1], p_s[at + 1:to + 1])
        for j in range(at, to):
            packed = pack_row(packed, j)

    @pl.when(jnp.logical_not(has_w))
    def _():
        hx[...] = jnp.zeros_like(hx)
        cbuf[0] = jnp.zeros_like(cbuf[0])
        ebuf[0] = jnp.zeros_like(ebuf[0])

    @pl.when(jnp.logical_not(has_e))
    def _():
        cbuf[2] = jnp.zeros_like(cbuf[2])
        ebuf[1] = jnp.zeros_like(ebuf[1])

    @pl.when(jnp.logical_not(has_n))
    def _():
        hyd[...] = jnp.zeros_like(hyd)
        wbuf[0:2] = jnp.zeros_like(wbuf[0:2])
        pbuf[0:2] = jnp.zeros_like(pbuf[0:2])
        xtr[0] = jnp.zeros_like(xtr[0])
        for d in range(3):
            cbuf[d, :, 0:3] = jnp.zeros_like(cbuf[d, :, 0:3])

    @pl.when(jnp.logical_not(has_s))
    def _():
        hyu[...] = jnp.zeros_like(hyu)
        wbuf[CY + 2:] = jnp.zeros_like(wbuf[CY + 2:])
        pbuf[CY + 2:] = jnp.zeros_like(pbuf[CY + 2:])
        xtr[1] = jnp.zeros_like(xtr[1])
        for d in range(3):
            cbuf[d, :, 3 + CY:] = jnp.zeros_like(cbuf[d, :, 3 + CY:])

    await_recv(sx0, hx, ssem, s0.at[0], (east, gy), has_w)
    await_recv(sy0.at[0:2], hyd, ssem, s0.at[1], (gx, south), has_n)
    await_recv(sy0.at[2:3], hyu, ssem, s0.at[2], (gx, north), has_s)

    yl_s[0] = hyd[0]
    for j in range(Y):
        xl_s[j] = jnp.where(lane == 0, hx[:, SLOTS * j + XC:SLOTS * j + XC + 1], pltpu.roll(xc_s[j], 1, 1))

    ysteps = strides_of(Y)
    for lo in range(0, Z, 8):
        zs = slice(lo, lo + 8)
        a = [yl_s[j, zs] for j in range(Y)]
        c = [yc_s[j, zs] for j in range(Y)]
        e = [xl_s[j, zs] + xc_s[j, zs] + zd_s[j, zs] for j in range(Y)]
        for n, s in enumerate(ysteps):
            inv = [1.0 / (a[j] + c[j] + e[j]) for j in range(Y)]
            ai, ci = [a[j] * inv[j] for j in range(Y)], [c[j] * inv[j] for j in range(Y)]
            for j in range(Y):
                if j + s < Y:
                    wy_s[n, 0, j, zs] = ci[j]
                if j >= s:
                    wy_s[n, 1, j, zs] = ai[j]
            e2 = []
            for j in range(Y):
                v = e[j]
                if j >= s:
                    v = v + ci[j - s] * e[j - s]
                if j + s < Y:
                    v = v + ai[j + s] * e[j + s]
                e2.append(v)
            a = [a[j] * ai[j - s] if j >= s else a[j] for j in range(Y)]
            c = [c[j] * ci[j + s] if j + s < Y else c[j] for j in range(Y)]
            e = e2
        for j in range(Y):
            inv = 1.0 / (a[j] + c[j] + e[j])
            iy_s[j, zs], ly_s[j, zs], ry_s[j, zs] = inv, a[j] * inv, c[j] * inv

    k_top, k_end = jnp.sqrt(yl_s[0]), jnp.sqrt(yc_s[Y - 1])
    i_top = jnp.where(has_n, 1.0 / jnp.where(has_n, k_top, 1.0), 0.0)
    ysc[0], ysc[1] = i_top, 1.0 / k_end
    syc[0], syc[1], syc[2] = ly_s[0], ly_s[Y - 1] * k_end * i_top, ry_s[Y - 1]
    ycb[gy] = syc[...]
    for j in y_peers:
        comm.send(syc, ycb.at[gy], syco.at[gy], (gx, j))

    x_factor(0, 1, yl_s[0:1])
    x_source(0, 1, hyd[1:2], p_s[1:2])
    x_source(Y - 1, Y, p_s[Y - 2:Y - 1], hyu[0:1])
    for lo in range(0, Y, Y - 1):
        packed = pack_row(packed, lo)
    packed = jnp.where(item == XC, sx0[...], packed)
    sxb[...] = packed
    xb[gx] = packed
    for i in x_peers:
        comm.send(sxb, xb.at[gx], sx.at[0, gx], (i, gy))

    def x_local():
        for lo in range(0, Y, CH):
            part = slice(lo, lo + CH)
            r = r_s[part]
            for n, s in enumerate(strides_of(X)):
                r = r + pltpu.roll(wx_s[n, 0, part] * r, s, 2) + pltpu.roll(wx_s[n, 1, part] * r, X - s, 2)
            g_s[part] = r * ix_s[part]

    def y_local():
        for lo in range(0, Z, 8):
            zs = slice(lo, lo + 8)
            r = [r_s[j, zs] for j in range(Y)]
            for n, s in enumerate(ysteps):
                low = [wy_s[n, 0, j, zs] * r[j] if j + s < Y else None for j in range(Y)]
                high = [wy_s[n, 1, j, zs] * r[j] if j >= s else None for j in range(Y)]
                r2 = []
                for j in range(Y):
                    v = r[j]
                    if j >= s:
                        v = v + low[j - s]
                    if j + s < Y:
                        v = v + high[j + s]
                    r2.append(v)
                r = r2
            for j in range(Y):
                g_s[j, zs] = r[j] * iy_s[j, zs]

    x_local()

    half = X // 2
    off = half // 2
    ii = lax.broadcasted_iota(jnp.int32, (X, X), 0)
    mm = lax.broadcasted_iota(jnp.int32, (X, X), 1)

    def selection(step, start):
        target = lax.rem((ii + (step + 2)) // 2 - 1 + start + X, X)
        return jnp.where(mm == target, 0.125, 0.0)

    def level_pairs(n, levels):
        for k, v in enumerate(levels):
            pair_s[n, k * Z:(k + 1) * Z] = v
        count = len(levels) * CZ
        return pair_s[n, pl.ds(0, count, stride=2), :] + pair_s[n, pl.ds(1, count, stride=2), :]

    def pairs(n, field):
        return level_pairs(n, [field(2 * k) + field(2 * k + 1) for k in range(CY)])

    def gathered(parts, first):
        v = jnp.concatenate(parts, axis=1)
        high = v.astype(jnp.bfloat16)
        v = v - high.astype(f32)
        mid = v.astype(jnp.bfloat16)
        low = (v - mid.astype(f32)).astype(jnp.bfloat16)
        sel = sel_s[first * X:(first + len(parts)) * X]
        return sum(jnp.dot(u, sel, preferred_element_type=f32) for u in (low, mid, high))

    for n, sel in enumerate((selection(1, off), selection(-1, off), selection(0, off), selection(0, half + off))):
        sel_s[n * X:(n + 1) * X] = sel.astype(jnp.bfloat16)
    for m, (u, v) in enumerate(((lambda j: xc_s[j], lambda j: yc_s[j]), (lambda j: rows(z_ref, j), lambda j: rows(d_ref, j)))):
        part = gathered([pairs(0, u), pairs(1, v)], 2).reshape(CY, CZ, X)
        cown[m] = part
        cbuf[1, m, 3:3 + CY] = part

    for k in range(CY):
        j = 2 * k
        for n, (g, scale) in enumerate(((ly_s, ysc[0]), (ry_s, ysc[1]))):
            u, v = g[j] * scale, g[j + 1] * scale
            at = 2 + k
            wbuf[at, n] = xc_s[j] * u + xc_s[j + 1] * v
            wbuf[at, 2 + n] = xl_s[j] * u + xl_s[j + 1] * v
            wbuf[at, 4 + n] = zl_s[j] * pltpu.roll(u, 1, 0) + zl_s[j + 1] * pltpu.roll(v, 1, 0)
            wbuf[at, 6 + n] = zt_s[j] * pltpu.roll(u, Z - 1, 0) + zt_s[j + 1] * pltpu.roll(v, Z - 1, 0)

    def to_rows(buf, sems, starting):
        for n, (dev, there, here) in enumerate((((gx, north), has_n, has_s), ((gx, south), has_s, has_n))):
            src = buf.at[pl.ds(2 if n == 0 else CY, 2)]
            dst = buf.at[pl.ds(CY + 2 if n == 0 else 0, 2)]
            if starting:
                comm.send(src, dst, sems.at[n], dev, there)
            else:
                await_recv(src, dst, ssem, sems.at[n], dev, here)

    def coarse_parts(straight):
        def rows_of(slot, lo, n):
            return cbuf.at[slot, :, pl.ds(lo, n)]

        out = []
        for slot, i, ok, back in ((0, west, has_w, 2), (1, gx, None, 1), (2, east, has_e, 0)):
            both_ok = (lambda c: c) if ok is None else (lambda c, ok=ok: jnp.logical_and(c, ok))
            if straight:
                if ok is not None:
                    out.append((cown, 3, CY, 0, slot, back, (i, gy), ok, ok))
            else:
                out.append((cown.at[:, pl.ds(CY - 3, 3)], 0, 3, 1, slot, back, (i, south), both_ok(has_s), both_ok(has_n)))
                out.append((cown.at[:, pl.ds(0, 2)], 3 + CY, 2, 2, slot, back, (i, north), both_ok(has_n), both_ok(has_s)))
        return rows_of, out

    def coarse_send(straight):
        rows_of, parts = coarse_parts(straight)
        for src, lo, n, kind, slot, back, dev, ok, _ in parts:
            comm.send(src, rows_of(back, lo, n), sc.at[kind, back], dev, ok)

    def coarse_wait():
        for straight in (True, False):
            rows_of, parts = coarse_parts(straight)
            for src, lo, n, kind, slot, back, dev, _, ok in parts:
                await_recv(src, rows_of(slot, lo, n), ssem, sc.at[kind, slot], dev, ok)

    def slot(v, k):
        return v if k == 0 else pltpu.roll(v, X - k, 1)

    def expand(v):
        return jnp.concatenate([v, pltpu.roll(v, X - 1, 1)], axis=0)

    def x_solve(hl, hr, gs, ge):
        alpha = jnp.zeros((Z, X), f32)
        for d in range(nx - 1):
            alpha = jnp.where(d < gx, hl(d) + xtau[d] * alpha, alpha)
        gamma = jnp.zeros((Z, X), f32)
        for d in reversed(range(1, nx)):
            gamma = jnp.where(d > gx, hr(d) + xtau2[d] * gamma, gamma)
        p = xrho[gx] * alpha + xbet[gx] * gs
        q = gamma + xdlt[gx] * ge
        return xkk[0] * p + xkk[1] * q, xkk[2] * q + xkk[3] * p

    def x_first():
        for i in x_peers:
            await_recv(sxb, xb.at[i], ssem, sx.at[0, i], (i, gy))
        tiles = [xb[d] for d in range(nx)]
        cut = [[slot(t, k) for t in tiles] for k in range(SLOTS - 1)]
        own = [slot(sxb[...], k) for k in range(SLOTS - 1)]
        inv = [1.0 / v for v in cut[XC]]
        ge = [cut[GE][d] * inv[d] for d in range(nx)]
        gs = cut[GS]
        xown[0] = 1.0 / own[XC]
        chain_factor(nx, gx, cut[LS], cut[LE], cut[RS], cut[RE], cut[XC], [own[LS], own[LE], own[RS], own[RE]],
                     xrho, xtau, xsig, xbet, xtau2, xsig2, xscl, xdlt, xkk)
        return x_solve(
            lambda d: ge[d] + xsig[d] * gs[d], lambda d: xscl[d] * gs[d] + xsig2[d] * ge[d], own[GS], own[GE] * xown[0]
        )

    def x_second():
        packed = jnp.zeros((Z, X), f32)
        for j in range(Y):
            gs, ge = edge_sums(j)
            packed = jnp.where(group == j, jnp.where(item == 0, gs, ge), packed)
        gs, ge = packed, pltpu.roll(packed, X - 1, 1) * xown[0]
        for side, h in enumerate((ge + xsig[gx] * gs, xscl[gx] * gs + xsig2[gx] * ge)):
            sx1[side] = jnp.where(item[:CZ] == 0, h[:CZ], pltpu.roll(h[CZ:], 1, 1))
        for i in x_peers:
            comm.send(sx1.at[jnp.where(i > gx, 0, 1)], xb1.at[gx], sx.at[1, gx], (i, gy))
        to_rows(wbuf, sw.at[0], True)
        coarse_send(False)
        x_local()
        for i in x_peers:
            await_recv(sx1.at[0], xb1.at[i], ssem, sx.at[1, i], (i, gy))
        return x_solve(lambda d: expand(xb1[d]), lambda d: expand(xb1[d]), gs, ge)

    def y_half(m, left, right):
        top, end = jnp.zeros((Z, X), f32), jnp.zeros((Z, X), f32)
        for j in range(Y):
            u = jnp.broadcast_to(left[:, SLOTS * j:SLOTS * j + 1], (Z, X))
            w = jnp.broadcast_to(right[:, SLOTS * j:SLOTS * j + 1], (Z, X))
            v = g_s[j] + lx_s[j] * u + rx_s[j] * w
            q_s[j] = v
            before = jnp.where(lane == 0, v, pltpu.roll(v, 1, 1))
            after = jnp.where(lane == X - 1, w, pltpu.roll(v, X - 1, 1))
            r = fo_s[j] + xl_s[j] * before + xc_s[j] * after + jnp.where(lane == 0, u - v, 0.0)
            r = r + zl_s[j] * pltpu.roll(v, 1, 0) + zt_s[j] * pltpu.roll(v, Z - 1, 0)
            r_s[j] = r
            top, end = top + ly_s[j] * r, end + ry_s[j] * r
        top, end = top * ysc[0], end * ysc[1]
        if m == 0:
            for j in y_peers:
                await_recv(syc, ycb.at[j], ssem, syco.at[j], (gx, j))
            ls, mid, re = [[ycb[d, k] for d in range(ny)] for k in range(3)]
            interface_factor(
                ny, gy, ls, mid, mid, re, [syc[0], syc[1], syc[1], syc[2]],
                ytau, ysig, ybet, ytau2, ysig2, ydlt, ykk,
            )
        shy[m, 0] = end + ysig[gy] * top
        shy[m, 1] = top + ysig2[gy] * end
        yb[m, gy] = shy[m, 0]
        for j in y_peers:
            side = jnp.where(j > gy, 0, 1)
            comm.send(shy.at[m, side], yb.at[m, gy], sy.at[m, gy], (gx, j))
        if m:
            sxt[0], sxt[1] = end, top
            comm.send(sxt.at[0], xtr.at[1], sw.at[1, 0], (gx, north), has_n)
            comm.send(sxt.at[1], xtr.at[0], sw.at[1, 1], (gx, south), has_s)
        y_local()
        if m == 0:
            coarse_send(True)
        else:
            for j in range(Y):
                r_s[j] = g_s[j] - q_s[j]
            pbuf[2:CY + 2] = gathered([
                pairs(0, lambda j: xc_s[j] * r_s[j]),
                pairs(1, lambda j: xl_s[j] * r_s[j]),
                pairs(2, lambda j: zl_s[j] * pltpu.roll(r_s[j], 1, 0) + zt_s[j] * pltpu.roll(r_s[j], Z - 1, 0)),
            ], 0).reshape(CY, CZ, X)
            to_rows(pbuf, sw.at[2], True)
            coarse_wait()
            coefs = planes()
            to_rows(wbuf, sw.at[0], False)
        for j in y_peers:
            await_recv(shy.at[m, 0], yb.at[m, j], ssem, sy.at[m, j], (gx, j))
        above, below = interface_solve(ny, gy, lambda d: yb[m, d], lambda d: yb[m, d], top, end, ytau, ytau2, ykk)
        if m == 0:
            return above * ysc[0], below * ysc[1]
        await_recv(sxt.at[0], xtr.at[1], ssem, sw.at[1, 0], (gx, north), has_s)
        await_recv(sxt.at[1], xtr.at[0], ssem, sw.at[1, 1], (gx, south), has_n)
        alpha, gamma = jnp.zeros((Z, X), f32), jnp.zeros((Z, X), f32)
        for d in range(ny - 2):
            alpha = jnp.where(d < gy - 1, yb[m, d] + ytau[d] * alpha, alpha)
        for d in reversed(range(2, ny)):
            gamma = jnp.where(d > gy + 1, yb[m, d] + ytau2[d] * gamma, gamma)
        q_top = top + syc[0] * above + syc[1] * below
        q_end = end + syc[1] * above + syc[2] * below
        beta, delta = ybet[north], ydlt[south]
        over = (alpha + beta * (xtr[0] + ycb[north, 1] * q_top)) / (1.0 - beta * ycb[north, 0])
        under = (gamma + delta * (xtr[1] + ycb[south, 1] * q_end)) / (1.0 - delta * ycb[south, 2])
        return above, below, coefs, [(over, q_top), (above, below), (q_end, under)]

    centre = jnp.logical_and(lane3 >= off, lane3 < off + half)
    H = CY + 4
    row = lax.broadcasted_iota(jnp.int32, (H, 1, 1), 0)
    inside = jnp.logical_and(
        jnp.logical_or(row >= 2, has_n), jnp.logical_or(row < 2 + CY, has_s)
    )
    inside = jnp.logical_and(
        inside,
        jnp.logical_and(jnp.logical_or(lane3 >= off, has_w), jnp.logical_or(lane3 < off + half, has_e)),
    )

    def planes():
        out = []
        for m in range(2):
            w, o, e = cbuf[0, m], cbuf[1, m], cbuf[2, m]
            out.append(jnp.where(centre, o, pltpu.roll(jnp.where(lane3 >= half, w, e), half, 2)))
            out.append(jnp.where(centre, pltpu.roll(o, half, 2), jnp.where(lane3 < half, w, e)))
        cx, cy, cz, cd = out
        czl = lax.broadcasted_iota(jnp.int32, (1, CZ, 1), 1)
        cyl, cy = cy[:H], cy[1:]
        cx, cz, cd = cx[1:], cz[1:], cd[1:]
        cd = jnp.where(inside, cd, 1.0)
        ct = jnp.where(czl < CZ - 1, cz, 0.0)
        cl = pltpu.roll(ct, 1, 1)
        cxl = pltpu.roll(cx, 1, 2)
        diag = cxl + cx + cyl + cy + cl + ct + cd
        return cx, cxl, cy, cyl, cl, ct, diag, RELAX / diag

    left, right = x_first()
    above, below = y_half(0, left, right)
    p_s[...] = g_s[...] + ly_s[...] * above[None] + ry_s[...] * below[None]
    for lo in range(0, Y, CH):
        hi = lo + CH
        lower = jnp.concatenate([above[None], p_s[0:hi - 1]], axis=0) if lo == 0 else p_s[lo - 1:hi - 1]
        upper = jnp.concatenate([p_s[lo + 1:Y], below[None]], axis=0) if hi == Y else p_s[lo + 1:hi + 1]
        x_source(lo, hi, lower, upper)
    left, right = x_second()
    above, below, coefs, ghosts = y_half(1, left, right)
    cx, cxl, cy, cyl, cl, ct, diag, scale = coefs
    sides = [[], [], []]
    for at in range(H):
        a, b = ghosts[0 if at < 2 else 1 if at < CY + 2 else 2]
        w = [wbuf[at, n] for n in range(8)]
        sides[0].append(w[0] * a + w[1] * b)
        sides[1].append(w[2] * a + w[3] * b)
        a1, b1, a2, b2 = pltpu.roll(a, 1, 0), pltpu.roll(b, 1, 0), pltpu.roll(a, Z - 1, 0), pltpu.roll(b, Z - 1, 0)
        sides[2].append(w[4] * a1 + w[5] * b1 + w[6] * a2 + w[7] * b2)
    partial = gathered([level_pairs(n, v) for n, v in enumerate(sides)], 0).reshape(H, CZ, X)
    to_rows(pbuf, sw.at[2], False)
    res = jnp.where(inside, partial + pbuf[...], 0.0)
    clane = lax.broadcasted_iota(jnp.int32, (CZ, X), 1)
    inner = clane % half

    def fringe(v):
        edge = jnp.zeros((CZ, X), f32)
        for r in range(CY):
            edge = jnp.where(inner >= SLOTS * r, pltpu.roll(v[r], half - off + 3 + SLOTS * r, 1), edge)
        return edge

    cor = scale * res
    for repeat in range(COARSE - 1):
        lo, n = 1 + repeat, H - 2 - 2 * repeat
        cut = slice(lo, lo + n)
        mid, over, under = cor[1:-1], cor[:-2], cor[2:]
        applied = (
            diag[cut] * mid
            - cxl[cut] * pltpu.roll(mid, 1, 2)
            - cx[cut] * pltpu.roll(mid, X - 1, 2)
            - cyl[cut] * over
            - cy[cut] * under
            - cl[cut] * pltpu.roll(mid, 1, 1)
            - ct[cut] * pltpu.roll(mid, CZ - 1, 1)
        )
        cor = jnp.where(inside[cut], mid + scale[cut] * (res[cut] - applied), 0.0)
    hj = CY // 2
    fown[0:hj] = jnp.where(lane3 < half, pltpu.roll(cor[:hj], X - off, 2), pltpu.roll(cor[hj:], off, 2))
    fown[hj] = fringe(cor)
    fbuf[gx] = fown[...]
    for i in x_peers:
        comm.send(fown, fbuf.at[gx], sf.at[gx], (i, gy))
    sedge[...] = fringe(res[2:CY + 2])
    comm.send(sedge, ebuf.at[1], sr.at[1], (west, gy), has_w)
    comm.send(sedge, ebuf.at[0], sr.at[0], (east, gy), has_e)
    above, below = above * ysc[0], below * ysc[1]
    for j in range(Y):
        op_ref[pl.ds(j, Z, stride=Y), :] = g_s[j] + ly_s[j] * above + ry_s[j] * below
    await_recv(sedge, ebuf.at[0], ssem, sr.at[0], (west, gy), has_w)
    await_recv(sedge, ebuf.at[1], ssem, sr.at[1], (east, gy), has_e)
    both = jnp.where(clane < half, ebuf[0], ebuf[1])
    for r in range(CY):
        v = pltpu.roll(both, (off - 3 - SLOTS * r) % X, 1)
        v = res[2 + r] + jnp.where(jnp.logical_or(clane == off, clane == off + half - 1), v, 0.0)
        flip[pl.ds(r, CZ, stride=CY), :] = pltpu.roll(v, X - off, 1)
    or_ref[...] = flip[0:CZ * CY, :half]
    for i in x_peers:
        await_recv(fown, fbuf.at[i], ssem, sf.at[i], (i, gy))
    nothing = jnp.zeros((CZ, X), f32)
    edges = [nothing] + [fbuf[d, hj] for d in range(nx)] + [nothing]
    spill = jnp.logical_or(clane >= X - 3, jnp.logical_and(clane >= half, clane < half + 3))
    spill2 = jnp.logical_or(clane < 3, jnp.logical_and(clane >= half - 3, clane < half))
    for t in range(nx // 2):
        u, v = fbuf[2 * t, 0:hj], fbuf[2 * t + 1, 0:hj]
        top = jnp.where(lane3 < half, u, pltpu.roll(v, half, 2))
        low = jnp.where(lane3 < half, pltpu.roll(u, half, 2), v)
        one = jnp.where(clane < half, edges[2 * t + 1], edges[2 * t + 3])
        two = jnp.where(clane < half, edges[2 * t], edges[2 * t + 2])
        base = (t + 1) * CZ * CY
        for j in range(CY):
            turn = (half - 3 - SLOTS * j) % X
            v = top[j] if j < hj else low[j - hj]
            v = v + jnp.where(spill, pltpu.roll(one, turn, 1), 0.0)
            v = v + jnp.where(spill2, pltpu.roll(two, (turn + half) % X, 1), 0.0)
            flip[pl.ds(base + j, CZ, stride=CY), :] = v
        oc_ref[:, t * X:(t + 1) * X] = flip[base:base + CZ * CY, :]
    comm.finish()


def put(*refs):
    sems = refs[6]
    give = [pltpu.make_async_copy(refs[m], refs[3 + m], sems.at[m]) for m in range(3)]
    for copy in give:
        copy.start()
    for copy in give:
        copy.wait()


def body(nx, ny, *args):
    Z, Y, X = args[0].shape
    CZ, CY = Z // 2, Y // 2
    flat = [v.reshape(Z * Y, X) for v in args]
    f32 = jnp.float32

    def vm(*shape):
        return pltpu.VMEM(shape, f32)

    block = (Y, Z, X)
    assert Y * SLOTS <= X and CY * SLOTS <= X // 2
    nsx, nsy = len(strides_of(X)), len(strides_of(Y))
    sends = 3 + (ny - 1) * 3 + (nx - 1) * 3 + 8 + 6 + 2
    dma = pltpu.SemaphoreType.DMA
    scratch = (
        [vm(*block) for _ in range(12)]
        + [vm(*block), vm(*block), vm(*block), vm(nsx, 2, *block), vm(*block), vm(*block), vm(*block), vm(nsy, 2, *block)]
        + [vm(Z, X), vm(3, Z, X), vm(Z, X), vm(2, Z, X), vm(1, Z, X)]
        + [vm(nx, Z, X), vm(Z, X), vm(nx, CZ, X), vm(2, CZ, X)]
        + [vm(ny, 3, Z, X), vm(3, Z, X), vm(2, ny, Z, X), vm(2, 2, Z, X)]
        + [vm(1, Z, X)] + [vm(nx, Z, X) for _ in range(8)] + [vm(4, Z, X)]
        + [vm(ny, Z, X) for _ in range(6)] + [vm(6, Z, X), vm(2, Z, X)]
        + [vm(3, (CY + 4) * Z, X), pltpu.VMEM((4 * X, X), jnp.bfloat16), vm(2, CY, CZ, X), vm(3, 2, CY + 5, CZ, X),
           vm(CY + 4, 8, Z, X), vm(CY + 4, CZ, X), vm(2, Z, X), vm(2, Z, X),
           vm(2, CZ, X), vm(CZ, X), vm(CY // 2 + 1, CZ, X), vm(nx, CY // 2 + 1, CZ, X), vm((nx // 2 + 1) * CZ * CY, X)]
        + [dma((sends,)), dma((3,)), dma((2, nx)), dma((ny,)), dma((2, ny)), dma((3, 3)), dma((2,)), dma((3, 2)), dma((nx,))]
        + [vm(6, Z * Y, X), dma((6,))]
    )
    p, r, c = pl.pallas_call(
        functools.partial(kernel, nx, ny),
        out_shape=(
            vm(Z * Y, X),
            vm(CZ * CY, X // 2),
            vm(CZ * CY, nx * X // 2),
        ),
        in_specs=[pl.BlockSpec(memory_space=pltpu.HBM)] * 6,
        out_specs=[pl.BlockSpec(memory_space=pltpu.VMEM)] * 3,
        scratch_shapes=scratch,
        compiler_params=pltpu.CompilerParams(
            collective_id=0, has_side_effects=True, vmem_limit_bytes=60000000
        ),
    )(*flat)
    p, r, c = pl.pallas_call(
        put,
        out_shape=tuple(jax.ShapeDtypeStruct(v.shape, f32) for v in (p, r, c)),
        in_specs=[pl.BlockSpec(memory_space=pltpu.VMEM)] * 3,
        out_specs=[pl.BlockSpec(memory_space=pltpu.HBM)] * 3,
        scratch_shapes=[dma((3,))],
    )(*[pltpu.with_memory_space_constraint(v, pltpu.VMEM) for v in (p, r, c)])
    return p.reshape(Z, Y, X), r.reshape(CZ, CY, X // 2), c.reshape(CZ, CY, nx * X // 2)


def solution(mesh):
    nx, ny = mesh.shape["gx"], mesh.shape["gy"]
    split = P(None, "gy", "gx")
    return jax.shard_map(
        functools.partial(body, nx, ny),
        mesh=mesh,
        in_specs=(split,) * 6,
        out_specs=(split, split, P(None, "gy", None)),
        check_vma=False,
    )
```

```python
import functools

import jax
import jax.numpy as jnp
from jax import lax
from jax.experimental import pallas as pl
from jax.experimental.pallas import tpu as pltpu
from jax.sharding import PartitionSpec as P

COARSE = 3
RELAX = 0.8
LE, LS, RE, RS, GS, GE, XC = range(7)
SLOTS = 8
MESH = pl.DeviceIdType.MESH


def strides_of(length):
    out, s = [], 1
    while s < length:
        out.append(s)
        s *= 2
    return out


class Comm:
    def __init__(self, send_sems):
        self.sems, self.used, self.pending = send_sems, 0, []

    def send(self, src, dst, recv, dev, cond=None):
        copy = pltpu.make_async_remote_copy(
            src_ref=src, dst_ref=dst, send_sem=self.sems.at[self.used], recv_sem=recv,
            device_id=dev, device_id_type=MESH,
        )
        self.used += 1
        self.pending.append((copy, cond))
        if cond is None:
            copy.start()
        else:
            pl.when(cond)(copy.start)

    def finish(self):
        for copy, cond in self.pending:
            if cond is None:
                copy.wait_send()
            else:
                pl.when(cond)(copy.wait_send)
        self.pending = []


def await_recv(src, dst, sems, recv, dev, cond=None):
    copy = pltpu.make_async_remote_copy(
        src_ref=src, dst_ref=dst, send_sem=sems.at[0], recv_sem=recv, device_id=dev, device_id_type=MESH
    )
    if cond is None:
        copy.wait_recv()
    else:
        pl.when(cond)(copy.wait_recv)


def farthest_first(me, n):
    out = []
    for k in range(n - 1):
        down = jnp.where(n - 1 - k > me, n - 1 - k, n - 2 - k)
        up = jnp.where(k < me, k, k + 1)
        out.append(jnp.where(2 * me < n, down, up))
    return out


def flipped(me, n):
    if n & (n - 1):
        return [lax.rem(me + o, n) for o in range(1, n)]
    out = []
    for mask in range(n - 1, 0, -1):
        peer, bit = 0, 1
        while bit < n:
            value = lax.rem(me // bit, 2)
            peer = peer + bit * (1 - value if mask & bit else value)
            bit *= 2
        out.append(peer)
    return out


def interface_factor(n, me, ls, le, rs, re, own, tau, sig, bet, tau2, sig2, dlt, kk):
    beta = jnp.zeros_like(ls[0])
    for d in range(n):
        bet[d] = beta
        w = 1.0 / (1.0 - ls[d] * beta)
        t = le[d] * w
        tau[d] = t
        s = t * beta
        sig[d] = s
        beta = re[d] + s * rs[d]
    delta = jnp.zeros_like(ls[0])
    for d in reversed(range(n)):
        dlt[d] = delta
        w = 1.0 / (1.0 - re[d] * delta)
        t = rs[d] * w
        tau2[d] = t
        s = t * delta
        sig2[d] = s
        delta = ls[d] + s * le[d]
    ls_m, le_m, rs_m, re_m = own
    beta, delta = bet[me], dlt[me]
    a, b = 1.0 - beta * ls_m, 1.0 - delta * re_m
    o1, o2 = beta * rs_m, delta * le_m
    inv = 1.0 / (a * b - o1 * o2)
    kk[0], kk[1], kk[2], kk[3] = b * inv, o1 * inv, a * inv, o2 * inv
    kk[4], kk[5] = beta, delta


def interface_solve(n, me, h_left, h_right, gs, ge, tau, tau2, kk):
    alpha = jnp.zeros_like(gs)
    for d in range(n - 1):
        alpha = jnp.where(d < me, h_left(d) + tau[d] * alpha, alpha)
    gamma = jnp.zeros_like(gs)
    for d in reversed(range(1, n)):
        gamma = jnp.where(d > me, h_right(d) + tau2[d] * gamma, gamma)
    p = alpha + kk[4] * gs
    q = gamma + kk[5] * ge
    return kk[0] * p + kk[1] * q, kk[2] * q + kk[3] * p


def chain_factor(n, me, ls, le, rs, re, xc, own, rho, tau, sig, bet, tau2, sig2, scl, dlt, kk):
    one, zero = jnp.ones_like(ls[0]), jnp.zeros_like(ls[0])
    beta = zero
    for d in range(n):
        r = zero if d == 0 else xc[d - 1]
        b = one if d == 0 else 1.0 - r * (1.0 - beta)
        rho[d], bet[d] = r, b
        w = 1.0 / (1.0 - ls[d] * b)
        t = le[d] * w
        tau[d] = t * r
        s = t * b
        sig[d] = s
        beta = re[d] + s * rs[d]
    delta = zero
    for d in reversed(range(n)):
        dlt[d] = delta
        t = rs[d] / (1.0 - re[d] * delta)
        s = t * delta
        q = ls[d] + s * le[d]
        if d > 0:
            v = 1.0 / (1.0 - q + q * xc[d - 1])
            scl[d], tau2[d], sig2[d] = v, v * t, v * s
            delta = v * q * xc[d - 1]
        else:
            scl[d], tau2[d], sig2[d] = zero, zero, zero
    ls_m, le_m, rs_m, re_m = own
    beta, delta = bet[me], dlt[me]
    a, b = 1.0 - beta * ls_m, 1.0 - delta * re_m
    o1, o2 = beta * rs_m, delta * le_m
    inv = 1.0 / (a * b - o1 * o2)
    kk[0], kk[1], kk[2], kk[3] = b * inv, o1 * inv, a * inv, o2 * inv


def kernel(nx, ny, f_hbm, p_hbm, x_hbm, y_hbm, z_hbm, d_hbm, op_ref, or_ref, oc_ref,
           xl_s, xc_s, yl_s, yc_s, zl_s, zt_s, zd_s, fo_s, p_s, r_s, g_s, q_s,
           ct_s, rt_s, gt_s, lx_s, rx_s, ix_s, wx_s, ly_s, ry_s, iy_s, wy_s,
           sx0, sy0, hx, hyd, hyu, xb, sxb, xb1, sx1, ycb, syc, yb, shy,
           xown, xrho, xtau, xsig, xbet, xtau2, xsig2, xscl, xdlt, xkk,
           ytau, ysig, ybet, ytau2, ysig2, ydlt, ykk, ysc,
           pair_s, sel_s, cown, cbuf, wbuf, pbuf, sxt, xtr, ebuf, sedge, fown, fbuf, flip,
           ssem, s0, sx, syco, sy, sc, sr, sw, sf, ins, sin):
    Y, Z, X = xc_s.shape
    CY, CZ = Y // 2, Z // 2
    f32 = jnp.float32
    gx, gy = lax.axis_index("gx"), lax.axis_index("gy")
    has_w, has_e = gx > 0, gx < nx - 1
    has_n, has_s = gy > 0, gy < ny - 1
    west, east = jnp.maximum(gx - 1, 0), jnp.minimum(gx + 1, nx - 1)
    north, south = jnp.maximum(gy - 1, 0), jnp.minimum(gy + 1, ny - 1)
    x_peers = farthest_first(gx, nx)
    y_peers = flipped(gy, ny)

    loads = []
    for m, ref in enumerate((y_hbm, p_hbm, x_hbm, z_hbm, d_hbm, f_hbm)):
        loads.append(pltpu.make_async_copy(ref, ins.at[m], sin.at[m]))
        loads[m].start()
    y_ref, p_ref, x_ref, z_ref, d_ref, f_ref = [ins.at[m] for m in range(6)]

    barrier = pltpu.get_barrier_semaphore()

    def greet(dev):
        pl.semaphore_signal(barrier, inc=1, device_id=dev, device_id_type=MESH)

    for i in x_peers:
        greet((i, gy))
    for j in y_peers:
        greet((gx, j))

    corners = [
        (jnp.logical_and(h, v), (i, j)) for h, i in ((has_w, west), (has_e, east)) for v, j in ((has_n, north), (has_s, south))
    ]
    for cond, dev in corners:
        pl.when(cond)(functools.partial(greet, dev))

    lane = lax.broadcasted_iota(jnp.int32, (Z, X), 1)
    level = lax.broadcasted_iota(jnp.int32, (Z, X), 0)
    lane3 = lax.broadcasted_iota(jnp.int32, (1, 1, X), 2)

    def rows(ref, j):
        return ref[pl.ds(j, Z, stride=Y), :]

    for m in range(2):
        loads[m].wait()
    sy0[0] = rows(y_ref, Y - 1)
    sy0[1] = rows(p_ref, Y - 1)
    sy0[2] = rows(p_ref, 0)

    n_corners = sum(cond.astype(jnp.int32) for cond, _ in corners)
    pl.semaphore_wait(barrier, (nx - 1) + (ny - 1) + n_corners)

    comm = Comm(ssem)
    comm.send(sy0.at[0:2], hyd, s0.at[1], (gx, south), has_s)
    comm.send(sy0.at[2:3], hyu, s0.at[2], (gx, north), has_n)

    loads[2].wait()
    packed = jnp.zeros((Z, X), f32)
    for j in range(Y):
        v = rows(x_ref, j)
        xc_s[j] = v
        packed = jnp.where(lane == SLOTS * j + XC, v[:, X - 1:], packed)
    sx0[...] = packed
    comm.send(sx0, hx, s0.at[0], (east, gy), has_e)

    for j in range(Y):
        yc_s[j] = rows(y_ref, j)
        p_s[j] = rows(p_ref, j)
    for m in range(3, 6):
        loads[m].wait()
    for j in range(Y):
        zv = jnp.where(level < Z - 1, rows(z_ref, j), 0.0)
        zt_s[j] = zv
        zl = pltpu.roll(zv, 1, 0)
        zl_s[j] = zl
        zd_s[j] = zv + zl + rows(d_ref, j)
        fo_s[j] = rows(f_ref, j)

    per, groups, blocks = X // Z, Y * Z // X, X // 8
    sub = lax.broadcasted_iota(jnp.int32, (8, X), 0)

    def turned(ref, g):
        return ref[g * per:(g + 1) * per].reshape(X, X).T

    def split(v):
        return [v[8 * k:8 * k + 8] for k in range(blocks)]

    def shift(v, s, fill):
        if s % 8 == 0:
            m = s // 8
            return [v[k - m] if 0 <= k - m < blocks else fill for k in range(blocks)]
        turn = [pltpu.roll(u, s % 8, 0) for u in v]
        if s > 0:
            return [jnp.where(sub < s, fill if k == 0 else turn[k - 1], turn[k]) for k in range(blocks)]
        return [jnp.where(sub >= 8 + s, fill if k == blocks - 1 else turn[k + 1], turn[k]) for k in range(blocks)]

    def scaled(u, v):
        return [a if b is None else b if a is None else a * b for a, b in zip(u, v)]

    def added(u, v):
        return [a if b is None else a + b for a, b in zip(u, v)]

    def fill_of(s, value):
        return None if s % 8 == 0 else value

    def store(ref, at, v):
        for k in range(blocks):
            ref[at + (slice(8 * k, 8 * k + 8),)] = v[k]

    def load(ref, at):
        return [ref[at + (slice(8 * k, 8 * k + 8),)] for k in range(blocks)]

    xsteps = strides_of(X)

    def x_factor(g):
        c = load(ct_s, (g,))
        a = shift(c, 1, 1.0)
        for j in range(g * per, (g + 1) * per):
            g_s[j] = yl_s[j] + yc_s[j] + zd_s[j]
        e = split(turned(g_s, g))
        for n, s in enumerate(xsteps):
            inv = [1.0 / (u + v + w) for u, v, w in zip(a, c, e)]
            ai, ci = scaled(a, inv), scaled(c, inv)
            store(wx_s, (n, 0, g), ci)
            store(wx_s, (n, 1, g), ai)
            ae, ce = scaled(ai, e), scaled(ci, e)
            a = scaled(a, shift(ai, s, fill_of(s, 1.0)))
            c = scaled(c, shift(ci, -s, fill_of(s, 1.0)))
            e = added(added(e, shift(ce, s, fill_of(s, 0.0))), shift(ae, -s, fill_of(s, 0.0)))
        inv = [1.0 / (u + v + w) for u, v, w in zip(a, c, e)]
        a, c = scaled(a, inv), scaled(c, inv)
        store(ix_s, (g,), inv)
        store(lx_s, (g,), a)
        store(rx_s, (g,), c)
        one = slice(g, g + 1)
        sxb[LE, one], sxb[LS, one] = a[-1][7:8], a[0][0:1]
        sxb[RE, one], sxb[RS, one] = c[-1][7:8], c[0][0:1]
        sxb[XC, one] = ct_s[g, X - 1:X]

    def edge_sums(g):
        r = split(turned(r_s, g))
        store(rt_s, (g,), r)
        out = []
        for ref in (lx_s, rx_s):
            v = scaled(load(ref, (g,)), r)
            while len(v) > 1:
                v = [a + b for a, b in zip(v[0::2], v[1::2])]
            out.append(jnp.sum(v[0], axis=0, keepdims=True))
        return out

    def z_terms(v, part):
        return zl_s[part] * pltpu.roll(v, 1, 1) + zt_s[part] * pltpu.roll(v, Z - 1, 1)

    def x_source(lo, hi, lower, upper):
        part = slice(lo, hi)
        r_s[part] = fo_s[part] + yl_s[part] * lower + yc_s[part] * upper + z_terms(p_s[part], part)

    for g in range(groups):
        store(ct_s, (g,), split(turned(xc_s, g)))
    yl_s[1:Y] = yc_s[0:Y - 1]
    for g in range(1, groups):
        x_factor(g)
    x_source(1, Y - 1, p_s[0:Y - 2], p_s[2:Y])

    @pl.when(jnp.logical_not(has_w))
    def _():
        hx[...] = jnp.zeros_like(hx)
        cbuf[0] = jnp.zeros_like(cbuf[0])
        ebuf[0] = jnp.zeros_like(ebuf[0])

    @pl.when(jnp.logical_not(has_e))
    def _():
        cbuf[2] = jnp.zeros_like(cbuf[2])
        ebuf[1] = jnp.zeros_like(ebuf[1])

    @pl.when(jnp.logical_not(has_n))
    def _():
        hyd[...] = jnp.zeros_like(hyd)
        wbuf[0:2] = jnp.zeros_like(wbuf[0:2])
        pbuf[0:2] = jnp.zeros_like(pbuf[0:2])
        xtr[0] = jnp.zeros_like(xtr[0])
        for d in range(3):
            cbuf[d, :, 0:3] = jnp.zeros_like(cbuf[d, :, 0:3])

    @pl.when(jnp.logical_not(has_s))
    def _():
        hyu[...] = jnp.zeros_like(hyu)
        wbuf[CY + 2:] = jnp.zeros_like(wbuf[CY + 2:])
        pbuf[CY + 2:] = jnp.zeros_like(pbuf[CY + 2:])
        xtr[1] = jnp.zeros_like(xtr[1])
        for d in range(3):
            cbuf[d, :, 3 + CY:] = jnp.zeros_like(cbuf[d, :, 3 + CY:])

    await_recv(sx0, hx, ssem, s0.at[0], (east, gy), has_w)
    await_recv(sy0.at[0:2], hyd, ssem, s0.at[1], (gx, south), has_n)
    await_recv(sy0.at[2:3], hyu, ssem, s0.at[2], (gx, north), has_s)

    yl_s[0] = hyd[0]
    x_factor(0)
    x_source(0, 1, hyd[1:2], p_s[1:2])
    x_source(Y - 1, Y, p_s[Y - 2:Y - 1], hyu[0:1])
    for g in range(groups):
        one = slice(g, g + 1)
        sxb[GS, one], sxb[GE, one] = edge_sums(g)
    xb[gx] = sxb[...]
    for i in x_peers:
        comm.send(sxb, xb.at[gx], sx.at[0, gx], (i, gy))

    for j in range(Y):
        xl_s[j] = jnp.where(lane == 0, hx[:, SLOTS * j + XC:SLOTS * j + XC + 1], pltpu.roll(xc_s[j], 1, 1))

    ysteps = strides_of(Y)
    for lo in range(0, Z, 8):
        zs = slice(lo, lo + 8)
        a = [yl_s[j, zs] for j in range(Y)]
        c = [yc_s[j, zs] for j in range(Y)]
        e = [xl_s[j, zs] + xc_s[j, zs] + zd_s[j, zs] for j in range(Y)]
        for n, s in enumerate(ysteps):
            inv = [1.0 / (a[j] + c[j] + e[j]) for j in range(Y)]
            ai, ci = [a[j] * inv[j] for j in range(Y)], [c[j] * inv[j] for j in range(Y)]
            for j in range(Y):
                if j + s < Y:
                    wy_s[n, 0, j, zs] = ci[j]
                if j >= s:
                    wy_s[n, 1, j, zs] = ai[j]
            e2 = []
            for j in range(Y):
                v = e[j]
                if j >= s:
                    v = v + ci[j - s] * e[j - s]
                if j + s < Y:
                    v = v + ai[j + s] * e[j + s]
                e2.append(v)
            a = [a[j] * ai[j - s] if j >= s else a[j] for j in range(Y)]
            c = [c[j] * ci[j + s] if j + s < Y else c[j] for j in range(Y)]
            e = e2
        for j in range(Y):
            inv = 1.0 / (a[j] + c[j] + e[j])
            iy_s[j, zs], ly_s[j, zs], ry_s[j, zs] = inv, a[j] * inv, c[j] * inv

    k_top, k_end = jnp.sqrt(yl_s[0]), jnp.sqrt(yc_s[Y - 1])
    i_top = jnp.where(has_n, 1.0 / jnp.where(has_n, k_top, 1.0), 0.0)
    ysc[0], ysc[1] = i_top, 1.0 / k_end
    syc[0], syc[1], syc[2] = ly_s[0], ly_s[Y - 1] * k_end * i_top, ry_s[Y - 1]
    ycb[gy] = syc[...]
    for j in y_peers:
        comm.send(syc, ycb.at[gy], syco.at[gy], (gx, j))

    def x_local():
        for g in range(groups):
            r = load(rt_s, (g,))
            for n, s in enumerate(xsteps):
                low = shift(scaled(load(wx_s, (n, 0, g)), r), s, fill_of(s, 0.0))
                high = shift(scaled(load(wx_s, (n, 1, g)), r), -s, fill_of(s, 0.0))
                r = added(added(r, low), high)
            store(gt_s, (g,), scaled(r, load(ix_s, (g,))))

    def y_local():
        for lo in range(0, Z, 8):
            zs = slice(lo, lo + 8)
            r = [r_s[j, zs] for j in range(Y)]
            for n, s in enumerate(ysteps):
                low = [wy_s[n, 0, j, zs] * r[j] if j + s < Y else None for j in range(Y)]
                high = [wy_s[n, 1, j, zs] * r[j] if j >= s else None for j in range(Y)]
                r2 = []
                for j in range(Y):
                    v = r[j]
                    if j >= s:
                        v = v + low[j - s]
                    if j + s < Y:
                        v = v + high[j + s]
                    r2.append(v)
                r = r2
            for j in range(Y):
                g_s[j, zs] = r[j] * iy_s[j, zs]

    x_local()

    half = X // 2
    off = half // 2
    ii = lax.broadcasted_iota(jnp.int32, (X, X), 0)
    mm = lax.broadcasted_iota(jnp.int32, (X, X), 1)

    def selection(step, start):
        target = lax.rem((ii + (step + 2)) // 2 - 1 + start + X, X)
        return jnp.where(mm == target, 0.125, 0.0)

    def level_pairs(n, levels):
        for k, v in enumerate(levels):
            pair_s[n, k * Z:(k + 1) * Z] = v
        count = len(levels) * CZ
        return pair_s[n, pl.ds(0, count, stride=2), :] + pair_s[n, pl.ds(1, count, stride=2), :]

    def pairs(n, field):
        return level_pairs(n, [field(2 * k) + field(2 * k + 1) for k in range(CY)])

    def gathered(parts, first):
        v = jnp.concatenate(parts, axis=1)
        high = v.astype(jnp.bfloat16)
        v = v - high.astype(f32)
        mid = v.astype(jnp.bfloat16)
        low = (v - mid.astype(f32)).astype(jnp.bfloat16)
        sel = sel_s[first * X:(first + len(parts)) * X]
        return sum(jnp.dot(u, sel, preferred_element_type=f32) for u in (low, mid, high))

    for n, sel in enumerate((selection(1, off), selection(-1, off), selection(0, off), selection(0, half + off))):
        sel_s[n * X:(n + 1) * X] = sel.astype(jnp.bfloat16)
    for m, (u, v) in enumerate(((lambda j: xc_s[j], lambda j: yc_s[j]), (lambda j: rows(z_ref, j), lambda j: rows(d_ref, j)))):
        part = gathered([pairs(0, u), pairs(1, v)], 2).reshape(CY, CZ, X)
        cown[m] = part
        cbuf[1, m, 3:3 + CY] = part

    for k in range(CY):
        j = 2 * k
        for n, (g, scale) in enumerate(((ly_s, ysc[0]), (ry_s, ysc[1]))):
            u, v = g[j] * scale, g[j + 1] * scale
            at = 2 + k
            wbuf[at, n] = xc_s[j] * u + xc_s[j + 1] * v
            wbuf[at, 2 + n] = xl_s[j] * u + xl_s[j + 1] * v
            wbuf[at, 4 + n] = zl_s[j] * pltpu.roll(u, 1, 0) + zl_s[j + 1] * pltpu.roll(v, 1, 0)
            wbuf[at, 6 + n] = zt_s[j] * pltpu.roll(u, Z - 1, 0) + zt_s[j + 1] * pltpu.roll(v, Z - 1, 0)

    def to_rows(buf, sems, starting):
        for n, (dev, there, here) in enumerate((((gx, north), has_n, has_s), ((gx, south), has_s, has_n))):
            src = buf.at[pl.ds(2 if n == 0 else CY, 2)]
            dst = buf.at[pl.ds(CY + 2 if n == 0 else 0, 2)]
            if starting:
                comm.send(src, dst, sems.at[n], dev, there)
            else:
                await_recv(src, dst, ssem, sems.at[n], dev, here)

    def coarse_parts(straight):
        def rows_of(slot, lo, n):
            return cbuf.at[slot, :, pl.ds(lo, n)]

        out = []
        for slot, i, ok, back in ((0, west, has_w, 2), (1, gx, None, 1), (2, east, has_e, 0)):
            both_ok = (lambda c: c) if ok is None else (lambda c, ok=ok: jnp.logical_and(c, ok))
            if straight:
                if ok is not None:
                    out.append((cown, 3, CY, 0, slot, back, (i, gy), ok, ok))
            else:
                out.append((cown.at[:, pl.ds(CY - 3, 3)], 0, 3, 1, slot, back, (i, south), both_ok(has_s), both_ok(has_n)))
                out.append((cown.at[:, pl.ds(0, 2)], 3 + CY, 2, 2, slot, back, (i, north), both_ok(has_n), both_ok(has_s)))
        return rows_of, out

    def coarse_send(straight):
        rows_of, parts = coarse_parts(straight)
        for src, lo, n, kind, slot, back, dev, ok, _ in parts:
            comm.send(src, rows_of(back, lo, n), sc.at[kind, back], dev, ok)

    def coarse_wait():
        for straight in (True, False):
            rows_of, parts = coarse_parts(straight)
            for src, lo, n, kind, slot, back, dev, _, ok in parts:
                await_recv(src, rows_of(slot, lo, n), ssem, sc.at[kind, slot], dev, ok)

    def x_solve(hl, hr, gs, ge):
        alpha = jnp.zeros((groups, X), f32)
        for d in range(nx - 1):
            alpha = jnp.where(d < gx, hl(d) + xtau[d] * alpha, alpha)
        gamma = jnp.zeros((groups, X), f32)
        for d in reversed(range(1, nx)):
            gamma = jnp.where(d > gx, hr(d) + xtau2[d] * gamma, gamma)
        p = xrho[gx] * alpha + xbet[gx] * gs
        q = gamma + xdlt[gx] * ge
        return xkk[0] * p + xkk[1] * q, xkk[2] * q + xkk[3] * p

    def x_first():
        for i in x_peers:
            await_recv(sxb, xb.at[i], ssem, sx.at[0, i], (i, gy))
        cut = [[xb[d, k] for d in range(nx)] for k in range(XC + 1)]
        own = [sxb[k] for k in range(XC + 1)]
        inv = [1.0 / v for v in cut[XC]]
        ge = [cut[GE][d] * inv[d] for d in range(nx)]
        gs = cut[GS]
        xown[0] = 1.0 / own[XC]
        chain_factor(nx, gx, cut[LS], cut[LE], cut[RS], cut[RE], cut[XC], [own[LS], own[LE], own[RS], own[RE]],
                     xrho, xtau, xsig, xbet, xtau2, xsig2, xscl, xdlt, xkk)
        return x_solve(
            lambda d: ge[d] + xsig[d] * gs[d], lambda d: xscl[d] * gs[d] + xsig2[d] * ge[d], own[GS], own[GE] * xown[0]
        )

    def x_second():
        sums = [edge_sums(g) for g in range(groups)]
        gs, ge = [jnp.concatenate([v[n] for v in sums], axis=0) for n in range(2)]
        ge = ge * xown[0]
        sx1[0], sx1[1] = ge + xsig[gx] * gs, xscl[gx] * gs + xsig2[gx] * ge
        for i in x_peers:
            comm.send(sx1.at[jnp.where(i > gx, 0, 1)], xb1.at[gx], sx.at[1, gx], (i, gy))
        coarse_send(False)
        to_rows(wbuf, sw.at[0], True)
        x_local()
        for i in x_peers:
            await_recv(sx1.at[0], xb1.at[i], ssem, sx.at[1, i], (i, gy))
        return x_solve(lambda d: xb1[d], lambda d: xb1[d], gs, ge)

    def y_half(m, left, right):
        top, end = jnp.zeros((Z, X), f32), jnp.zeros((Z, X), f32)
        for g in range(groups):
            u, w = left[g:g + 1], right[g:g + 1]
            c, v = load(ct_s, (g,)), []
            for a, b, d in zip(load(gt_s, (g,)), load(lx_s, (g,)), load(rx_s, (g,))):
                v.append(a + b * u + d * w)
            edge = u + (xrho[gx][g:g + 1] - 1.0) * v[0][0:1]
            t = added(shift(scaled(c, v), 1, edge), scaled(c, shift(v, -1, w)))
            v = jnp.concatenate(v, axis=0).T.reshape(per, Z, X)
            t = jnp.concatenate(t, axis=0).T.reshape(per, Z, X)
            for n in range(per):
                j = g * per + n
                q_s[j] = v[n]
                r = fo_s[j] + t[n] + zl_s[j] * pltpu.roll(v[n], 1, 0) + zt_s[j] * pltpu.roll(v[n], Z - 1, 0)
                r_s[j] = r
                top, end = top + ly_s[j] * r, end + ry_s[j] * r
        top, end = top * ysc[0], end * ysc[1]
        if m == 0:
            for j in y_peers:
                await_recv(syc, ycb.at[j], ssem, syco.at[j], (gx, j))
            ls, mid, re = [[ycb[d, k] for d in range(ny)] for k in range(3)]
            interface_factor(
                ny, gy, ls, mid, mid, re, [syc[0], syc[1], syc[1], syc[2]],
                ytau, ysig, ybet, ytau2, ysig2, ydlt, ykk,
            )
        shy[m, 0] = end + ysig[gy] * top
        shy[m, 1] = top + ysig2[gy] * end
        yb[m, gy] = shy[m, 0]
        for j in y_peers:
            side = jnp.where(j > gy, 0, 1)
            comm.send(shy.at[m, side], yb.at[m, gy], sy.at[m, gy], (gx, j))
        if m:
            sxt[0], sxt[1] = end, top
            comm.send(sxt.at[0], xtr.at[1], sw.at[1, 0], (gx, north), has_n)
            comm.send(sxt.at[1], xtr.at[0], sw.at[1, 1], (gx, south), has_s)
        y_local()
        if m == 0:
            coarse_send(True)
        else:
            for j in range(Y):
                r_s[j] = g_s[j] - q_s[j]
            pbuf[2:CY + 2] = gathered([
                pairs(0, lambda j: xc_s[j] * r_s[j]),
                pairs(1, lambda j: xl_s[j] * r_s[j]),
                pairs(2, lambda j: zl_s[j] * pltpu.roll(r_s[j], 1, 0) + zt_s[j] * pltpu.roll(r_s[j], Z - 1, 0)),
            ], 0).reshape(CY, CZ, X)
            to_rows(pbuf, sw.at[2], True)
            coarse_wait()
            coefs = planes()
            to_rows(wbuf, sw.at[0], False)
        for j in y_peers:
            await_recv(shy.at[m, 0], yb.at[m, j], ssem, sy.at[m, j], (gx, j))
        above, below = interface_solve(ny, gy, lambda d: yb[m, d], lambda d: yb[m, d], top, end, ytau, ytau2, ykk)
        if m == 0:
            return above * ysc[0], below * ysc[1]
        await_recv(sxt.at[0], xtr.at[1], ssem, sw.at[1, 0], (gx, north), has_s)
        await_recv(sxt.at[1], xtr.at[0], ssem, sw.at[1, 1], (gx, south), has_n)
        alpha, gamma = jnp.zeros((Z, X), f32), jnp.zeros((Z, X), f32)
        for d in range(ny - 2):
            alpha = jnp.where(d < gy - 1, yb[m, d] + ytau[d] * alpha, alpha)
        for d in reversed(range(2, ny)):
            gamma = jnp.where(d > gy + 1, yb[m, d] + ytau2[d] * gamma, gamma)
        q_top = top + syc[0] * above + syc[1] * below
        q_end = end + syc[1] * above + syc[2] * below
        beta, delta = ybet[north], ydlt[south]
        over = (alpha + beta * (xtr[0] + ycb[north, 1] * q_top)) / (1.0 - beta * ycb[north, 0])
        under = (gamma + delta * (xtr[1] + ycb[south, 1] * q_end)) / (1.0 - delta * ycb[south, 2])
        return above, below, coefs, [(over, q_top), (above, below), (q_end, under)]

    centre = jnp.logical_and(lane3 >= off, lane3 < off + half)
    H = CY + 4
    row = lax.broadcasted_iota(jnp.int32, (H, 1, 1), 0)
    inside = jnp.logical_and(
        jnp.logical_or(row >= 2, has_n), jnp.logical_or(row < 2 + CY, has_s)
    )
    inside = jnp.logical_and(
        inside,
        jnp.logical_and(jnp.logical_or(lane3 >= off, has_w), jnp.logical_or(lane3 < off + half, has_e)),
    )

    def planes():
        out = []
        for m in range(2):
            w, o, e = cbuf[0, m], cbuf[1, m], cbuf[2, m]
            out.append(jnp.where(centre, o, pltpu.roll(jnp.where(lane3 >= half, w, e), half, 2)))
            out.append(jnp.where(centre, pltpu.roll(o, half, 2), jnp.where(lane3 < half, w, e)))
        cx, cy, cz, cd = out
        czl = lax.broadcasted_iota(jnp.int32, (1, CZ, 1), 1)
        cyl, cy = cy[:H], cy[1:]
        cx, cz, cd = cx[1:], cz[1:], cd[1:]
        cd = jnp.where(inside, cd, 1.0)
        ct = jnp.where(czl < CZ - 1, cz, 0.0)
        cl = pltpu.roll(ct, 1, 1)
        cxl = pltpu.roll(cx, 1, 2)
        diag = cxl + cx + cyl + cy + cl + ct + cd
        return cx, cxl, cy, cyl, cl, ct, diag, RELAX / diag

    left, right = x_first()
    above, below = y_half(0, left, right)
    p_s[...] = g_s[...] + ly_s[...] * above[None] + ry_s[...] * below[None]
    for lo in range(0, Y, 4):
        hi = lo + 4
        lower = jnp.concatenate([above[None], p_s[0:hi - 1]], axis=0) if lo == 0 else p_s[lo - 1:hi - 1]
        upper = jnp.concatenate([p_s[lo + 1:Y], below[None]], axis=0) if hi == Y else p_s[lo + 1:hi + 1]
        x_source(lo, hi, lower, upper)
    left, right = x_second()
    above, below, coefs, ghosts = y_half(1, left, right)
    cx, cxl, cy, cyl, cl, ct, diag, scale = coefs
    sides = [[], [], []]
    for at in range(H):
        a, b = ghosts[0 if at < 2 else 1 if at < CY + 2 else 2]
        w = [wbuf[at, n] for n in range(8)]
        sides[0].append(w[0] * a + w[1] * b)
        sides[1].append(w[2] * a + w[3] * b)
        a1, b1, a2, b2 = pltpu.roll(a, 1, 0), pltpu.roll(b, 1, 0), pltpu.roll(a, Z - 1, 0), pltpu.roll(b, Z - 1, 0)
        sides[2].append(w[4] * a1 + w[5] * b1 + w[6] * a2 + w[7] * b2)
    partial = gathered([level_pairs(n, v) for n, v in enumerate(sides)], 0).reshape(H, CZ, X)
    to_rows(pbuf, sw.at[2], False)
    res = jnp.where(inside, partial + pbuf[...], 0.0)
    clane = lax.broadcasted_iota(jnp.int32, (CZ, X), 1)
    inner = clane % half

    def fringe(v):
        edge = jnp.zeros((CZ, X), f32)
        for r in range(CY):
            edge = jnp.where(inner >= SLOTS * r, pltpu.roll(v[r], half - off + 3 + SLOTS * r, 1), edge)
        return edge

    sedge[...] = fringe(res[2:CY + 2])
    comm.send(sedge, ebuf.at[1], sr.at[1], (west, gy), has_w)
    comm.send(sedge, ebuf.at[0], sr.at[0], (east, gy), has_e)
    cor = scale * res
    for repeat in range(COARSE - 1):
        lo, n = 1 + repeat, H - 2 - 2 * repeat
        cut = slice(lo, lo + n)
        mid, over, under = cor[1:-1], cor[:-2], cor[2:]
        applied = (
            diag[cut] * mid
            - cxl[cut] * pltpu.roll(mid, 1, 2)
            - cx[cut] * pltpu.roll(mid, X - 1, 2)
            - cyl[cut] * over
            - cy[cut] * under
            - cl[cut] * pltpu.roll(mid, 1, 1)
            - ct[cut] * pltpu.roll(mid, CZ - 1, 1)
        )
        cor = jnp.where(inside[cut], mid + scale[cut] * (res[cut] - applied), 0.0)
    hj = CY // 2
    fown[0:hj] = jnp.where(lane3 < half, pltpu.roll(cor[:hj], X - off, 2), pltpu.roll(cor[hj:], off, 2))
    fown[hj] = fringe(cor)
    fbuf[gx] = fown[...]
    for i in x_peers:
        comm.send(fown, fbuf.at[gx], sf.at[gx], (i, gy))
    above, below = above * ysc[0], below * ysc[1]
    for j in range(Y):
        op_ref[pl.ds(j, Z, stride=Y), :] = g_s[j] + ly_s[j] * above + ry_s[j] * below
    comm.finish()
    await_recv(sedge, ebuf.at[0], ssem, sr.at[0], (west, gy), has_w)
    await_recv(sedge, ebuf.at[1], ssem, sr.at[1], (east, gy), has_e)
    both = jnp.where(clane < half, ebuf[0], ebuf[1])
    for r in range(CY):
        v = pltpu.roll(both, (off - 3 - SLOTS * r) % X, 1)
        v = res[2 + r] + jnp.where(jnp.logical_or(clane == off, clane == off + half - 1), v, 0.0)
        flip[pl.ds(r, CZ, stride=CY), :] = pltpu.roll(v, X - off, 1)
    or_ref[...] = flip[0:CZ * CY, :half]
    for i in x_peers:
        await_recv(fown, fbuf.at[i], ssem, sf.at[i], (i, gy))
    nothing = jnp.zeros((CZ, X), f32)
    edges = [nothing] + [fbuf[d, hj] for d in range(nx)] + [nothing]
    spill = jnp.logical_or(clane >= X - 3, jnp.logical_and(clane >= half, clane < half + 3))
    spill2 = jnp.logical_or(clane < 3, jnp.logical_and(clane >= half - 3, clane < half))
    for t in range(nx // 2):
        u, v = fbuf[2 * t, 0:hj], fbuf[2 * t + 1, 0:hj]
        top = jnp.where(lane3 < half, u, pltpu.roll(v, half, 2))
        low = jnp.where(lane3 < half, pltpu.roll(u, half, 2), v)
        one = jnp.where(clane < half, edges[2 * t + 1], edges[2 * t + 3])
        two = jnp.where(clane < half, edges[2 * t], edges[2 * t + 2])
        base = (t + 1) * CZ * CY
        for j in range(CY):
            turn = (half - 3 - SLOTS * j) % X
            v = top[j] if j < hj else low[j - hj]
            v = v + jnp.where(spill, pltpu.roll(one, turn, 1), 0.0)
            v = v + jnp.where(spill2, pltpu.roll(two, (turn + half) % X, 1), 0.0)
            flip[pl.ds(base + j, CZ, stride=CY), :] = v
        oc_ref[:, t * X:(t + 1) * X] = flip[base:base + CZ * CY, :]
    comm.finish()


def put(*refs):
    sems = refs[6]
    give = [pltpu.make_async_copy(refs[m], refs[3 + m], sems.at[m]) for m in range(3)]
    for copy in give:
        copy.start()
    for copy in give:
        copy.wait()


def body(nx, ny, *args):
    Z, Y, X = args[0].shape
    CZ, CY = Z // 2, Y // 2
    flat = [v.reshape(Z * Y, X) for v in args]
    f32 = jnp.float32

    def vm(*shape):
        return pltpu.VMEM(shape, f32)

    block, square, groups = (Y, Z, X), (Y * Z // X, X, X), Y * Z // X
    assert Y * SLOTS <= X and CY * SLOTS <= X // 2 and X % Z == 0 and Y * Z % X == 0 and X % 8 == 0
    nsx, nsy = len(strides_of(X)), len(strides_of(Y))
    sends = 3 + (ny - 1) * 3 + (nx - 1) * 3 + 8 + 6 + 2
    dma = pltpu.SemaphoreType.DMA
    scratch = (
        [vm(*block) for _ in range(12)]
        + [vm(*square) for _ in range(6)] + [vm(nsx, 2, *square), vm(*block), vm(*block), vm(*block), vm(nsy, 2, *block)]
        + [vm(Z, X), vm(3, Z, X), vm(Z, X), vm(2, Z, X), vm(1, Z, X)]
        + [vm(nx, XC + 1, groups, X), vm(XC + 1, groups, X), vm(nx, groups, X), vm(2, groups, X)]
        + [vm(ny, 3, Z, X), vm(3, Z, X), vm(2, ny, Z, X), vm(2, 2, Z, X)]
        + [vm(1, groups, X)] + [vm(nx, groups, X) for _ in range(8)] + [vm(4, groups, X)]
        + [vm(ny, Z, X) for _ in range(6)] + [vm(6, Z, X), vm(2, Z, X)]
        + [vm(3, (CY + 4) * Z, X), pltpu.VMEM((4 * X, X), jnp.bfloat16), vm(2, CY, CZ, X), vm(3, 2, CY + 5, CZ, X),
           vm(CY + 4, 8, Z, X), vm(CY + 4, CZ, X), vm(2, Z, X), vm(2, Z, X),
           vm(2, CZ, X), vm(CZ, X), vm(CY // 2 + 1, CZ, X), vm(nx, CY // 2 + 1, CZ, X), vm((nx // 2 + 1) * CZ * CY, X)]
        + [dma((sends,)), dma((3,)), dma((2, nx)), dma((ny,)), dma((2, ny)), dma((3, 3)), dma((2,)), dma((3, 2)), dma((nx,))]
        + [vm(6, Z * Y, X), dma((6,))]
    )
    p, r, c = pl.pallas_call(
        functools.partial(kernel, nx, ny),
        out_shape=(
            vm(Z * Y, X),
            vm(CZ * CY, X // 2),
            vm(CZ * CY, nx * X // 2),
        ),
        in_specs=[pl.BlockSpec(memory_space=pltpu.HBM)] * 6,
        out_specs=[pl.BlockSpec(memory_space=pltpu.VMEM)] * 3,
        scratch_shapes=scratch,
        compiler_params=pltpu.CompilerParams(
            collective_id=0, has_side_effects=True, vmem_limit_bytes=60000000
        ),
    )(*flat)
    p, r, c = pl.pallas_call(
        put,
        out_shape=tuple(jax.ShapeDtypeStruct(v.shape, f32) for v in (p, r, c)),
        in_specs=[pl.BlockSpec(memory_space=pltpu.VMEM)] * 3,
        out_specs=[pl.BlockSpec(memory_space=pltpu.HBM)] * 3,
        scratch_shapes=[dma((3,))],
    )(*[pltpu.with_memory_space_constraint(v, pltpu.VMEM) for v in (p, r, c)])
    return p.reshape(Z, Y, X), r.reshape(CZ, CY, X // 2), c.reshape(CZ, CY, nx * X // 2)


def solution(mesh):
    nx, ny = mesh.shape["gx"], mesh.shape["gy"]
    split = P(None, "gy", "gx")
    return jax.shard_map(
        functools.partial(body, nx, ny),
        mesh=mesh,
        in_specs=(split,) * 6,
        out_specs=(split, split, P(None, "gy", None)),
        check_vma=False,
    )
```

```python
import functools

import jax
import jax.numpy as jnp
from jax import lax
from jax.experimental import pallas as pl
from jax.experimental.pallas import tpu as pltpu
from jax.sharding import PartitionSpec as P

COARSE = 3
RELAX = 0.8
LE, LS, RE, RS, GS, GE, XC = range(7)
SLOTS = 8
EDGE = 4
MESH = pl.DeviceIdType.MESH


def strides_of(length):
    out, s = [], 1
    while s < length:
        out.append(s)
        s *= 2
    return out


class Comm:
    def __init__(self, send_sems):
        self.sems, self.used, self.pending = send_sems, 0, []

    def copy(self, src, dst, sem, recv, dev):
        return pltpu.make_async_remote_copy(
            src_ref=src, dst_ref=dst, send_sem=sem, recv_sem=recv, device_id=dev, device_id_type=MESH
        )

    def send(self, src, dst, recv, dev, cond=None):
        copy = self.copy(src, dst, self.sems.at[self.used], recv, dev)
        self.used += 1
        self.pending.append((copy, cond))
        if cond is None:
            copy.start()
        else:
            pl.when(cond)(copy.start)

    def send_all(self, src, dst, recv, devs, received):
        sem = self.sems.at[self.used]
        self.used += 1
        for dev in devs:
            self.copy(src(dev), dst, sem, recv, dev).start()
        self.pending.append((self.copy(received, received, sem, recv, devs[0]), None))

    def finish(self):
        for copy, cond in self.pending:
            if cond is None:
                copy.wait_send()
            else:
                pl.when(cond)(copy.wait_send)
        self.used, self.pending = 0, []


def await_recv(src, dst, sems, recv, dev, cond=None):
    copy = pltpu.make_async_remote_copy(
        src_ref=src, dst_ref=dst, send_sem=sems.at[0], recv_sem=recv, device_id=dev, device_id_type=MESH
    )
    if cond is None:
        copy.wait_recv()
    else:
        pl.when(cond)(copy.wait_recv)


def await_all(part, recv, dev):
    pltpu.make_async_remote_copy(
        src_ref=part, dst_ref=part, send_sem=recv, recv_sem=recv, device_id=dev, device_id_type=MESH
    ).wait_recv()


def farthest_first(me, n):
    out = []
    for k in range(n - 1):
        down = jnp.where(n - 1 - k > me, n - 1 - k, n - 2 - k)
        up = jnp.where(k < me, k, k + 1)
        out.append(jnp.where(2 * me < n, down, up))
    return out


def flipped(me, n):
    if n & (n - 1):
        return [lax.rem(me + o, n) for o in range(1, n)]
    def peer_of(mask):
        peer, bit = 0, 1
        while bit < n:
            value = lax.rem(me // bit, 2)
            peer = peer + bit * (1 - value if mask & bit else value)
            bit *= 2
        return peer

    masks = list(range(n - 1, 0, -1))
    even, odd = [m for m in masks if m % 2 == 0], [m for m in masks if m % 2]
    first = lax.rem(me, 2) == 0
    return [jnp.where(first, peer_of(a), peer_of(b)) for a, b in zip(even + odd, odd + even)]


def interface_factor(n, me, ls, le, rs, re, own, tau, sig, bet, tau2, sig2, dlt, kk):
    beta = jnp.zeros_like(ls[0])
    for d in range(n):
        bet[d] = beta
        w = 1.0 / (1.0 - ls[d] * beta)
        t = le[d] * w
        tau[d] = t
        s = t * beta
        sig[d] = s
        beta = re[d] + s * rs[d]
    delta = jnp.zeros_like(ls[0])
    for d in reversed(range(n)):
        dlt[d] = delta
        w = 1.0 / (1.0 - re[d] * delta)
        t = rs[d] * w
        tau2[d] = t
        s = t * delta
        sig2[d] = s
        delta = ls[d] + s * le[d]
    ls_m, le_m, rs_m, re_m = own
    beta, delta = bet[me], dlt[me]
    a, b = 1.0 - beta * ls_m, 1.0 - delta * re_m
    o1, o2 = beta * rs_m, delta * le_m
    inv = 1.0 / (a * b - o1 * o2)
    kk[0], kk[1], kk[2], kk[3] = b * inv, o1 * inv, a * inv, o2 * inv
    kk[4], kk[5] = beta, delta


def interface_solve(n, me, h_left, h_right, gs, ge, tau, tau2, kk):
    alpha = jnp.zeros_like(gs)
    for d in range(n - 1):
        alpha = jnp.where(d < me, h_left(d) + tau[d] * alpha, alpha)
    gamma = jnp.zeros_like(gs)
    for d in reversed(range(1, n)):
        gamma = jnp.where(d > me, h_right(d) + tau2[d] * gamma, gamma)
    p = alpha + kk[4] * gs
    q = gamma + kk[5] * ge
    return kk[0] * p + kk[1] * q, kk[2] * q + kk[3] * p


def chain_factor(n, me, ls, le, rs, re, xc, own, rho, tau, sig, bet, tau2, sig2, scl, dlt, kk):
    one, zero = jnp.ones_like(ls[0]), jnp.zeros_like(ls[0])
    beta = zero
    for d in range(n):
        r = zero if d == 0 else xc[d - 1]
        b = one if d == 0 else 1.0 - r * (1.0 - beta)
        rho[d], bet[d] = r, b
        w = 1.0 / (1.0 - ls[d] * b)
        t = le[d] * w
        tau[d] = t * r
        s = t * b
        sig[d] = s
        beta = re[d] + s * rs[d]
    delta = zero
    for d in reversed(range(n)):
        dlt[d] = delta
        t = rs[d] / (1.0 - re[d] * delta)
        s = t * delta
        q = ls[d] + s * le[d]
        if d > 0:
            v = 1.0 / (1.0 - q + q * xc[d - 1])
            scl[d], tau2[d], sig2[d] = v, v * t, v * s
            delta = v * q * xc[d - 1]
        else:
            scl[d], tau2[d], sig2[d] = zero, zero, zero
    ls_m, le_m, rs_m, re_m = own
    beta, delta = bet[me], dlt[me]
    a, b = 1.0 - beta * ls_m, 1.0 - delta * re_m
    o1, o2 = beta * rs_m, delta * le_m
    inv = 1.0 / (a * b - o1 * o2)
    kk[0], kk[1], kk[2], kk[3] = b * inv, o1 * inv, a * inv, o2 * inv


def kernel(nx, ny, f_hbm, p_hbm, x_hbm, y_hbm, z_hbm, d_hbm, op_ref, or_ref, oc_ref,
           xl_s, xc_s, yl_s, yc_s, zl_s, zt_s, zd_s, fo_s, p_s, r_s, g_s, q_s,
           ct_s, rt_s, gt_s, lx_s, rx_s, ix_s, wx_s, ly_s, ry_s, iy_s, wy_s,
           sx0, sy0, hx, hyd, hyu, xb, sxb, xb1, sx1, ycb, syc, yb0, yb1, shy,
           xown, xrho, xtau, xsig, xbet, xtau2, xsig2, xscl, xdlt, xkk,
           ytau, ysig, ybet, ytau2, ysig2, ydlt, ykk, ysc,
           pair_s, sel_s, cown, cbuf, wbuf, elr, nbr, pbuf, sxt, xtr, ebuf, sedge, fown, fbuf, flip,
           ssem, s0, sx, sy, sc, sr, sw, sf, ins, sin):
    Y, Z, X = xc_s.shape
    CY, CZ = Y // 2, Z // 2
    f32 = jnp.float32
    gx, gy = lax.axis_index("gx"), lax.axis_index("gy")
    has_w, has_e = gx > 0, gx < nx - 1
    has_n, has_s = gy > 0, gy < ny - 1
    west, east = jnp.maximum(gx - 1, 0), jnp.minimum(gx + 1, nx - 1)
    north, south = jnp.maximum(gy - 1, 0), jnp.minimum(gy + 1, ny - 1)
    x_peers = [(i, gy) for i in farthest_first(gx, nx)]
    y_peers = [(gx, j) for j in flipped(gy, ny)]

    stages = ((0, 2), (2, 3), (3, 6))
    sources = (y_hbm, p_hbm, x_hbm, z_hbm, d_hbm, f_hbm)
    for n, (lo, hi) in enumerate(stages):
        for m in range(lo, hi):
            pltpu.make_async_copy(sources[m], ins.at[m], sin.at[n]).start()

    def loaded(n):
        part = ins.at[pl.ds(stages[n][0], stages[n][1] - stages[n][0])]
        pltpu.make_async_copy(part, part, sin.at[n]).wait()

    y_ref, p_ref, x_ref, z_ref, d_ref, f_ref = [ins.at[m] for m in range(6)]

    barrier = pltpu.get_barrier_semaphore()

    def greet(dev):
        pl.semaphore_signal(barrier, inc=1, device_id=dev, device_id_type=MESH)

    for dev in x_peers + y_peers:
        greet(dev)

    corners = [
        (jnp.logical_and(h, v), (i, j)) for h, i in ((has_w, west), (has_e, east)) for v, j in ((has_n, north), (has_s, south))
    ]
    for cond, dev in corners:
        pl.when(cond)(functools.partial(greet, dev))

    lane = lax.broadcasted_iota(jnp.int32, (Z, X), 1)
    level = lax.broadcasted_iota(jnp.int32, (Z, X), 0)
    lane3 = lax.broadcasted_iota(jnp.int32, (1, 1, X), 2)

    def rows(ref, j):
        return ref[pl.ds(j, Z, stride=Y), :]

    loaded(0)
    sy0[0] = rows(y_ref, Y - 1)
    sy0[1] = rows(p_ref, Y - 1)
    sy0[2] = rows(p_ref, 0)

    n_corners = sum(cond.astype(jnp.int32) for cond, _ in corners)
    pl.semaphore_wait(barrier, (nx - 1) + (ny - 1) + n_corners)

    comm = Comm(ssem)
    comm.send(sy0.at[0:2], hyd, s0.at[1], (gx, south), has_s)
    comm.send(sy0.at[2:3], hyu, s0.at[2], (gx, north), has_n)

    loaded(1)
    packed = jnp.zeros((Z, X), f32)
    for j in range(Y):
        v = rows(x_ref, j)
        xc_s[j] = v
        packed = jnp.where(lane == SLOTS * j + XC, v[:, X - 1:], packed)
    sx0[...] = packed
    comm.send(sx0, hx, s0.at[0], (east, gy), has_e)

    for j in range(Y):
        yc_s[j] = rows(y_ref, j)
        p_s[j] = rows(p_ref, j)
    loaded(2)
    for j in range(Y):
        zv = jnp.where(level < Z - 1, rows(z_ref, j), 0.0)
        zt_s[j] = zv
        zl = pltpu.roll(zv, 1, 0)
        zl_s[j] = zl
        zd_s[j] = zv + zl + rows(d_ref, j)
        fo_s[j] = rows(f_ref, j)

    to_sides = (((gx, south), has_s, has_n), ((gx, north), has_n, has_s))
    for n, (dev, there, _) in enumerate(to_sides):
        for k, ref in enumerate((xc_s, zt_s)):
            src = ref.at[pl.ds(0 if n else Y - EDGE, EDGE)]
            comm.send(src, nbr.at[n, pl.ds(k * EDGE, EDGE)], sw.at[0, n], dev, there)

    per, groups, blocks = X // Z, Y * Z // X, X // 8
    sub = lax.broadcasted_iota(jnp.int32, (8, X), 0)

    def turned(ref, g):
        return ref[g * per:(g + 1) * per].reshape(X, X).T

    def split(v):
        return [v[8 * k:8 * k + 8] for k in range(blocks)]

    def shift(v, s, fill):
        if s % 8 == 0:
            m = s // 8
            return [v[k - m] if 0 <= k - m < blocks else fill for k in range(blocks)]
        turn = [pltpu.roll(u, s % 8, 0) for u in v]
        if s > 0:
            return [jnp.where(sub < s, fill if k == 0 else turn[k - 1], turn[k]) for k in range(blocks)]
        return [jnp.where(sub >= 8 + s, fill if k == blocks - 1 else turn[k + 1], turn[k]) for k in range(blocks)]

    def scaled(u, v):
        return [a if b is None else b if a is None else a * b for a, b in zip(u, v)]

    def added(u, v):
        return [a if b is None else a + b for a, b in zip(u, v)]

    def fill_of(s, value):
        return None if s % 8 == 0 else value

    def store(ref, at, v):
        for k in range(blocks):
            ref[at + (slice(8 * k, 8 * k + 8),)] = v[k]

    def load(ref, at):
        return [ref[at + (slice(8 * k, 8 * k + 8),)] for k in range(blocks)]

    xsteps = strides_of(X)

    def x_factor(g):
        c = load(ct_s, (g,))
        a = shift(c, 1, 1.0)
        for j in range(g * per, (g + 1) * per):
            g_s[j] = yl_s[j] + yc_s[j] + zd_s[j]
        e = split(turned(g_s, g))
        for n, s in enumerate(xsteps):
            inv = [1.0 / (u + v + w) for u, v, w in zip(a, c, e)]
            ai, ci = scaled(a, inv), scaled(c, inv)
            store(wx_s, (n, 0, g), ci)
            store(wx_s, (n, 1, g), ai)
            ae, ce = scaled(ai, e), scaled(ci, e)
            a = scaled(a, shift(ai, s, fill_of(s, 1.0)))
            c = scaled(c, shift(ci, -s, fill_of(s, 1.0)))
            e = added(added(e, shift(ce, s, fill_of(s, 0.0))), shift(ae, -s, fill_of(s, 0.0)))
        inv = [1.0 / (u + v + w) for u, v, w in zip(a, c, e)]
        a, c = scaled(a, inv), scaled(c, inv)
        store(ix_s, (g,), inv)
        store(lx_s, (g,), a)
        store(rx_s, (g,), c)
        one = slice(g, g + 1)
        sxb[LE, one], sxb[LS, one] = a[-1][7:8], a[0][0:1]
        sxb[RE, one], sxb[RS, one] = c[-1][7:8], c[0][0:1]
        sxb[XC, one] = ct_s[g, X - 1:X]

    def edge_sums(g):
        r = split(turned(r_s, g))
        store(rt_s, (g,), r)
        out = []
        for ref in (lx_s, rx_s):
            v = scaled(load(ref, (g,)), r)
            while len(v) > 1:
                v = [a + b for a, b in zip(v[0::2], v[1::2])]
            out.append(jnp.sum(v[0], axis=0, keepdims=True))
        return out

    def z_terms(v, part):
        return zl_s[part] * pltpu.roll(v, 1, 1) + zt_s[part] * pltpu.roll(v, Z - 1, 1)

    def x_source(lo, hi, lower, upper):
        part = slice(lo, hi)
        r_s[part] = fo_s[part] + yl_s[part] * lower + yc_s[part] * upper + z_terms(p_s[part], part)

    for g in range(groups):
        store(ct_s, (g,), split(turned(xc_s, g)))
    yl_s[1:Y] = yc_s[0:Y - 1]
    for g in range(1, groups):
        x_factor(g)
    x_source(1, Y - 1, p_s[0:Y - 2], p_s[2:Y])

    @pl.when(jnp.logical_not(has_w))
    def _():
        hx[...] = jnp.zeros_like(hx)
        cbuf[0] = jnp.zeros_like(cbuf[0])
        ebuf[0] = jnp.zeros_like(ebuf[0])

    @pl.when(jnp.logical_not(has_e))
    def _():
        cbuf[2] = jnp.zeros_like(cbuf[2])
        ebuf[1] = jnp.zeros_like(ebuf[1])

    @pl.when(jnp.logical_not(has_n))
    def _():
        hyd[...] = jnp.zeros_like(hyd)
        nbr[0] = jnp.zeros_like(nbr[0])
        pbuf[0:2] = jnp.zeros_like(pbuf[0:2])
        xtr[0] = jnp.zeros_like(xtr[0])
        for d in range(3):
            cbuf[d, :, 0:3] = jnp.zeros_like(cbuf[d, :, 0:3])

    @pl.when(jnp.logical_not(has_s))
    def _():
        hyu[...] = jnp.zeros_like(hyu)
        nbr[1] = jnp.zeros_like(nbr[1])
        pbuf[CY + 2:] = jnp.zeros_like(pbuf[CY + 2:])
        xtr[1] = jnp.zeros_like(xtr[1])
        for d in range(3):
            cbuf[d, :, 3 + CY:] = jnp.zeros_like(cbuf[d, :, 3 + CY:])

    await_recv(sy0.at[0:2], hyd, ssem, s0.at[1], (gx, south), has_n)
    await_recv(sy0.at[2:3], hyu, ssem, s0.at[2], (gx, north), has_s)

    yl_s[0] = hyd[0]
    x_factor(0)
    x_source(0, 1, hyd[1:2], p_s[1:2])
    x_source(Y - 1, Y, p_s[Y - 2:Y - 1], hyu[0:1])
    for g in range(groups):
        one = slice(g, g + 1)
        sxb[GS, one], sxb[GE, one] = edge_sums(g)
    xb[gx] = sxb[...]
    comm.send_all(lambda dev: sxb, xb.at[gx], sx.at[0], x_peers, xb.at[pl.ds(0, nx - 1)])

    await_recv(sx0, hx, ssem, s0.at[0], (east, gy), has_w)
    for j in range(Y):
        xl_s[j] = jnp.where(lane == 0, hx[:, SLOTS * j + XC:SLOTS * j + XC + 1], pltpu.roll(xc_s[j], 1, 1))

    ysteps = strides_of(Y)
    for lo in range(0, Z, 8):
        zs = slice(lo, lo + 8)
        a = [yl_s[j, zs] for j in range(Y)]
        c = [yc_s[j, zs] for j in range(Y)]
        e = [xl_s[j, zs] + xc_s[j, zs] + zd_s[j, zs] for j in range(Y)]
        for n, s in enumerate(ysteps):
            inv = [1.0 / (a[j] + c[j] + e[j]) for j in range(Y)]
            ai, ci = [a[j] * inv[j] for j in range(Y)], [c[j] * inv[j] for j in range(Y)]
            for j in range(Y):
                if j + s < Y:
                    wy_s[n, 0, j, zs] = ci[j]
                if j >= s:
                    wy_s[n, 1, j, zs] = ai[j]
            e2 = []
            for j in range(Y):
                v = e[j]
                if j >= s:
                    v = v + ci[j - s] * e[j - s]
                if j + s < Y:
                    v = v + ai[j + s] * e[j + s]
                e2.append(v)
            a = [a[j] * ai[j - s] if j >= s else a[j] for j in range(Y)]
            c = [c[j] * ci[j + s] if j + s < Y else c[j] for j in range(Y)]
            e = e2
        for j in range(Y):
            inv = 1.0 / (a[j] + c[j] + e[j])
            iy_s[j, zs], ly_s[j, zs], ry_s[j, zs] = inv, a[j] * inv, c[j] * inv

    k_top, k_end = jnp.sqrt(yl_s[0]), jnp.sqrt(yc_s[Y - 1])
    i_top = jnp.where(has_n, 1.0 / jnp.where(has_n, k_top, 1.0), 0.0)
    ysc[0], ysc[1] = i_top, 1.0 / k_end
    syc[0], syc[1], syc[2] = ly_s[0], ly_s[Y - 1] * k_end * i_top, ry_s[Y - 1]
    ycb[gy] = syc[...]
    comm.send_all(lambda dev: syc, ycb.at[gy], sy.at[2], y_peers, ycb.at[pl.ds(0, ny - 1)])

    def x_local():
        for g in range(groups):
            r = load(rt_s, (g,))
            for n, s in enumerate(xsteps):
                low = shift(scaled(load(wx_s, (n, 0, g)), r), s, fill_of(s, 0.0))
                high = shift(scaled(load(wx_s, (n, 1, g)), r), -s, fill_of(s, 0.0))
                r = added(added(r, low), high)
            store(gt_s, (g,), scaled(r, load(ix_s, (g,))))

    def y_local():
        for lo in range(0, Z, 8):
            zs = slice(lo, lo + 8)
            r = [r_s[j, zs] for j in range(Y)]
            for n, s in enumerate(ysteps):
                low = [wy_s[n, 0, j, zs] * r[j] if j + s < Y else None for j in range(Y)]
                high = [wy_s[n, 1, j, zs] * r[j] if j >= s else None for j in range(Y)]
                r2 = []
                for j in range(Y):
                    v = r[j]
                    if j >= s:
                        v = v + low[j - s]
                    if j + s < Y:
                        v = v + high[j + s]
                    r2.append(v)
                r = r2
            for j in range(Y):
                g_s[j, zs] = r[j] * iy_s[j, zs]

    x_local()

    half = X // 2
    off = half // 2
    ii = lax.broadcasted_iota(jnp.int32, (X, X), 0)
    mm = lax.broadcasted_iota(jnp.int32, (X, X), 1)

    def selection(step, start):
        target = lax.rem((ii + (step + 2)) // 2 - 1 + start + X, X)
        return jnp.where(mm == target, 0.125, 0.0)

    def level_pairs(n, levels):
        for k, v in enumerate(levels):
            pair_s[n, k * Z:(k + 1) * Z] = v
        count = len(levels) * CZ
        return pair_s[n, pl.ds(0, count, stride=2), :] + pair_s[n, pl.ds(1, count, stride=2), :]

    def pairs(n, field):
        return level_pairs(n, [field(2 * k) + field(2 * k + 1) for k in range(CY)])

    def gathered(parts, first):
        v = jnp.concatenate(parts, axis=1)
        high = v.astype(jnp.bfloat16)
        v = v - high.astype(f32)
        mid = v.astype(jnp.bfloat16)
        low = (v - mid.astype(f32)).astype(jnp.bfloat16)
        sel = sel_s[first * X:(first + len(parts)) * X]
        return sum(jnp.dot(u, sel, preferred_element_type=f32) for u in (low, mid, high))

    for n, sel in enumerate((selection(1, off), selection(-1, off), selection(0, off), selection(0, half + off))):
        sel_s[n * X:(n + 1) * X] = sel.astype(jnp.bfloat16)
    for m, (u, v) in enumerate(((lambda j: xc_s[j], lambda j: yc_s[j]), (lambda j: rows(z_ref, j), lambda j: rows(d_ref, j)))):
        part = gathered([pairs(0, u), pairs(1, v)], 2).reshape(CY, CZ, X)
        cown[m] = part
        cbuf[1, m, 3:3 + CY] = part

    def operator(at, xc, xl, zl, zt, sides):
        for n, (u, v) in enumerate(sides):
            wbuf[at, n] = xc[0] * u + xc[1] * v
            wbuf[at, 2 + n] = xl[0] * u + xl[1] * v
            wbuf[at, 4 + n] = zl[0] * pltpu.roll(u, 1, 0) + zl[1] * pltpu.roll(v, 1, 0)
            wbuf[at, 6 + n] = zt[0] * pltpu.roll(u, Z - 1, 0) + zt[1] * pltpu.roll(v, Z - 1, 0)

    for k in range(EDGE):
        for n, j in enumerate((Y - EDGE + k, k)):
            elr[n, k], elr[n, EDGE + k] = ly_s[j] * ysc[0], ry_s[j] * ysc[1]
    for n in range(2):
        elr[n, 2 * EDGE] = hx[...]
    for k in range(CY):
        two = (2 * k, 2 * k + 1)
        operator(2 + k, *[[ref[j] for j in two] for ref in (xc_s, xl_s, zl_s, zt_s)],
                 [[ref[j] * ysc[n] for j in two] for n, ref in enumerate((ly_s, ry_s))])

    def edge_columns():
        for n, (dev, there, _) in enumerate(to_sides):
            comm.send(elr.at[n], nbr.at[n, pl.ds(2 * EDGE, 2 * EDGE + 1)], sw.at[0, n], dev, there)

    def edge_operators():
        for n, (dev, _, here) in enumerate(to_sides):
            await_recv(nbr.at[n], nbr.at[n], ssem, sw.at[0, n], dev, here)
        for n, first in enumerate((Y - EDGE, 0)):
            for k in range(0, EDGE, 2):
                xc = [nbr[n, k + i] for i in range(2)]
                zt = [nbr[n, EDGE + k + i] for i in range(2)]
                cols = [SLOTS * (first + k + i) + XC for i in range(2)]
                xl = [jnp.where(lane == 0, nbr[n, 4 * EDGE, :, c:c + 1], pltpu.roll(v, 1, 1)) for c, v in zip(cols, xc)]
                operator(n * (CY + 2) + k // 2, xc, xl, [pltpu.roll(v, 1, 0) for v in zt], zt,
                         [[nbr[n, (2 + m) * EDGE + k + i] for i in range(2)] for m in range(2)])

    def to_rows(buf, sems, starting):
        for n, (dev, there, here) in enumerate((((gx, north), has_n, has_s), ((gx, south), has_s, has_n))):
            src = buf.at[pl.ds(2 if n == 0 else CY, 2)]
            dst = buf.at[pl.ds(CY + 2 if n == 0 else 0, 2)]
            if starting:
                comm.send(src, dst, sems.at[n], dev, there)
            else:
                await_recv(src, dst, ssem, sems.at[n], dev, here)

    def coarse_send(straight):
        for i, ok, back in ((west, has_w, 2), (gx, None, 1), (east, has_e, 0)):
            both = (lambda c: c) if ok is None else (lambda c, ok=ok: jnp.logical_and(c, ok))
            if straight:
                if ok is not None:
                    comm.send(cown, cbuf.at[back, :, pl.ds(3, CY)], sc.at[back], (i, gy), ok)
            else:
                comm.send(cown.at[:, pl.ds(CY - 3, 3)], cbuf.at[back, :, pl.ds(0, 3)], sc.at[back], (i, south), both(has_s))
                comm.send(cown.at[:, pl.ds(0, 2)], cbuf.at[back, :, pl.ds(3 + CY, 2)], sc.at[back], (i, north), both(has_n))

    def coarse_wait():
        for slot, i, ok in ((0, west, has_w), (1, gx, None), (2, east, has_e)):
            kept = 0 if ok is None else CY
            for n, s in ((True, True), (True, False), (False, True)):
                cond = jnp.logical_and(has_n if n else jnp.logical_not(has_n), has_s if s else jnp.logical_not(has_s))
                cond = cond if ok is None else jnp.logical_and(cond, ok)
                part = cbuf.at[slot, :, pl.ds(0, kept + (3 if n else 0) + (2 if s else 0))]
                await_recv(part, part, ssem, sc.at[slot], (i, gy), cond)

    def x_solve(hl, hr, gs, ge):
        alpha = jnp.zeros((groups, X), f32)
        for d in range(nx - 1):
            alpha = jnp.where(d < gx, hl(d) + xtau[d] * alpha, alpha)
        gamma = jnp.zeros((groups, X), f32)
        for d in reversed(range(1, nx)):
            gamma = jnp.where(d > gx, hr(d) + xtau2[d] * gamma, gamma)
        p = xrho[gx] * alpha + xbet[gx] * gs
        q = gamma + xdlt[gx] * ge
        return xkk[0] * p + xkk[1] * q, xkk[2] * q + xkk[3] * p

    def x_first():
        await_all(xb.at[pl.ds(0, nx - 1)], sx.at[0], x_peers[0])
        cut = [[xb[d, k] for d in range(nx)] for k in range(XC + 1)]
        own = [sxb[k] for k in range(XC + 1)]
        inv = [1.0 / v for v in cut[XC]]
        ge = [cut[GE][d] * inv[d] for d in range(nx)]
        gs = cut[GS]
        xown[0] = 1.0 / own[XC]
        chain_factor(nx, gx, cut[LS], cut[LE], cut[RS], cut[RE], cut[XC], [own[LS], own[LE], own[RS], own[RE]],
                     xrho, xtau, xsig, xbet, xtau2, xsig2, xscl, xdlt, xkk)
        return x_solve(
            lambda d: ge[d] + xsig[d] * gs[d], lambda d: xscl[d] * gs[d] + xsig2[d] * ge[d], own[GS], own[GE] * xown[0]
        )

    def x_second():
        sums = [edge_sums(g) for g in range(groups)]
        gs, ge = [jnp.concatenate([v[n] for v in sums], axis=0) for n in range(2)]
        ge = ge * xown[0]
        sx1[0], sx1[1] = ge + xsig[gx] * gs, xscl[gx] * gs + xsig2[gx] * ge
        comm.send_all(
            lambda dev: sx1.at[jnp.where(dev[0] > gx, 0, 1)], xb1.at[gx], sx.at[1], x_peers, xb1.at[pl.ds(0, nx - 1)]
        )
        coarse_send(False)
        edge_columns()
        x_local()
        await_all(xb1.at[pl.ds(0, nx - 1)], sx.at[1], x_peers[0])
        return x_solve(lambda d: xb1[d], lambda d: xb1[d], gs, ge)

    def y_half(m, left, right):
        top, end = jnp.zeros((Z, X), f32), jnp.zeros((Z, X), f32)
        for g in range(groups):
            u, w = left[g:g + 1], right[g:g + 1]
            c, v = load(ct_s, (g,)), []
            for a, b, d in zip(load(gt_s, (g,)), load(lx_s, (g,)), load(rx_s, (g,))):
                v.append(a + b * u + d * w)
            edge = u + (xrho[gx][g:g + 1] - 1.0) * v[0][0:1]
            t = added(shift(scaled(c, v), 1, edge), scaled(c, shift(v, -1, w)))
            v = jnp.concatenate(v, axis=0).T.reshape(per, Z, X)
            t = jnp.concatenate(t, axis=0).T.reshape(per, Z, X)
            for n in range(per):
                j = g * per + n
                q_s[j] = v[n]
                r = fo_s[j] + t[n] + zl_s[j] * pltpu.roll(v[n], 1, 0) + zt_s[j] * pltpu.roll(v[n], Z - 1, 0)
                r_s[j] = r
                top, end = top + ly_s[j] * r, end + ry_s[j] * r
        top, end = top * ysc[0], end * ysc[1]
        if m == 0:
            shy[0, 0], shy[0, 1] = top, end
            yb0[gy] = shy[0]
            comm.send_all(lambda dev: shy.at[0], yb0.at[gy], sy.at[0], y_peers, yb0.at[pl.ds(0, ny - 1)])
        else:
            shy[1, 0] = end + ysig[gy] * top
            shy[1, 1] = top + ysig2[gy] * end
            yb1[gy] = shy[1, 0]
            comm.send_all(
                lambda dev: shy.at[1, jnp.where(dev[1] > gy, 0, 1)], yb1.at[gy], sy.at[1], y_peers, yb1.at[pl.ds(0, ny - 1)]
            )
        if m:
            sxt[0], sxt[1] = end, top
            comm.send(sxt.at[0], xtr.at[1], sw.at[1, 0], (gx, north), has_n)
            comm.send(sxt.at[1], xtr.at[0], sw.at[1, 1], (gx, south), has_s)
        y_local()
        if m == 0:
            coarse_send(True)
            await_all(ycb.at[pl.ds(0, ny - 1)], sy.at[2], y_peers[0])
            ls, mid, re = [[ycb[d, k] for d in range(ny)] for k in range(3)]
            interface_factor(
                ny, gy, ls, mid, mid, re, [syc[0], syc[1], syc[1], syc[2]],
                ytau, ysig, ybet, ytau2, ysig2, ydlt, ykk,
            )
            comm.finish()
            await_all(yb0.at[pl.ds(0, ny - 1)], sy.at[0], y_peers[0])
            above, below = interface_solve(
                ny, gy, lambda d: yb0[d, 1] + ysig[d] * yb0[d, 0], lambda d: yb0[d, 0] + ysig2[d] * yb0[d, 1],
                top, end, ytau, ytau2, ykk,
            )
            return above * ysc[0], below * ysc[1]
        else:
            for j in range(Y):
                r_s[j] = g_s[j] - q_s[j]
            pbuf[2:CY + 2] = gathered([
                pairs(0, lambda j: xc_s[j] * r_s[j]),
                pairs(1, lambda j: xl_s[j] * r_s[j]),
                pairs(2, lambda j: zl_s[j] * pltpu.roll(r_s[j], 1, 0) + zt_s[j] * pltpu.roll(r_s[j], Z - 1, 0)),
            ], 0).reshape(CY, CZ, X)
            to_rows(pbuf, sw.at[2], True)
            coarse_wait()
            coefs = planes()
            edge_operators()
        await_all(yb1.at[pl.ds(0, ny - 1)], sy.at[1], y_peers[0])
        above, below = interface_solve(ny, gy, lambda d: yb1[d], lambda d: yb1[d], top, end, ytau, ytau2, ykk)
        await_recv(sxt.at[0], xtr.at[1], ssem, sw.at[1, 0], (gx, north), has_s)
        await_recv(sxt.at[1], xtr.at[0], ssem, sw.at[1, 1], (gx, south), has_n)
        alpha, gamma = jnp.zeros((Z, X), f32), jnp.zeros((Z, X), f32)
        for d in range(ny - 2):
            alpha = jnp.where(d < gy - 1, yb1[d] + ytau[d] * alpha, alpha)
        for d in reversed(range(2, ny)):
            gamma = jnp.where(d > gy + 1, yb1[d] + ytau2[d] * gamma, gamma)
        q_top = top + syc[0] * above + syc[1] * below
        q_end = end + syc[1] * above + syc[2] * below
        beta, delta = ybet[north], ydlt[south]
        over = (alpha + beta * (xtr[0] + ycb[north, 1] * q_top)) / (1.0 - beta * ycb[north, 0])
        under = (gamma + delta * (xtr[1] + ycb[south, 1] * q_end)) / (1.0 - delta * ycb[south, 2])
        return above, below, coefs, [(over, q_top), (above, below), (q_end, under)]

    centre = jnp.logical_and(lane3 >= off, lane3 < off + half)
    H = CY + 4
    row = lax.broadcasted_iota(jnp.int32, (H, 1, 1), 0)
    inside = jnp.logical_and(
        jnp.logical_or(row >= 2, has_n), jnp.logical_or(row < 2 + CY, has_s)
    )
    inside = jnp.logical_and(
        inside,
        jnp.logical_and(jnp.logical_or(lane3 >= off, has_w), jnp.logical_or(lane3 < off + half, has_e)),
    )

    def planes():
        out = []
        for m in range(2):
            w, o, e = cbuf[0, m], cbuf[1, m], cbuf[2, m]
            out.append(jnp.where(centre, o, pltpu.roll(jnp.where(lane3 >= half, w, e), half, 2)))
            out.append(jnp.where(centre, pltpu.roll(o, half, 2), jnp.where(lane3 < half, w, e)))
        cx, cy, cz, cd = out
        czl = lax.broadcasted_iota(jnp.int32, (1, CZ, 1), 1)
        cyl, cy = cy[:H], cy[1:]
        cx, cz, cd = cx[1:], cz[1:], cd[1:]
        cd = jnp.where(inside, cd, 1.0)
        ct = jnp.where(czl < CZ - 1, cz, 0.0)
        cl = pltpu.roll(ct, 1, 1)
        cxl = pltpu.roll(cx, 1, 2)
        diag = cxl + cx + cyl + cy + cl + ct + cd
        return cx, cxl, cy, cyl, cl, ct, diag, RELAX / diag

    left, right = x_first()
    above, below = y_half(0, left, right)
    p_s[...] = g_s[...] + ly_s[...] * above[None] + ry_s[...] * below[None]
    for lo in range(0, Y, 4):
        hi = lo + 4
        lower = jnp.concatenate([above[None], p_s[0:hi - 1]], axis=0) if lo == 0 else p_s[lo - 1:hi - 1]
        upper = jnp.concatenate([p_s[lo + 1:Y], below[None]], axis=0) if hi == Y else p_s[lo + 1:hi + 1]
        x_source(lo, hi, lower, upper)
    left, right = x_second()
    above, below, coefs, ghosts = y_half(1, left, right)
    cx, cxl, cy, cyl, cl, ct, diag, scale = coefs
    sides = [[], [], []]
    for at in range(H):
        a, b = ghosts[0 if at < 2 else 1 if at < CY + 2 else 2]
        w = [wbuf[at, n] for n in range(8)]
        sides[0].append(w[0] * a + w[1] * b)
        sides[1].append(w[2] * a + w[3] * b)
        a1, b1, a2, b2 = pltpu.roll(a, 1, 0), pltpu.roll(b, 1, 0), pltpu.roll(a, Z - 1, 0), pltpu.roll(b, Z - 1, 0)
        sides[2].append(w[4] * a1 + w[5] * b1 + w[6] * a2 + w[7] * b2)
    partial = gathered([level_pairs(n, v) for n, v in enumerate(sides)], 0).reshape(H, CZ, X)
    to_rows(pbuf, sw.at[2], False)
    res = jnp.where(inside, partial + pbuf[...], 0.0)
    clane = lax.broadcasted_iota(jnp.int32, (CZ, X), 1)
    inner = clane % half

    def fringe(v):
        edge = jnp.zeros((CZ, X), f32)
        for r in range(CY):
            edge = jnp.where(inner >= SLOTS * r, pltpu.roll(v[r], half - off + 3 + SLOTS * r, 1), edge)
        return edge

    sedge[...] = fringe(res[2:CY + 2])
    comm.send(sedge, ebuf.at[1], sr.at[1], (west, gy), has_w)
    comm.send(sedge, ebuf.at[0], sr.at[0], (east, gy), has_e)
    cor = scale * res
    for repeat in range(COARSE - 1):
        lo, n = 1 + repeat, H - 2 - 2 * repeat
        cut = slice(lo, lo + n)
        mid, over, under = cor[1:-1], cor[:-2], cor[2:]
        applied = (
            diag[cut] * mid
            - cxl[cut] * pltpu.roll(mid, 1, 2)
            - cx[cut] * pltpu.roll(mid, X - 1, 2)
            - cyl[cut] * over
            - cy[cut] * under
            - cl[cut] * pltpu.roll(mid, 1, 1)
            - ct[cut] * pltpu.roll(mid, CZ - 1, 1)
        )
        cor = jnp.where(inside[cut], mid + scale[cut] * (res[cut] - applied), 0.0)
    hj = CY // 2
    fown[0:hj] = jnp.where(lane3 < half, pltpu.roll(cor[:hj], X - off, 2), pltpu.roll(cor[hj:], off, 2))
    fown[hj] = fringe(cor)
    fbuf[gx] = fown[...]
    comm.send_all(lambda dev: fown, fbuf.at[gx], sf.at[0], x_peers, fbuf.at[pl.ds(0, nx - 1)])
    above, below = above * ysc[0], below * ysc[1]
    for j in range(Y):
        op_ref[pl.ds(j, Z, stride=Y), :] = g_s[j] + ly_s[j] * above + ry_s[j] * below
    comm.finish()
    await_recv(sedge, ebuf.at[0], ssem, sr.at[0], (west, gy), has_w)
    await_recv(sedge, ebuf.at[1], ssem, sr.at[1], (east, gy), has_e)
    both = jnp.where(clane < half, ebuf[0], ebuf[1])
    for r in range(CY):
        v = pltpu.roll(both, (off - 3 - SLOTS * r) % X, 1)
        v = res[2 + r] + jnp.where(jnp.logical_or(clane == off, clane == off + half - 1), v, 0.0)
        flip[pl.ds(r, CZ, stride=CY), :] = pltpu.roll(v, X - off, 1)
    or_ref[...] = flip[0:CZ * CY, :half]
    await_all(fbuf.at[pl.ds(0, nx - 1)], sf.at[0], x_peers[0])
    nothing = jnp.zeros((CZ, X), f32)
    edges = [nothing] + [fbuf[d, hj] for d in range(nx)] + [nothing]
    spill = jnp.logical_or(clane >= X - 3, jnp.logical_and(clane >= half, clane < half + 3))
    spill2 = jnp.logical_or(clane < 3, jnp.logical_and(clane >= half - 3, clane < half))
    for t in range(nx // 2):
        u, v = fbuf[2 * t, 0:hj], fbuf[2 * t + 1, 0:hj]
        top = jnp.where(lane3 < half, u, pltpu.roll(v, half, 2))
        low = jnp.where(lane3 < half, pltpu.roll(u, half, 2), v)
        one = jnp.where(clane < half, edges[2 * t + 1], edges[2 * t + 3])
        two = jnp.where(clane < half, edges[2 * t], edges[2 * t + 2])
        base = (t + 1) * CZ * CY
        for j in range(CY):
            turn = (half - 3 - SLOTS * j) % X
            v = top[j] if j < hj else low[j - hj]
            v = v + jnp.where(spill, pltpu.roll(one, turn, 1), 0.0)
            v = v + jnp.where(spill2, pltpu.roll(two, (turn + half) % X, 1), 0.0)
            flip[pl.ds(base + j, CZ, stride=CY), :] = v
        oc_ref[:, t * X:(t + 1) * X] = flip[base:base + CZ * CY, :]
    comm.finish()


def put(*refs):
    sems = refs[6]
    give = [pltpu.make_async_copy(refs[m], refs[3 + m], sems.at[m]) for m in range(3)]
    for copy in give:
        copy.start()
    for copy in give:
        copy.wait()


def body(nx, ny, *args):
    Z, Y, X = args[0].shape
    CZ, CY = Z // 2, Y // 2
    flat = [v.reshape(Z * Y, X) for v in args]
    f32 = jnp.float32

    def vm(*shape):
        return pltpu.VMEM(shape, f32)

    block, square, groups = (Y, Z, X), (Y * Z // X, X, X), Y * Z // X
    assert Y * SLOTS <= X and CY * SLOTS <= X // 2 and X % Z == 0 and Y * Z % X == 0 and X % 8 == 0
    nsx, nsy = len(strides_of(X)), len(strides_of(Y))
    assert nx > 1 and ny > 1
    dma = pltpu.SemaphoreType.DMA
    scratch = (
        [vm(*block) for _ in range(12)]
        + [vm(*square) for _ in range(6)] + [vm(nsx, 2, *square), vm(*block), vm(*block), vm(*block), vm(nsy, 2, *block)]
        + [vm(Z, X), vm(3, Z, X), vm(Z, X), vm(2, Z, X), vm(1, Z, X)]
        + [vm(nx, XC + 1, groups, X), vm(XC + 1, groups, X), vm(nx, groups, X), vm(2, groups, X)]
        + [vm(ny, 3, Z, X), vm(3, Z, X), vm(ny, 2, Z, X), vm(ny, Z, X), vm(2, 2, Z, X)]
        + [vm(1, groups, X)] + [vm(nx, groups, X) for _ in range(8)] + [vm(4, groups, X)]
        + [vm(ny, Z, X) for _ in range(6)] + [vm(6, Z, X), vm(2, Z, X)]
        + [vm(3, (CY + 4) * Z, X), pltpu.VMEM((4 * X, X), jnp.bfloat16), vm(2, CY, CZ, X), vm(3, 2, CY + 5, CZ, X),
           vm(CY + 4, 8, Z, X), vm(2, 2 * EDGE + 1, Z, X), vm(2, 4 * EDGE + 1, Z, X), vm(CY + 4, CZ, X), vm(2, Z, X), vm(2, Z, X),
           vm(2, CZ, X), vm(CZ, X), vm(CY // 2 + 1, CZ, X), vm(nx, CY // 2 + 1, CZ, X), vm((nx // 2 + 1) * CZ * CY, X)]
        + [dma((18,)), dma((3,)), dma((2,)), dma((3,)), dma((3,)), dma((2,)), dma((3, 2)), dma((1,))]
        + [vm(6, Z * Y, X), dma((3,))]
    )
    p, r, c = pl.pallas_call(
        functools.partial(kernel, nx, ny),
        out_shape=(
            vm(Z * Y, X),
            vm(CZ * CY, X // 2),
            vm(CZ * CY, nx * X // 2),
        ),
        in_specs=[pl.BlockSpec(memory_space=pltpu.HBM)] * 6,
        out_specs=[pl.BlockSpec(memory_space=pltpu.VMEM)] * 3,
        scratch_shapes=scratch,
        compiler_params=pltpu.CompilerParams(
            collective_id=0, has_side_effects=True, vmem_limit_bytes=60000000
        ),
    )(*flat)
    p, r, c = pl.pallas_call(
        put,
        out_shape=tuple(jax.ShapeDtypeStruct(v.shape, f32) for v in (p, r, c)),
        in_specs=[pl.BlockSpec(memory_space=pltpu.VMEM)] * 3,
        out_specs=[pl.BlockSpec(memory_space=pltpu.HBM)] * 3,
        scratch_shapes=[dma((3,))],
    )(*[pltpu.with_memory_space_constraint(v, pltpu.VMEM) for v in (p, r, c)])
    return p.reshape(Z, Y, X), r.reshape(CZ, CY, X // 2), c.reshape(CZ, CY, nx * X // 2)


def solution(mesh):
    nx, ny = mesh.shape["gx"], mesh.shape["gy"]
    split = P(None, "gy", "gx")
    return jax.shard_map(
        functools.partial(body, nx, ny),
        mesh=mesh,
        in_specs=(split,) * 6,
        out_specs=(split, split, P(None, "gy", None)),
        check_vma=False,
    )
```

```python
import functools

import jax
import jax.numpy as jnp
from jax import lax
from jax.experimental import pallas as pl
from jax.experimental.pallas import tpu as pltpu
from jax.sharding import PartitionSpec as P

COARSE = 3
RELAX = 0.8
LE, LS, RE, RS, GS, GE, XC = range(7)
SLOTS = 8
EDGE = 4
MESH = pl.DeviceIdType.MESH


def strides_of(length):
    out, s = [], 1
    while s < length:
        out.append(s)
        s *= 2
    return out


class Comm:
    def __init__(self, send_sems):
        self.sems, self.used, self.pending = send_sems, 0, []

    def copy(self, src, dst, sem, recv, dev):
        return pltpu.make_async_remote_copy(
            src_ref=src, dst_ref=dst, send_sem=sem, recv_sem=recv, device_id=dev, device_id_type=MESH
        )

    def send(self, src, dst, recv, dev, cond=None):
        copy = self.copy(src, dst, self.sems.at[self.used], recv, dev)
        self.used += 1
        self.pending.append((copy, cond))
        if cond is None:
            copy.start()
        else:
            pl.when(cond)(copy.start)

    def send_all(self, src, dst, recv, devs, received):
        sem = self.sems.at[self.used]
        self.used += 1
        for dev in devs:
            self.copy(src(dev), dst, sem, recv, dev).start()
        self.pending.append((self.copy(received, received, sem, recv, devs[0]), None))

    def finish(self):
        for copy, cond in self.pending:
            if cond is None:
                copy.wait_send()
            else:
                pl.when(cond)(copy.wait_send)
        self.used, self.pending = 0, []


def await_recv(src, dst, sems, recv, dev, cond=None):
    copy = pltpu.make_async_remote_copy(
        src_ref=src, dst_ref=dst, send_sem=sems.at[0], recv_sem=recv, device_id=dev, device_id_type=MESH
    )
    if cond is None:
        copy.wait_recv()
    else:
        pl.when(cond)(copy.wait_recv)


def await_sides(buf, recv, dev, one, two):
    both = jnp.logical_and(one, two)
    pl.when(both)(lambda: await_all(buf, recv, dev))
    pl.when(jnp.logical_and(jnp.logical_or(one, two), jnp.logical_not(both)))(lambda: await_all(buf.at[0], recv, dev))


def await_all(part, recv, dev):
    pltpu.make_async_remote_copy(
        src_ref=part, dst_ref=part, send_sem=recv, recv_sem=recv, device_id=dev, device_id_type=MESH
    ).wait_recv()


def farthest_first(me, n):
    out = []
    for k in range(n - 1):
        down = jnp.where(n - 1 - k > me, n - 1 - k, n - 2 - k)
        up = jnp.where(k < me, k, k + 1)
        out.append(jnp.where(2 * me < n, down, up))
    return out


def flipped(me, n):
    if n & (n - 1):
        return [lax.rem(me + o, n) for o in range(1, n)]
    def peer_of(mask):
        peer, bit = 0, 1
        while bit < n:
            value = lax.rem(me // bit, 2)
            peer = peer + bit * (1 - value if mask & bit else value)
            bit *= 2
        return peer

    masks = list(range(n - 1, 0, -1))
    even, odd = [m for m in masks if m % 2 == 0], [m for m in masks if m % 2]
    first = lax.rem(me, 2) == 0
    return [jnp.where(first, peer_of(a), peer_of(b)) for a, b in zip(even + odd, odd + even)]


def interface_factor(n, me, ls, le, rs, re, own, tau, sig, bet, tau2, sig2, dlt, kk):
    beta = jnp.zeros_like(ls[0])
    for d in range(n):
        bet[d] = beta
        w = 1.0 / (1.0 - ls[d] * beta)
        t = le[d] * w
        tau[d] = t
        s = t * beta
        sig[d] = s
        beta = re[d] + s * rs[d]
    delta = jnp.zeros_like(ls[0])
    for d in reversed(range(n)):
        dlt[d] = delta
        w = 1.0 / (1.0 - re[d] * delta)
        t = rs[d] * w
        tau2[d] = t
        s = t * delta
        sig2[d] = s
        delta = ls[d] + s * le[d]
    ls_m, le_m, rs_m, re_m = own
    beta, delta = bet[me], dlt[me]
    a, b = 1.0 - beta * ls_m, 1.0 - delta * re_m
    o1, o2 = beta * rs_m, delta * le_m
    inv = 1.0 / (a * b - o1 * o2)
    kk[0], kk[1], kk[2], kk[3] = b * inv, o1 * inv, a * inv, o2 * inv
    kk[4], kk[5] = beta, delta


def interface_solve(n, me, h_left, h_right, gs, ge, tau, tau2, kk):
    alpha = jnp.zeros_like(gs)
    for d in range(n - 1):
        alpha = jnp.where(d < me, h_left(d) + tau[d] * alpha, alpha)
    gamma = jnp.zeros_like(gs)
    for d in reversed(range(1, n)):
        gamma = jnp.where(d > me, h_right(d) + tau2[d] * gamma, gamma)
    p = alpha + kk[4] * gs
    q = gamma + kk[5] * ge
    return kk[0] * p + kk[1] * q, kk[2] * q + kk[3] * p


def chain_factor(n, me, ls, le, rs, re, xc, own, rho, tau, sig, bet, tau2, sig2, scl, dlt, kk):
    one, zero = jnp.ones_like(ls[0]), jnp.zeros_like(ls[0])
    beta = zero
    for d in range(n):
        r = zero if d == 0 else xc[d - 1]
        b = one if d == 0 else 1.0 - r * (1.0 - beta)
        rho[d], bet[d] = r, b
        w = 1.0 / (1.0 - ls[d] * b)
        t = le[d] * w
        tau[d] = t * r
        s = t * b
        sig[d] = s
        beta = re[d] + s * rs[d]
    delta = zero
    for d in reversed(range(n)):
        dlt[d] = delta
        t = rs[d] / (1.0 - re[d] * delta)
        s = t * delta
        q = ls[d] + s * le[d]
        if d > 0:
            v = 1.0 / (1.0 - q + q * xc[d - 1])
            scl[d], tau2[d], sig2[d] = v, v * t, v * s
            delta = v * q * xc[d - 1]
        else:
            scl[d], tau2[d], sig2[d] = zero, zero, zero
    ls_m, le_m, rs_m, re_m = own
    beta, delta = bet[me], dlt[me]
    a, b = 1.0 - beta * ls_m, 1.0 - delta * re_m
    o1, o2 = beta * rs_m, delta * le_m
    inv = 1.0 / (a * b - o1 * o2)
    kk[0], kk[1], kk[2], kk[3] = b * inv, o1 * inv, a * inv, o2 * inv


def kernel(nx, ny, f_hbm, p_hbm, x_hbm, y_hbm, z_hbm, d_hbm, op_ref, or_ref, oc_ref,
           xl_s, xc_s, yl_s, yc_s, zl_s, zt_s, zd_s, fo_s, p_s, r_s, g_s, q_s,
           ct_s, rt_s, gt_s, lx_s, rx_s, ix_s, wx_s, ly_s, ry_s, iy_s, wy_s,
           sx0, sy0, hx, hy, xb, sxb, xb1, sx1, ycb, syc, yb0, yb1, shy,
           xown, xrho, xtau, xsig, xbet, xtau2, xsig2, xscl, xdlt, xkk,
           ytau, ysig, ybet, ytau2, ysig2, ydlt, ykk, ysc,
           pair_s, sel_s, cown, cbuf, wbuf, elr, nbr, pbuf, sxt, xtr, ebuf, sedge, fown, fbuf, flip,
           ssem, s0, sx, sy, sc, sr, sw, ins):
    Y, Z, X = xc_s.shape
    CY, CZ = Y // 2, Z // 2
    f32 = jnp.float32
    gx, gy = lax.axis_index("gx"), lax.axis_index("gy")
    has_w, has_e = gx > 0, gx < nx - 1
    has_n, has_s = gy > 0, gy < ny - 1
    west, east = jnp.maximum(gx - 1, 0), jnp.minimum(gx + 1, nx - 1)
    north, south = jnp.maximum(gy - 1, 0), jnp.minimum(gy + 1, ny - 1)
    x_peers = [(i, gy) for i in farthest_first(gx, nx)]
    y_peers = [(gx, j) for j in flipped(gy, ny)]

    half = X // 2
    off = half // 2
    hj = CY // 2
    clane = lax.broadcasted_iota(jnp.int32, (CZ, X), 1)
    lane3 = lax.broadcasted_iota(jnp.int32, (1, 1, X), 2)
    inner = clane % half

    def fringe(v):
        edge = jnp.zeros((CZ, X), f32)
        for r in range(CY):
            edge = jnp.where(inner >= SLOTS * r, pltpu.roll(v[r], half - off + 3 + SLOTS * r, 1), edge)
        return edge

    def sweeps(ssem, sin):
        stages = ((0, 2), (2, 3), (3, 6))
        sources = (y_hbm, p_hbm, x_hbm, z_hbm, d_hbm, f_hbm)
        for n, (lo, hi) in enumerate(stages):
            for m in range(lo, hi):
                pltpu.make_async_copy(sources[m], ins.at[m], sin.at[n]).start()

        def loaded(n):
            part = ins.at[pl.ds(stages[n][0], stages[n][1] - stages[n][0])]
            pltpu.make_async_copy(part, part, sin.at[n]).wait()

        y_ref, p_ref, x_ref, z_ref, d_ref, f_ref = [ins.at[m] for m in range(6)]

        barrier = pltpu.get_barrier_semaphore()

        def greet(dev):
            pl.semaphore_signal(barrier, inc=1, device_id=dev, device_id_type=MESH)

        for dev in x_peers + y_peers:
            greet(dev)

        lane = lax.broadcasted_iota(jnp.int32, (Z, X), 1)
        level = lax.broadcasted_iota(jnp.int32, (Z, X), 0)

        def rows(ref, j):
            return ref[pl.ds(j, Z, stride=Y), :]

        loaded(0)
        sy0[0] = rows(y_ref, Y - 1)
        sy0[1] = rows(p_ref, Y - 1)
        sy0[2] = rows(p_ref, 0)

        pl.semaphore_wait(barrier, (nx - 1) + (ny - 1))

        comm = Comm(ssem)
        comm.send(sy0.at[0:2], hy.at[0:2], s0.at[1], (gx, south), has_s)
        comm.send(sy0.at[2:3], hy.at[2:3], s0.at[1], (gx, north), has_n)

        loaded(1)
        packed = jnp.zeros((Z, X), f32)
        for j in range(Y):
            v = rows(x_ref, j)
            xc_s[j] = v
            packed = jnp.where(lane == SLOTS * j + XC, v[:, X - 1:], packed)
        sx0[...] = packed
        comm.send(sx0, hx, s0.at[0], (east, gy), has_e)

        for j in range(Y):
            yc_s[j] = rows(y_ref, j)
            p_s[j] = rows(p_ref, j)
        loaded(2)
        for j in range(Y):
            zv = jnp.where(level < Z - 1, rows(z_ref, j), 0.0)
            zt_s[j] = zv
            zl = pltpu.roll(zv, 1, 0)
            zl_s[j] = zl
            zd_s[j] = zv + zl + rows(d_ref, j)
            fo_s[j] = rows(f_ref, j)

        to_sides = (((gx, south), has_s, has_n), ((gx, north), has_n, has_s))
        per, groups, blocks = X // Z, Y * Z // X, X // 8
        sub = lax.broadcasted_iota(jnp.int32, (8, X), 0)

        def turned(ref, g):
            return ref[g * per:(g + 1) * per].reshape(X, X).T

        def split(v):
            return [v[8 * k:8 * k + 8] for k in range(blocks)]

        def shift(v, s, fill):
            if s % 8 == 0:
                m = s // 8
                return [v[k - m] if 0 <= k - m < blocks else fill for k in range(blocks)]
            turn = [pltpu.roll(u, s % 8, 0) for u in v]
            if s > 0:
                return [jnp.where(sub < s, fill if k == 0 else turn[k - 1], turn[k]) for k in range(blocks)]
            return [jnp.where(sub >= 8 + s, fill if k == blocks - 1 else turn[k + 1], turn[k]) for k in range(blocks)]

        def scaled(u, v):
            return [a if b is None else b if a is None else a * b for a, b in zip(u, v)]

        def added(u, v):
            return [a if b is None else a + b for a, b in zip(u, v)]

        def fill_of(s, value):
            return None if s % 8 == 0 else value

        def store(ref, at, v):
            for k in range(blocks):
                ref[at + (slice(8 * k, 8 * k + 8),)] = v[k]

        def load(ref, at):
            return [ref[at + (slice(8 * k, 8 * k + 8),)] for k in range(blocks)]

        xsteps = strides_of(X)

        def x_factor(g):
            c = load(ct_s, (g,))
            a = shift(c, 1, 1.0)
            for j in range(g * per, (g + 1) * per):
                g_s[j] = yl_s[j] + yc_s[j] + zd_s[j]
            e = split(turned(g_s, g))
            for n, s in enumerate(xsteps):
                inv = [1.0 / (u + v + w) for u, v, w in zip(a, c, e)]
                ai, ci = scaled(a, inv), scaled(c, inv)
                store(wx_s, (n, 0, g), ci)
                store(wx_s, (n, 1, g), ai)
                ae, ce = scaled(ai, e), scaled(ci, e)
                a = scaled(a, shift(ai, s, fill_of(s, 1.0)))
                c = scaled(c, shift(ci, -s, fill_of(s, 1.0)))
                e = added(added(e, shift(ce, s, fill_of(s, 0.0))), shift(ae, -s, fill_of(s, 0.0)))
            inv = [1.0 / (u + v + w) for u, v, w in zip(a, c, e)]
            a, c = scaled(a, inv), scaled(c, inv)
            store(ix_s, (g,), inv)
            store(lx_s, (g,), a)
            store(rx_s, (g,), c)
            one = slice(g, g + 1)
            sxb[LE, one], sxb[LS, one] = a[-1][7:8], a[0][0:1]
            sxb[RE, one], sxb[RS, one] = c[-1][7:8], c[0][0:1]
            sxb[XC, one] = ct_s[g, X - 1:X]

        def edge_sums(g):
            r = split(turned(r_s, g))
            store(rt_s, (g,), r)
            out = []
            for ref in (lx_s, rx_s):
                v = scaled(load(ref, (g,)), r)
                while len(v) > 1:
                    v = [a + b for a, b in zip(v[0::2], v[1::2])]
                out.append(jnp.sum(v[0], axis=0, keepdims=True))
            return out

        def z_terms(v, part):
            return zl_s[part] * pltpu.roll(v, 1, 1) + zt_s[part] * pltpu.roll(v, Z - 1, 1)

        def x_source(lo, hi, lower, upper):
            part = slice(lo, hi)
            r_s[part] = fo_s[part] + yl_s[part] * lower + yc_s[part] * upper + z_terms(p_s[part], part)

        for g in range(groups):
            store(ct_s, (g,), split(turned(xc_s, g)))
        yl_s[1:Y] = yc_s[0:Y - 1]
        for g in range(1, groups):
            x_factor(g)
        x_source(1, Y - 1, p_s[0:Y - 2], p_s[2:Y])

        @pl.when(jnp.logical_not(has_w))
        def _():
            hx[...] = jnp.zeros_like(hx)
            cbuf[0] = jnp.zeros_like(cbuf[0])
            ebuf[0] = jnp.zeros_like(ebuf[0])

        @pl.when(jnp.logical_not(has_e))
        def _():
            cbuf[2] = jnp.zeros_like(cbuf[2])
            ebuf[1] = jnp.zeros_like(ebuf[1])

        @pl.when(jnp.logical_not(has_n))
        def _():
            hy[0:2] = jnp.zeros_like(hy[0:2])
            nbr[0] = jnp.zeros_like(nbr[0])
            pbuf[0:2] = jnp.zeros_like(pbuf[0:2])
            xtr[0] = jnp.zeros_like(xtr[0])
            for d in range(3):
                cbuf[d, :, 0:3] = jnp.zeros_like(cbuf[d, :, 0:3])

        @pl.when(jnp.logical_not(has_s))
        def _():
            hy[2] = jnp.zeros_like(hy[2])
            nbr[1] = jnp.zeros_like(nbr[1])
            pbuf[CY + 2:] = jnp.zeros_like(pbuf[CY + 2:])
            xtr[1] = jnp.zeros_like(xtr[1])
            for d in range(3):
                cbuf[d, :, 3 + CY:] = jnp.zeros_like(cbuf[d, :, 3 + CY:])

        for n, u in ((True, True), (True, False), (False, True)):
            cond = jnp.logical_and(has_n if n else jnp.logical_not(has_n), has_s if u else jnp.logical_not(has_s))
            part = hy.at[pl.ds(0, (2 if n else 0) + (1 if u else 0))]
            await_recv(part, part, ssem, s0.at[1], (gx, north), cond)

        yl_s[0] = hy[0]
        x_factor(0)
        x_source(0, 1, hy[1:2], p_s[1:2])
        x_source(Y - 1, Y, p_s[Y - 2:Y - 1], hy[2:3])
        for g in range(groups):
            one = slice(g, g + 1)
            sxb[GS, one], sxb[GE, one] = edge_sums(g)
        xb[gx] = sxb[...]
        comm.send_all(lambda dev: sxb, xb.at[gx], sx.at[0], x_peers, xb.at[pl.ds(0, nx - 1)])

        for n, (dev, there, _) in enumerate(to_sides):
            for k, ref in enumerate((xc_s, zt_s)):
                src = ref.at[pl.ds(0 if n else Y - EDGE, EDGE)]
                comm.send(src, nbr.at[n, pl.ds(k * EDGE, EDGE)], sw.at[0], dev, there)

        await_recv(sx0, hx, ssem, s0.at[0], (east, gy), has_w)
        for j in range(Y):
            xl_s[j] = jnp.where(lane == 0, hx[:, SLOTS * j + XC:SLOTS * j + XC + 1], pltpu.roll(xc_s[j], 1, 1))

        ysteps = strides_of(Y)
        for lo in range(0, Z, 8):
            zs = slice(lo, lo + 8)
            a = [yl_s[j, zs] for j in range(Y)]
            c = [yc_s[j, zs] for j in range(Y)]
            e = [xl_s[j, zs] + xc_s[j, zs] + zd_s[j, zs] for j in range(Y)]
            for n, s in enumerate(ysteps):
                inv = [1.0 / (a[j] + c[j] + e[j]) for j in range(Y)]
                ai, ci = [a[j] * inv[j] for j in range(Y)], [c[j] * inv[j] for j in range(Y)]
                for j in range(Y):
                    if j + s < Y:
                        wy_s[n, 0, j, zs] = ci[j]
                    if j >= s:
                        wy_s[n, 1, j, zs] = ai[j]
                e2 = []
                for j in range(Y):
                    v = e[j]
                    if j >= s:
                        v = v + ci[j - s] * e[j - s]
                    if j + s < Y:
                        v = v + ai[j + s] * e[j + s]
                    e2.append(v)
                a = [a[j] * ai[j - s] if j >= s else a[j] for j in range(Y)]
                c = [c[j] * ci[j + s] if j + s < Y else c[j] for j in range(Y)]
                e = e2
            for j in range(Y):
                inv = 1.0 / (a[j] + c[j] + e[j])
                iy_s[j, zs], ly_s[j, zs], ry_s[j, zs] = inv, a[j] * inv, c[j] * inv

        k_top, k_end = jnp.sqrt(yl_s[0]), jnp.sqrt(yc_s[Y - 1])
        i_top = jnp.where(has_n, 1.0 / jnp.where(has_n, k_top, 1.0), 0.0)
        ysc[0], ysc[1] = i_top, 1.0 / k_end
        syc[0], syc[1], syc[2] = ly_s[0], ly_s[Y - 1] * k_end * i_top, ry_s[Y - 1]
        ycb[gy] = syc[...]
        comm.send_all(lambda dev: syc, ycb.at[gy], sy.at[2], y_peers, ycb.at[pl.ds(0, ny - 1)])

        def x_local():
            for g in range(groups):
                r = load(rt_s, (g,))
                for n, s in enumerate(xsteps):
                    low = shift(scaled(load(wx_s, (n, 0, g)), r), s, fill_of(s, 0.0))
                    high = shift(scaled(load(wx_s, (n, 1, g)), r), -s, fill_of(s, 0.0))
                    r = added(added(r, low), high)
                store(gt_s, (g,), scaled(r, load(ix_s, (g,))))

        def y_local():
            for lo in range(0, Z, 8):
                zs = slice(lo, lo + 8)
                r = [r_s[j, zs] for j in range(Y)]
                for n, s in enumerate(ysteps):
                    low = [wy_s[n, 0, j, zs] * r[j] if j + s < Y else None for j in range(Y)]
                    high = [wy_s[n, 1, j, zs] * r[j] if j >= s else None for j in range(Y)]
                    r2 = []
                    for j in range(Y):
                        v = r[j]
                        if j >= s:
                            v = v + low[j - s]
                        if j + s < Y:
                            v = v + high[j + s]
                        r2.append(v)
                    r = r2
                for j in range(Y):
                    g_s[j, zs] = r[j] * iy_s[j, zs]

        x_local()

        ii = lax.broadcasted_iota(jnp.int32, (X, X), 0)
        mm = lax.broadcasted_iota(jnp.int32, (X, X), 1)

        def selection(step, start):
            target = lax.rem((ii + (step + 2)) // 2 - 1 + start + X, X)
            return jnp.where(mm == target, 0.125, 0.0)

        def level_pairs(n, levels):
            for k, v in enumerate(levels):
                pair_s[n, k * Z:(k + 1) * Z] = v
            count = len(levels) * CZ
            return pair_s[n, pl.ds(0, count, stride=2), :] + pair_s[n, pl.ds(1, count, stride=2), :]

        def pairs(n, field):
            return level_pairs(n, [field(2 * k) + field(2 * k + 1) for k in range(CY)])

        def gathered(parts, first):
            v = jnp.concatenate(parts, axis=1)
            high = v.astype(jnp.bfloat16)
            v = v - high.astype(f32)
            mid = v.astype(jnp.bfloat16)
            low = (v - mid.astype(f32)).astype(jnp.bfloat16)
            sel = sel_s[first * X:(first + len(parts)) * X]
            return sum(jnp.dot(u, sel, preferred_element_type=f32) for u in (low, mid, high))

        for n, sel in enumerate((selection(1, off), selection(-1, off), selection(0, off), selection(0, half + off))):
            sel_s[n * X:(n + 1) * X] = sel.astype(jnp.bfloat16)
        for m, (u, v) in enumerate(((lambda j: xc_s[j], lambda j: yc_s[j]), (lambda j: rows(z_ref, j), lambda j: rows(d_ref, j)))):
            part = gathered([pairs(0, u), pairs(1, v)], 2).reshape(CY, CZ, X)
            cown[m] = part
            cbuf[1, m, 3:3 + CY] = part

        def operator(at, xc, xl, zl, zt, sides):
            for n, (u, v) in enumerate(sides):
                wbuf[at, n] = xc[0] * u + xc[1] * v
                wbuf[at, 2 + n] = xl[0] * u + xl[1] * v
                wbuf[at, 4 + n] = zl[0] * pltpu.roll(u, 1, 0) + zl[1] * pltpu.roll(v, 1, 0)
                wbuf[at, 6 + n] = zt[0] * pltpu.roll(u, Z - 1, 0) + zt[1] * pltpu.roll(v, Z - 1, 0)

        for k in range(EDGE):
            for n, j in enumerate((Y - EDGE + k, k)):
                elr[n, k], elr[n, EDGE + k] = ly_s[j] * ysc[0], ry_s[j] * ysc[1]
        for n in range(2):
            elr[n, 2 * EDGE] = hx[...]
        for k in range(CY):
            two = (2 * k, 2 * k + 1)
            operator(2 + k, *[[ref[j] for j in two] for ref in (xc_s, xl_s, zl_s, zt_s)],
                     [[ref[j] * ysc[n] for j in two] for n, ref in enumerate((ly_s, ry_s))])

        def edge_columns():
            for n, (dev, there, _) in enumerate(to_sides):
                comm.send(elr.at[n], nbr.at[n, pl.ds(2 * EDGE, 2 * EDGE + 1)], sw.at[0], dev, there)

        def edge_operators():
            await_sides(nbr, sw.at[0], (gx, north), has_n, has_s)
            for n, first in enumerate((Y - EDGE, 0)):
                for k in range(0, EDGE, 2):
                    xc = [nbr[n, k + i] for i in range(2)]
                    zt = [nbr[n, EDGE + k + i] for i in range(2)]
                    cols = [SLOTS * (first + k + i) + XC for i in range(2)]
                    xl = [jnp.where(lane == 0, nbr[n, 4 * EDGE, :, c:c + 1], pltpu.roll(v, 1, 1)) for c, v in zip(cols, xc)]
                    operator(n * (CY + 2) + k // 2, xc, xl, [pltpu.roll(v, 1, 0) for v in zt], zt,
                             [[nbr[n, (2 + m) * EDGE + k + i] for i in range(2)] for m in range(2)])

        def edge_rows():
            for dev, there, src, dst in (((gx, north), has_n, 2, CY + 2), ((gx, south), has_s, CY, 0)):
                comm.send(pbuf.at[pl.ds(src, 2)], pbuf.at[pl.ds(dst, 2)], sw.at[2], dev, there)

        def coarse_send(straight):
            for i, ok, back in ((west, has_w, 2), (gx, None, 1), (east, has_e, 0)):
                both = (lambda c: c) if ok is None else (lambda c, ok=ok: jnp.logical_and(c, ok))
                if straight:
                    if ok is not None:
                        comm.send(cown, cbuf.at[back, :, pl.ds(3, CY)], sc.at[back], (i, gy), ok)
                else:
                    comm.send(cown.at[:, pl.ds(CY - 3, 3)], cbuf.at[back, :, pl.ds(0, 3)], sc.at[back], (i, south), both(has_s))
                    comm.send(cown.at[:, pl.ds(0, 2)], cbuf.at[back, :, pl.ds(3 + CY, 2)], sc.at[back], (i, north), both(has_n))

        def coarse_wait():
            for slot, i, ok in ((0, west, has_w), (1, gx, None), (2, east, has_e)):
                kept = 0 if ok is None else CY
                for n, s in ((True, True), (True, False), (False, True)):
                    cond = jnp.logical_and(has_n if n else jnp.logical_not(has_n), has_s if s else jnp.logical_not(has_s))
                    cond = cond if ok is None else jnp.logical_and(cond, ok)
                    part = cbuf.at[slot, :, pl.ds(0, kept + (3 if n else 0) + (2 if s else 0))]
                    await_recv(part, part, ssem, sc.at[slot], (i, gy), cond)

        def x_solve(hl, hr, gs, ge):
            alpha = jnp.zeros((groups, X), f32)
            for d in range(nx - 1):
                alpha = jnp.where(d < gx, hl(d) + xtau[d] * alpha, alpha)
            gamma = jnp.zeros((groups, X), f32)
            for d in reversed(range(1, nx)):
                gamma = jnp.where(d > gx, hr(d) + xtau2[d] * gamma, gamma)
            p = xrho[gx] * alpha + xbet[gx] * gs
            q = gamma + xdlt[gx] * ge
            return xkk[0] * p + xkk[1] * q, xkk[2] * q + xkk[3] * p

        def x_first():
            await_all(xb.at[pl.ds(0, nx - 1)], sx.at[0], x_peers[0])
            cut = [[xb[d, k] for d in range(nx)] for k in range(XC + 1)]
            own = [sxb[k] for k in range(XC + 1)]
            inv = [1.0 / v for v in cut[XC]]
            ge = [cut[GE][d] * inv[d] for d in range(nx)]
            gs = cut[GS]
            xown[0] = 1.0 / own[XC]
            chain_factor(nx, gx, cut[LS], cut[LE], cut[RS], cut[RE], cut[XC], [own[LS], own[LE], own[RS], own[RE]],
                         xrho, xtau, xsig, xbet, xtau2, xsig2, xscl, xdlt, xkk)
            return x_solve(
                lambda d: ge[d] + xsig[d] * gs[d], lambda d: xscl[d] * gs[d] + xsig2[d] * ge[d], own[GS], own[GE] * xown[0]
            )

        def x_second():
            sums = [edge_sums(g) for g in range(groups)]
            gs, ge = [jnp.concatenate([v[n] for v in sums], axis=0) for n in range(2)]
            ge = ge * xown[0]
            sx1[0], sx1[1] = ge + xsig[gx] * gs, xscl[gx] * gs + xsig2[gx] * ge
            comm.send_all(
                lambda dev: sx1.at[jnp.where(dev[0] > gx, 0, 1)], xb1.at[gx], sx.at[1], x_peers, xb1.at[pl.ds(0, nx - 1)]
            )
            coarse_send(False)
            edge_columns()
            x_local()
            await_all(xb1.at[pl.ds(0, nx - 1)], sx.at[1], x_peers[0])
            return x_solve(lambda d: xb1[d], lambda d: xb1[d], gs, ge)

        def y_half(m, left, right):
            top, end = jnp.zeros((Z, X), f32), jnp.zeros((Z, X), f32)
            for g in range(groups):
                u, w = left[g:g + 1], right[g:g + 1]
                c, v = load(ct_s, (g,)), []
                for a, b, d in zip(load(gt_s, (g,)), load(lx_s, (g,)), load(rx_s, (g,))):
                    v.append(a + b * u + d * w)
                edge = u + (xrho[gx][g:g + 1] - 1.0) * v[0][0:1]
                t = added(shift(scaled(c, v), 1, edge), scaled(c, shift(v, -1, w)))
                v = jnp.concatenate(v, axis=0).T.reshape(per, Z, X)
                t = jnp.concatenate(t, axis=0).T.reshape(per, Z, X)
                for n in range(per):
                    j = g * per + n
                    q_s[j] = v[n]
                    r = fo_s[j] + t[n] + zl_s[j] * pltpu.roll(v[n], 1, 0) + zt_s[j] * pltpu.roll(v[n], Z - 1, 0)
                    r_s[j] = r
                    top, end = top + ly_s[j] * r, end + ry_s[j] * r
            top, end = top * ysc[0], end * ysc[1]
            if m == 0:
                shy[0, 0], shy[0, 1] = top, end
                yb0[gy] = shy[0]
                comm.send_all(lambda dev: shy.at[0], yb0.at[gy], sy.at[0], y_peers, yb0.at[pl.ds(0, ny - 1)])
            else:
                shy[1, 0] = end + ysig[gy] * top
                shy[1, 1] = top + ysig2[gy] * end
                yb1[gy] = shy[1, 0]
                comm.send_all(
                    lambda dev: shy.at[1, jnp.where(dev[1] > gy, 0, 1)], yb1.at[gy], sy.at[1], y_peers, yb1.at[pl.ds(0, ny - 1)]
                )
            if m:
                sxt[0], sxt[1] = end, top
                comm.send(sxt.at[0], xtr.at[1], sw.at[1], (gx, north), has_n)
                comm.send(sxt.at[1], xtr.at[0], sw.at[1], (gx, south), has_s)
            y_local()
            if m == 0:
                coarse_send(True)
                await_all(ycb.at[pl.ds(0, ny - 1)], sy.at[2], y_peers[0])
                ls, mid, re = [[ycb[d, k] for d in range(ny)] for k in range(3)]
                interface_factor(
                    ny, gy, ls, mid, mid, re, [syc[0], syc[1], syc[1], syc[2]],
                    ytau, ysig, ybet, ytau2, ysig2, ydlt, ykk,
                )
                comm.finish()
                await_all(yb0.at[pl.ds(0, ny - 1)], sy.at[0], y_peers[0])
                above, below = interface_solve(
                    ny, gy, lambda d: yb0[d, 1] + ysig[d] * yb0[d, 0], lambda d: yb0[d, 0] + ysig2[d] * yb0[d, 1],
                    top, end, ytau, ytau2, ykk,
                )
                return above * ysc[0], below * ysc[1]
            else:
                for j in range(Y):
                    r_s[j] = g_s[j] - q_s[j]
                pbuf[2:CY + 2] = gathered([
                    pairs(0, lambda j: xc_s[j] * r_s[j]),
                    pairs(1, lambda j: xl_s[j] * r_s[j]),
                    pairs(2, lambda j: zl_s[j] * pltpu.roll(r_s[j], 1, 0) + zt_s[j] * pltpu.roll(r_s[j], Z - 1, 0)),
                ], 0).reshape(CY, CZ, X)
                edge_rows()
                comm.finish()
                coarse_wait()
                coefs = planes()
                edge_operators()
            await_all(yb1.at[pl.ds(0, ny - 1)], sy.at[1], y_peers[0])
            above, below = interface_solve(ny, gy, lambda d: yb1[d], lambda d: yb1[d], top, end, ytau, ytau2, ykk)
            await_sides(xtr, sw.at[1], (gx, north), has_n, has_s)
            alpha, gamma = jnp.zeros((Z, X), f32), jnp.zeros((Z, X), f32)
            for d in range(ny - 2):
                alpha = jnp.where(d < gy - 1, yb1[d] + ytau[d] * alpha, alpha)
            for d in reversed(range(2, ny)):
                gamma = jnp.where(d > gy + 1, yb1[d] + ytau2[d] * gamma, gamma)
            q_top = top + syc[0] * above + syc[1] * below
            q_end = end + syc[1] * above + syc[2] * below
            beta, delta = ybet[north], ydlt[south]
            over = (alpha + beta * (xtr[0] + ycb[north, 1] * q_top)) / (1.0 - beta * ycb[north, 0])
            under = (gamma + delta * (xtr[1] + ycb[south, 1] * q_end)) / (1.0 - delta * ycb[south, 2])
            return above, below, coefs, [(over, q_top), (above, below), (q_end, under)]

        centre = jnp.logical_and(lane3 >= off, lane3 < off + half)
        H = CY + 4
        row = lax.broadcasted_iota(jnp.int32, (H, 1, 1), 0)
        inside = jnp.logical_and(
            jnp.logical_or(row >= 2, has_n), jnp.logical_or(row < 2 + CY, has_s)
        )
        inside = jnp.logical_and(
            inside,
            jnp.logical_and(jnp.logical_or(lane3 >= off, has_w), jnp.logical_or(lane3 < off + half, has_e)),
        )

        def planes():
            out = []
            for m in range(2):
                w, o, e = cbuf[0, m], cbuf[1, m], cbuf[2, m]
                out.append(jnp.where(centre, o, pltpu.roll(jnp.where(lane3 >= half, w, e), half, 2)))
                out.append(jnp.where(centre, pltpu.roll(o, half, 2), jnp.where(lane3 < half, w, e)))
            cx, cy, cz, cd = out
            czl = lax.broadcasted_iota(jnp.int32, (1, CZ, 1), 1)
            cyl, cy = cy[:H], cy[1:]
            cx, cz, cd = cx[1:], cz[1:], cd[1:]
            cd = jnp.where(inside, cd, 1.0)
            ct = jnp.where(czl < CZ - 1, cz, 0.0)
            cl = pltpu.roll(ct, 1, 1)
            cxl = pltpu.roll(cx, 1, 2)
            diag = cxl + cx + cyl + cy + cl + ct + cd
            return cx, cxl, cy, cyl, cl, ct, diag, RELAX / diag

        left, right = x_first()
        above, below = y_half(0, left, right)
        p_s[...] = g_s[...] + ly_s[...] * above[None] + ry_s[...] * below[None]
        for lo in range(0, Y, 4):
            hi = lo + 4
            lower = jnp.concatenate([above[None], p_s[0:hi - 1]], axis=0) if lo == 0 else p_s[lo - 1:hi - 1]
            upper = jnp.concatenate([p_s[lo + 1:Y], below[None]], axis=0) if hi == Y else p_s[lo + 1:hi + 1]
            x_source(lo, hi, lower, upper)
        left, right = x_second()
        above, below, coefs, ghosts = y_half(1, left, right)
        cx, cxl, cy, cyl, cl, ct, diag, scale = coefs
        sides = [[], [], []]
        for at in range(H):
            a, b = ghosts[0 if at < 2 else 1 if at < CY + 2 else 2]
            w = [wbuf[at, n] for n in range(8)]
            sides[0].append(w[0] * a + w[1] * b)
            sides[1].append(w[2] * a + w[3] * b)
            a1, b1, a2, b2 = pltpu.roll(a, 1, 0), pltpu.roll(b, 1, 0), pltpu.roll(a, Z - 1, 0), pltpu.roll(b, Z - 1, 0)
            sides[2].append(w[4] * a1 + w[5] * b1 + w[6] * a2 + w[7] * b2)
        partial = gathered([level_pairs(n, v) for n, v in enumerate(sides)], 0).reshape(H, CZ, X)
        await_sides(pbuf.at[pl.ds(0, 4)].reshape(2, 2, CZ, X), sw.at[2], (gx, north), has_n, has_s)
        res = jnp.where(inside, partial + pbuf[...], 0.0)
        cor = scale * res
        for repeat in range(COARSE - 1):
            lo, n = 1 + repeat, H - 2 - 2 * repeat
            cut = slice(lo, lo + n)
            mid, over, under = cor[1:-1], cor[:-2], cor[2:]
            applied = (
                diag[cut] * mid
                - cxl[cut] * pltpu.roll(mid, 1, 2)
                - cx[cut] * pltpu.roll(mid, X - 1, 2)
                - cyl[cut] * over
                - cy[cut] * under
                - cl[cut] * pltpu.roll(mid, 1, 1)
                - ct[cut] * pltpu.roll(mid, CZ - 1, 1)
            )
            cor = jnp.where(inside[cut], mid + scale[cut] * (res[cut] - applied), 0.0)
        fown[0:hj] = jnp.where(lane3 < half, pltpu.roll(cor[:hj], X - off, 2), pltpu.roll(cor[hj:], off, 2))
        fown[hj] = fringe(cor)
        fbuf[gx] = fown[...]
        return res, above, below

    res, above, below = pl.run_scoped(sweeps, pltpu.SemaphoreType.DMA((14,)), pltpu.SemaphoreType.DMA((3,)))
    comm = Comm(ssem)
    comm.send_all(lambda dev: fown, fbuf.at[gx], sx.at[0], x_peers, fbuf.at[pl.ds(0, nx - 1)])
    sedge[...] = fringe(res[2:CY + 2])
    comm.send(sedge, ebuf.at[1], sr.at[0], (west, gy), has_w)
    comm.send(sedge, ebuf.at[0], sr.at[0], (east, gy), has_e)
    above, below = above * ysc[0], below * ysc[1]
    for j in range(Y):
        op_ref[pl.ds(j, Z, stride=Y), :] = g_s[j] + ly_s[j] * above + ry_s[j] * below
    comm.finish()
    await_sides(ebuf, sr.at[0], (west, gy), has_w, has_e)
    both = jnp.where(clane < half, ebuf[0], ebuf[1])
    for r in range(CY):
        v = pltpu.roll(both, (off - 3 - SLOTS * r) % X, 1)
        v = res[2 + r] + jnp.where(jnp.logical_or(clane == off, clane == off + half - 1), v, 0.0)
        flip[pl.ds(r, CZ, stride=CY), :] = pltpu.roll(v, X - off, 1)
    or_ref[...] = flip[0:CZ * CY, :half]
    await_all(fbuf.at[pl.ds(0, nx - 1)], sx.at[0], x_peers[0])
    nothing = jnp.zeros((CZ, X), f32)
    edges = [nothing] + [fbuf[d, hj] for d in range(nx)] + [nothing]
    spill = jnp.logical_or(clane >= X - 3, jnp.logical_and(clane >= half, clane < half + 3))
    spill2 = jnp.logical_or(clane < 3, jnp.logical_and(clane >= half - 3, clane < half))
    for t in range(nx // 2):
        u, v = fbuf[2 * t, 0:hj], fbuf[2 * t + 1, 0:hj]
        top = jnp.where(lane3 < half, u, pltpu.roll(v, half, 2))
        low = jnp.where(lane3 < half, pltpu.roll(u, half, 2), v)
        one = jnp.where(clane < half, edges[2 * t + 1], edges[2 * t + 3])
        two = jnp.where(clane < half, edges[2 * t], edges[2 * t + 2])
        base = (t + 1) * CZ * CY
        for j in range(CY):
            turn = (half - 3 - SLOTS * j) % X
            v = top[j] if j < hj else low[j - hj]
            v = v + jnp.where(spill, pltpu.roll(one, turn, 1), 0.0)
            v = v + jnp.where(spill2, pltpu.roll(two, (turn + half) % X, 1), 0.0)
            flip[pl.ds(base + j, CZ, stride=CY), :] = v
        oc_ref[:, t * X:(t + 1) * X] = flip[base:base + CZ * CY, :]
    comm.finish()


def put(*refs):
    sems = refs[6]
    give = [pltpu.make_async_copy(refs[m], refs[3 + m], sems.at[m]) for m in range(3)]
    for copy in give:
        copy.start()
    for copy in give:
        copy.wait()


def body(nx, ny, *args):
    Z, Y, X = args[0].shape
    CZ, CY = Z // 2, Y // 2
    flat = [v.reshape(Z * Y, X) for v in args]
    f32 = jnp.float32

    def vm(*shape):
        return pltpu.VMEM(shape, f32)

    block, square, groups = (Y, Z, X), (Y * Z // X, X, X), Y * Z // X
    assert Y * SLOTS <= X and CY * SLOTS <= X // 2 and X % Z == 0 and Y * Z % X == 0 and X % 8 == 0
    nsx, nsy = len(strides_of(X)), len(strides_of(Y))
    assert nx > 1 and ny > 1
    dma = pltpu.SemaphoreType.DMA
    scratch = (
        [vm(*block) for _ in range(12)]
        + [vm(*square) for _ in range(6)] + [vm(nsx, 2, *square), vm(*block), vm(*block), vm(*block), vm(nsy, 2, *block)]
        + [vm(Z, X), vm(3, Z, X), vm(Z, X), vm(3, Z, X)]
        + [vm(nx, XC + 1, groups, X), vm(XC + 1, groups, X), vm(nx, groups, X), vm(2, groups, X)]
        + [vm(ny, 3, Z, X), vm(3, Z, X), vm(ny, 2, Z, X), vm(ny, Z, X), vm(2, 2, Z, X)]
        + [vm(1, groups, X)] + [vm(nx, groups, X) for _ in range(8)] + [vm(4, groups, X)]
        + [vm(ny, Z, X) for _ in range(6)] + [vm(6, Z, X), vm(2, Z, X)]
        + [vm(3, (CY + 4) * Z, X), pltpu.VMEM((4 * X, X), jnp.bfloat16), vm(2, CY, CZ, X), vm(3, 2, CY + 5, CZ, X),
           vm(CY + 4, 8, Z, X), vm(2, 2 * EDGE + 1, Z, X), vm(2, 4 * EDGE + 1, Z, X), vm(CY + 4, CZ, X), vm(2, Z, X), vm(2, Z, X),
           vm(2, CZ, X), vm(CZ, X), vm(CY // 2 + 1, CZ, X), vm(nx, CY // 2 + 1, CZ, X), vm((nx // 2 + 1) * CZ * CY, X)]
        + [dma((3,)), dma((2,)), dma((2,)), dma((3,)), dma((3,)), dma((1,)), dma((3,))]
        + [vm(6, Z * Y, X)]
    )
    p, r, c = pl.pallas_call(
        functools.partial(kernel, nx, ny),
        out_shape=(
            vm(Z * Y, X),
            vm(CZ * CY, X // 2),
            vm(CZ * CY, nx * X // 2),
        ),
        in_specs=[pl.BlockSpec(memory_space=pltpu.HBM)] * 6,
        out_specs=[pl.BlockSpec(memory_space=pltpu.VMEM)] * 3,
        scratch_shapes=scratch,
        compiler_params=pltpu.CompilerParams(
            collective_id=0, has_side_effects=True, vmem_limit_bytes=60000000
        ),
    )(*flat)
    p, r, c = pl.pallas_call(
        put,
        out_shape=tuple(jax.ShapeDtypeStruct(v.shape, f32) for v in (p, r, c)),
        in_specs=[pl.BlockSpec(memory_space=pltpu.VMEM)] * 3,
        out_specs=[pl.BlockSpec(memory_space=pltpu.HBM)] * 3,
        scratch_shapes=[dma((3,))],
    )(*[pltpu.with_memory_space_constraint(v, pltpu.VMEM) for v in (p, r, c)])
    return p.reshape(Z, Y, X), r.reshape(CZ, CY, X // 2), c.reshape(CZ, CY, nx * X // 2)


def solution(mesh):
    nx, ny = mesh.shape["gx"], mesh.shape["gy"]
    split = P(None, "gy", "gx")
    return jax.shard_map(
        functools.partial(body, nx, ny),
        mesh=mesh,
        in_specs=(split,) * 6,
        out_specs=(split, split, P(None, "gy", None)),
        check_vma=False,
    )
```

```python
import functools

import jax
import jax.numpy as jnp
from jax import lax
from jax.experimental import pallas as pl
from jax.experimental.pallas import tpu as pltpu
from jax.sharding import PartitionSpec as P

COARSE = 3
RELAX = 0.8
LE, LS, RE, RS, GS, GE, XC = range(7)
SLOTS = 8
EDGE = 4
MESH = pl.DeviceIdType.MESH


def strides_of(length):
    out, s = [], 1
    while s < length:
        out.append(s)
        s *= 2
    return out


class Comm:
    def __init__(self, send_sems):
        self.sems, self.used, self.pending = send_sems, 0, []

    def copy(self, src, dst, sem, recv, dev):
        return pltpu.make_async_remote_copy(
            src_ref=src, dst_ref=dst, send_sem=sem, recv_sem=recv, device_id=dev, device_id_type=MESH
        )

    def send(self, src, dst, recv, dev, cond=None):
        copy = self.copy(src, dst, self.sems.at[self.used], recv, dev)
        self.used += 1
        self.pending.append((copy, cond))
        if cond is None:
            copy.start()
        else:
            pl.when(cond)(copy.start)

    def send_all(self, src, dst, recv, devs, received):
        sem = self.sems.at[self.used]
        self.used += 1
        for dev in devs:
            self.copy(src(dev), dst, sem, recv, dev).start()
        self.pending.append((self.copy(received, received, sem, recv, devs[0]), None))

    def finish(self):
        for copy, cond in self.pending:
            if cond is None:
                copy.wait_send()
            else:
                pl.when(cond)(copy.wait_send)
        self.used, self.pending = 0, []


def await_recv(src, dst, sems, recv, dev, cond=None):
    copy = pltpu.make_async_remote_copy(
        src_ref=src, dst_ref=dst, send_sem=sems.at[0], recv_sem=recv, device_id=dev, device_id_type=MESH
    )
    if cond is None:
        copy.wait_recv()
    else:
        pl.when(cond)(copy.wait_recv)


def await_sides(buf, recv, dev, one, two):
    both = jnp.logical_and(one, two)
    pl.when(both)(lambda: await_all(buf, recv, dev))
    pl.when(jnp.logical_and(jnp.logical_or(one, two), jnp.logical_not(both)))(lambda: await_all(buf.at[0], recv, dev))


def await_all(part, recv, dev):
    pltpu.make_async_remote_copy(
        src_ref=part, dst_ref=part, send_sem=recv, recv_sem=recv, device_id=dev, device_id_type=MESH
    ).wait_recv()


def farthest_first(me, n):
    out = []
    for k in range(n - 1):
        down = jnp.where(n - 1 - k > me, n - 1 - k, n - 2 - k)
        up = jnp.where(k < me, k, k + 1)
        out.append(jnp.where(2 * me < n, down, up))
    return out


def flipped(me, n):
    if n & (n - 1):
        return [lax.rem(me + o, n) for o in range(1, n)]
    def peer_of(mask):
        peer, bit = 0, 1
        while bit < n:
            value = lax.rem(me // bit, 2)
            peer = peer + bit * (1 - value if mask & bit else value)
            bit *= 2
        return peer

    masks = list(range(n - 1, 0, -1))
    even, odd = [m for m in masks if m % 2 == 0], [m for m in masks if m % 2]
    first = lax.rem(me, 2) == 0
    return [jnp.where(first, peer_of(a), peer_of(b)) for a, b in zip(even + odd, odd + even)]


def interface_factor(n, me, ls, le, rs, re, own, tau, sig, bet, tau2, sig2, dlt, kk):
    beta = jnp.zeros_like(ls[0])
    for d in range(n):
        bet[d] = beta
        w = 1.0 / (1.0 - ls[d] * beta)
        t = le[d] * w
        tau[d] = t
        s = t * beta
        sig[d] = s
        beta = re[d] + s * rs[d]
    delta = jnp.zeros_like(ls[0])
    for d in reversed(range(n)):
        dlt[d] = delta
        w = 1.0 / (1.0 - re[d] * delta)
        t = rs[d] * w
        tau2[d] = t
        s = t * delta
        sig2[d] = s
        delta = ls[d] + s * le[d]
    ls_m, le_m, rs_m, re_m = own
    beta, delta = bet[me], dlt[me]
    a, b = 1.0 - beta * ls_m, 1.0 - delta * re_m
    o1, o2 = beta * rs_m, delta * le_m
    inv = 1.0 / (a * b - o1 * o2)
    kk[0], kk[1], kk[2], kk[3] = b * inv, o1 * inv, a * inv, o2 * inv
    kk[4], kk[5] = beta, delta


def interface_solve(n, me, h_left, h_right, gs, ge, tau, tau2, kk):
    alpha = jnp.zeros_like(gs)
    for d in range(n - 1):
        alpha = jnp.where(d < me, h_left(d) + tau[d] * alpha, alpha)
    gamma = jnp.zeros_like(gs)
    for d in reversed(range(1, n)):
        gamma = jnp.where(d > me, h_right(d) + tau2[d] * gamma, gamma)
    p = alpha + kk[4] * gs
    q = gamma + kk[5] * ge
    return kk[0] * p + kk[1] * q, kk[2] * q + kk[3] * p


def chain_factor(n, me, ls, le, rs, re, xc, own, rho, tau, sig, bet, tau2, sig2, scl, dlt, kk):
    one, zero = jnp.ones_like(ls[0]), jnp.zeros_like(ls[0])
    beta = zero
    for d in range(n):
        r = zero if d == 0 else xc[d - 1]
        b = one if d == 0 else 1.0 - r * (1.0 - beta)
        rho[d], bet[d] = r, b
        w = 1.0 / (1.0 - ls[d] * b)
        t = le[d] * w
        tau[d] = t * r
        s = t * b
        sig[d] = s
        beta = re[d] + s * rs[d]
    delta = zero
    for d in reversed(range(n)):
        dlt[d] = delta
        t = rs[d] / (1.0 - re[d] * delta)
        s = t * delta
        q = ls[d] + s * le[d]
        if d > 0:
            v = 1.0 / (1.0 - q + q * xc[d - 1])
            scl[d], tau2[d], sig2[d] = v, v * t, v * s
            delta = v * q * xc[d - 1]
        else:
            scl[d], tau2[d], sig2[d] = zero, zero, zero
    ls_m, le_m, rs_m, re_m = own
    beta, delta = bet[me], dlt[me]
    a, b = 1.0 - beta * ls_m, 1.0 - delta * re_m
    o1, o2 = beta * rs_m, delta * le_m
    inv = 1.0 / (a * b - o1 * o2)
    kk[0], kk[1], kk[2], kk[3] = b * inv, o1 * inv, a * inv, o2 * inv


def work(nx, ny, f_hbm, p_hbm, x_hbm, y_hbm, z_hbm, d_hbm, op_ref, or_ref, oc_ref,
           xl_s, xc_s, yl_s, yc_s, zl_s, zt_s, zd_s, fo_s, p_s, r_s, g_s, q_s,
           ct_s, rt_s, gt_s, lx_s, rx_s, ix_s, wx_s, ly_s, ry_s, iy_s, wy_s,
           sx0, sy0, hx, hy, xb, sxb, xb1, sx1, ycb, syc, yb0, yb1, shy,
           xown, xrho, xtau, xsig, xbet, xtau2, xsig2, xscl, xdlt, xkk,
           ytau, ysig, ybet, ytau2, ysig2, ydlt, ykk, ysc,
           pair_s, sel_s, cown, cbuf, wbuf, elr, nbr, pbuf, sxt, xtr, ebuf, sedge, fown, fbuf, flip,
           ins, ssem, s0, sx, sy, sc, sr, sw, sin):
    Y, Z, X = xc_s.shape
    CY, CZ = Y // 2, Z // 2
    f32 = jnp.float32
    gx, gy = lax.axis_index("gx"), lax.axis_index("gy")
    has_w, has_e = gx > 0, gx < nx - 1
    has_n, has_s = gy > 0, gy < ny - 1
    west, east = jnp.maximum(gx - 1, 0), jnp.minimum(gx + 1, nx - 1)
    north, south = jnp.maximum(gy - 1, 0), jnp.minimum(gy + 1, ny - 1)
    x_peers = [(i, gy) for i in farthest_first(gx, nx)]
    y_peers = [(gx, j) for j in flipped(gy, ny)]

    stages = ((0, 2), (2, 3), (3, 6))
    sources = (y_hbm, p_hbm, x_hbm, z_hbm, d_hbm, f_hbm)
    for n, (lo, hi) in enumerate(stages):
        for m in range(lo, hi):
            pltpu.make_async_copy(sources[m], ins.at[m], sin.at[n]).start()

    def loaded(n):
        part = ins.at[pl.ds(stages[n][0], stages[n][1] - stages[n][0])]
        pltpu.make_async_copy(part, part, sin.at[n]).wait()

    y_ref, p_ref, x_ref, z_ref, d_ref, f_ref = [ins.at[m] for m in range(6)]

    barrier = pltpu.get_barrier_semaphore()

    def greet(dev):
        pl.semaphore_signal(barrier, inc=1, device_id=dev, device_id_type=MESH)

    for dev in x_peers + y_peers:
        greet(dev)

    lane = lax.broadcasted_iota(jnp.int32, (Z, X), 1)
    level = lax.broadcasted_iota(jnp.int32, (Z, X), 0)
    lane3 = lax.broadcasted_iota(jnp.int32, (1, 1, X), 2)

    def rows(ref, j):
        return ref[pl.ds(j, Z, stride=Y), :]

    loaded(0)
    sy0[0] = rows(y_ref, Y - 1)
    sy0[1] = rows(p_ref, Y - 1)
    sy0[2] = rows(p_ref, 0)

    pl.semaphore_wait(barrier, (nx - 1) + (ny - 1))

    comm = Comm(ssem)
    comm.send(sy0.at[0:2], hy.at[0:2], s0.at[1], (gx, south), has_s)
    comm.send(sy0.at[2:3], hy.at[2:3], s0.at[1], (gx, north), has_n)

    loaded(1)
    packed = jnp.zeros((Z, X), f32)
    for j in range(Y):
        v = rows(x_ref, j)
        xc_s[j] = v
        packed = jnp.where(lane == SLOTS * j + XC, v[:, X - 1:], packed)
    sx0[...] = packed
    comm.send(sx0, hx, s0.at[0], (east, gy), has_e)

    for j in range(Y):
        yc_s[j] = rows(y_ref, j)
        p_s[j] = rows(p_ref, j)
    loaded(2)
    for j in range(Y):
        zv = jnp.where(level < Z - 1, rows(z_ref, j), 0.0)
        zt_s[j] = zv
        zl = pltpu.roll(zv, 1, 0)
        zl_s[j] = zl
        zd_s[j] = zv + zl + rows(d_ref, j)
        fo_s[j] = rows(f_ref, j)

    to_sides = (((gx, south), has_s, has_n), ((gx, north), has_n, has_s))
    per, groups, blocks = X // Z, Y * Z // X, X // 8
    sub = lax.broadcasted_iota(jnp.int32, (8, X), 0)

    def turned(ref, g):
        return ref[g * per:(g + 1) * per].reshape(X, X).T

    def split(v):
        return [v[8 * k:8 * k + 8] for k in range(blocks)]

    def shift(v, s, fill):
        if s % 8 == 0:
            m = s // 8
            return [v[k - m] if 0 <= k - m < blocks else fill for k in range(blocks)]
        turn = [pltpu.roll(u, s % 8, 0) for u in v]
        if s > 0:
            return [jnp.where(sub < s, fill if k == 0 else turn[k - 1], turn[k]) for k in range(blocks)]
        return [jnp.where(sub >= 8 + s, fill if k == blocks - 1 else turn[k + 1], turn[k]) for k in range(blocks)]

    def scaled(u, v):
        return [a if b is None else b if a is None else a * b for a, b in zip(u, v)]

    def added(u, v):
        return [a if b is None else a + b for a, b in zip(u, v)]

    def fill_of(s, value):
        return None if s % 8 == 0 else value

    def store(ref, at, v):
        for k in range(blocks):
            ref[at + (slice(8 * k, 8 * k + 8),)] = v[k]

    def load(ref, at):
        return [ref[at + (slice(8 * k, 8 * k + 8),)] for k in range(blocks)]

    xsteps = strides_of(X)

    def x_factor(g):
        c = load(ct_s, (g,))
        a = shift(c, 1, 1.0)
        for j in range(g * per, (g + 1) * per):
            g_s[j] = yl_s[j] + yc_s[j] + zd_s[j]
        e = split(turned(g_s, g))
        for n, s in enumerate(xsteps):
            inv = [1.0 / (u + v + w) for u, v, w in zip(a, c, e)]
            ai, ci = scaled(a, inv), scaled(c, inv)
            store(wx_s, (n, 0, g), ci)
            store(wx_s, (n, 1, g), ai)
            ae, ce = scaled(ai, e), scaled(ci, e)
            a = scaled(a, shift(ai, s, fill_of(s, 1.0)))
            c = scaled(c, shift(ci, -s, fill_of(s, 1.0)))
            e = added(added(e, shift(ce, s, fill_of(s, 0.0))), shift(ae, -s, fill_of(s, 0.0)))
        inv = [1.0 / (u + v + w) for u, v, w in zip(a, c, e)]
        a, c = scaled(a, inv), scaled(c, inv)
        store(ix_s, (g,), inv)
        store(lx_s, (g,), a)
        store(rx_s, (g,), c)
        one = slice(g, g + 1)
        sxb[LE, one], sxb[LS, one] = a[-1][7:8], a[0][0:1]
        sxb[RE, one], sxb[RS, one] = c[-1][7:8], c[0][0:1]
        sxb[XC, one] = ct_s[g, X - 1:X]

    def edge_sums(g):
        r = split(turned(r_s, g))
        store(rt_s, (g,), r)
        out = []
        for ref in (lx_s, rx_s):
            v = scaled(load(ref, (g,)), r)
            while len(v) > 1:
                v = [a + b for a, b in zip(v[0::2], v[1::2])]
            out.append(jnp.sum(v[0], axis=0, keepdims=True))
        return out

    def z_terms(v, part):
        return zl_s[part] * pltpu.roll(v, 1, 1) + zt_s[part] * pltpu.roll(v, Z - 1, 1)

    def x_source(lo, hi, lower, upper):
        part = slice(lo, hi)
        r_s[part] = fo_s[part] + yl_s[part] * lower + yc_s[part] * upper + z_terms(p_s[part], part)

    for g in range(groups):
        store(ct_s, (g,), split(turned(xc_s, g)))
    yl_s[1:Y] = yc_s[0:Y - 1]
    for g in range(1, groups):
        x_factor(g)
    x_source(1, Y - 1, p_s[0:Y - 2], p_s[2:Y])

    @pl.when(jnp.logical_not(has_w))
    def _():
        hx[...] = jnp.zeros_like(hx)
        cbuf[0] = jnp.zeros_like(cbuf[0])
        ebuf[0] = jnp.zeros_like(ebuf[0])

    @pl.when(jnp.logical_not(has_e))
    def _():
        cbuf[2] = jnp.zeros_like(cbuf[2])
        ebuf[1] = jnp.zeros_like(ebuf[1])

    @pl.when(jnp.logical_not(has_n))
    def _():
        hy[0:2] = jnp.zeros_like(hy[0:2])
        nbr[0] = jnp.zeros_like(nbr[0])
        pbuf[0:2] = jnp.zeros_like(pbuf[0:2])
        xtr[0] = jnp.zeros_like(xtr[0])
        for d in range(3):
            cbuf[d, :, 0:3] = jnp.zeros_like(cbuf[d, :, 0:3])

    @pl.when(jnp.logical_not(has_s))
    def _():
        hy[2] = jnp.zeros_like(hy[2])
        nbr[1] = jnp.zeros_like(nbr[1])
        pbuf[CY + 2:] = jnp.zeros_like(pbuf[CY + 2:])
        xtr[1] = jnp.zeros_like(xtr[1])
        for d in range(3):
            cbuf[d, :, 3 + CY:] = jnp.zeros_like(cbuf[d, :, 3 + CY:])

    for n, u in ((True, True), (True, False), (False, True)):
        cond = jnp.logical_and(has_n if n else jnp.logical_not(has_n), has_s if u else jnp.logical_not(has_s))
        part = hy.at[pl.ds(0, (2 if n else 0) + (1 if u else 0))]
        await_recv(part, part, ssem, s0.at[1], (gx, north), cond)

    yl_s[0] = hy[0]
    x_factor(0)
    x_source(0, 1, hy[1:2], p_s[1:2])
    x_source(Y - 1, Y, p_s[Y - 2:Y - 1], hy[2:3])
    for g in range(groups):
        one = slice(g, g + 1)
        sxb[GS, one], sxb[GE, one] = edge_sums(g)
    xb[gx] = sxb[...]
    comm.send_all(lambda dev: sxb, xb.at[gx], sx.at[0], x_peers, xb.at[pl.ds(0, nx - 1)])

    for n, (dev, there, _) in enumerate(to_sides):
        for k, ref in enumerate((xc_s, zt_s)):
            src = ref.at[pl.ds(0 if n else Y - EDGE, EDGE)]
            comm.send(src, nbr.at[n, pl.ds(k * EDGE, EDGE)], sw.at[0], dev, there)

    await_recv(sx0, hx, ssem, s0.at[0], (east, gy), has_w)
    for j in range(Y):
        xl_s[j] = jnp.where(lane == 0, hx[:, SLOTS * j + XC:SLOTS * j + XC + 1], pltpu.roll(xc_s[j], 1, 1))

    ysteps = strides_of(Y)
    for lo in range(0, Z, 8):
        zs = slice(lo, lo + 8)
        a = [yl_s[j, zs] for j in range(Y)]
        c = [yc_s[j, zs] for j in range(Y)]
        e = [xl_s[j, zs] + xc_s[j, zs] + zd_s[j, zs] for j in range(Y)]
        for n, s in enumerate(ysteps):
            inv = [1.0 / (a[j] + c[j] + e[j]) for j in range(Y)]
            ai, ci = [a[j] * inv[j] for j in range(Y)], [c[j] * inv[j] for j in range(Y)]
            for j in range(Y):
                if j + s < Y:
                    wy_s[n, 0, j, zs] = ci[j]
                if j >= s:
                    wy_s[n, 1, j, zs] = ai[j]
            e2 = []
            for j in range(Y):
                v = e[j]
                if j >= s:
                    v = v + ci[j - s] * e[j - s]
                if j + s < Y:
                    v = v + ai[j + s] * e[j + s]
                e2.append(v)
            a = [a[j] * ai[j - s] if j >= s else a[j] for j in range(Y)]
            c = [c[j] * ci[j + s] if j + s < Y else c[j] for j in range(Y)]
            e = e2
        for j in range(Y):
            inv = 1.0 / (a[j] + c[j] + e[j])
            iy_s[j, zs], ly_s[j, zs], ry_s[j, zs] = inv, a[j] * inv, c[j] * inv

    k_top, k_end = jnp.sqrt(yl_s[0]), jnp.sqrt(yc_s[Y - 1])
    i_top = jnp.where(has_n, 1.0 / jnp.where(has_n, k_top, 1.0), 0.0)
    ysc[0], ysc[1] = i_top, 1.0 / k_end
    syc[0], syc[1], syc[2] = ly_s[0], ly_s[Y - 1] * k_end * i_top, ry_s[Y - 1]
    ycb[gy] = syc[...]
    comm.send_all(lambda dev: syc, ycb.at[gy], sy.at[2], y_peers, ycb.at[pl.ds(0, ny - 1)])

    def x_local():
        for g in range(groups):
            r = load(rt_s, (g,))
            for n, s in enumerate(xsteps):
                low = shift(scaled(load(wx_s, (n, 0, g)), r), s, fill_of(s, 0.0))
                high = shift(scaled(load(wx_s, (n, 1, g)), r), -s, fill_of(s, 0.0))
                r = added(added(r, low), high)
            store(gt_s, (g,), scaled(r, load(ix_s, (g,))))

    def y_local():
        for lo in range(0, Z, 8):
            zs = slice(lo, lo + 8)
            r = [r_s[j, zs] for j in range(Y)]
            for n, s in enumerate(ysteps):
                low = [wy_s[n, 0, j, zs] * r[j] if j + s < Y else None for j in range(Y)]
                high = [wy_s[n, 1, j, zs] * r[j] if j >= s else None for j in range(Y)]
                r2 = []
                for j in range(Y):
                    v = r[j]
                    if j >= s:
                        v = v + low[j - s]
                    if j + s < Y:
                        v = v + high[j + s]
                    r2.append(v)
                r = r2
            for j in range(Y):
                g_s[j, zs] = r[j] * iy_s[j, zs]

    x_local()

    half = X // 2
    off = half // 2
    ii = lax.broadcasted_iota(jnp.int32, (X, X), 0)
    mm = lax.broadcasted_iota(jnp.int32, (X, X), 1)

    def selection(step, start):
        target = lax.rem((ii + (step + 2)) // 2 - 1 + start + X, X)
        return jnp.where(mm == target, 0.125, 0.0)

    def level_pairs(n, levels):
        for k, v in enumerate(levels):
            pair_s[n, k * Z:(k + 1) * Z] = v
        count = len(levels) * CZ
        return pair_s[n, pl.ds(0, count, stride=2), :] + pair_s[n, pl.ds(1, count, stride=2), :]

    def pairs(n, field):
        return level_pairs(n, [field(2 * k) + field(2 * k + 1) for k in range(CY)])

    def gathered(parts, first):
        v = jnp.concatenate(parts, axis=1)
        high = v.astype(jnp.bfloat16)
        v = v - high.astype(f32)
        mid = v.astype(jnp.bfloat16)
        low = (v - mid.astype(f32)).astype(jnp.bfloat16)
        sel = sel_s[first * X:(first + len(parts)) * X]
        return sum(jnp.dot(u, sel, preferred_element_type=f32) for u in (low, mid, high))

    for n, sel in enumerate((selection(1, off), selection(-1, off), selection(0, off), selection(0, half + off))):
        sel_s[n * X:(n + 1) * X] = sel.astype(jnp.bfloat16)
    for m, (u, v) in enumerate(((lambda j: xc_s[j], lambda j: yc_s[j]), (lambda j: rows(z_ref, j), lambda j: rows(d_ref, j)))):
        part = gathered([pairs(0, u), pairs(1, v)], 2).reshape(CY, CZ, X)
        cown[m] = part
        cbuf[1, m, 3:3 + CY] = part

    def operator(at, xc, xl, zl, zt, sides):
        for n, (u, v) in enumerate(sides):
            wbuf[at, n] = xc[0] * u + xc[1] * v
            wbuf[at, 2 + n] = xl[0] * u + xl[1] * v
            wbuf[at, 4 + n] = zl[0] * pltpu.roll(u, 1, 0) + zl[1] * pltpu.roll(v, 1, 0)
            wbuf[at, 6 + n] = zt[0] * pltpu.roll(u, Z - 1, 0) + zt[1] * pltpu.roll(v, Z - 1, 0)

    for k in range(EDGE):
        for n, j in enumerate((Y - EDGE + k, k)):
            elr[n, k], elr[n, EDGE + k] = ly_s[j] * ysc[0], ry_s[j] * ysc[1]
    for n in range(2):
        elr[n, 2 * EDGE] = hx[...]
    for k in range(CY):
        two = (2 * k, 2 * k + 1)
        operator(2 + k, *[[ref[j] for j in two] for ref in (xc_s, xl_s, zl_s, zt_s)],
                 [[ref[j] * ysc[n] for j in two] for n, ref in enumerate((ly_s, ry_s))])

    def edge_columns():
        for n, (dev, there, _) in enumerate(to_sides):
            comm.send(elr.at[n], nbr.at[n, pl.ds(2 * EDGE, 2 * EDGE + 1)], sw.at[0], dev, there)

    def edge_operators():
        await_sides(nbr, sw.at[0], (gx, north), has_n, has_s)
        for n, first in enumerate((Y - EDGE, 0)):
            for k in range(0, EDGE, 2):
                xc = [nbr[n, k + i] for i in range(2)]
                zt = [nbr[n, EDGE + k + i] for i in range(2)]
                cols = [SLOTS * (first + k + i) + XC for i in range(2)]
                xl = [jnp.where(lane == 0, nbr[n, 4 * EDGE, :, c:c + 1], pltpu.roll(v, 1, 1)) for c, v in zip(cols, xc)]
                operator(n * (CY + 2) + k // 2, xc, xl, [pltpu.roll(v, 1, 0) for v in zt], zt,
                         [[nbr[n, (2 + m) * EDGE + k + i] for i in range(2)] for m in range(2)])

    def edge_rows():
        for dev, there, src, dst in (((gx, north), has_n, 2, CY + 2), ((gx, south), has_s, CY, 0)):
            comm.send(pbuf.at[pl.ds(src, 2)], pbuf.at[pl.ds(dst, 2)], sw.at[2], dev, there)

    def coarse_send(straight):
        for i, ok, back in ((west, has_w, 2), (gx, None, 1), (east, has_e, 0)):
            both = (lambda c: c) if ok is None else (lambda c, ok=ok: jnp.logical_and(c, ok))
            if straight:
                if ok is not None:
                    comm.send(cown, cbuf.at[back, :, pl.ds(3, CY)], sc.at[back], (i, gy), ok)
            else:
                comm.send(cown.at[:, pl.ds(CY - 3, 3)], cbuf.at[back, :, pl.ds(0, 3)], sc.at[back], (i, south), both(has_s))
                comm.send(cown.at[:, pl.ds(0, 2)], cbuf.at[back, :, pl.ds(3 + CY, 2)], sc.at[back], (i, north), both(has_n))

    def coarse_wait():
        for slot, i, ok in ((0, west, has_w), (1, gx, None), (2, east, has_e)):
            kept = 0 if ok is None else CY
            for n, s in ((True, True), (True, False), (False, True)):
                cond = jnp.logical_and(has_n if n else jnp.logical_not(has_n), has_s if s else jnp.logical_not(has_s))
                cond = cond if ok is None else jnp.logical_and(cond, ok)
                part = cbuf.at[slot, :, pl.ds(0, kept + (3 if n else 0) + (2 if s else 0))]
                await_recv(part, part, ssem, sc.at[slot], (i, gy), cond)

    def x_solve(hl, hr, gs, ge):
        alpha = jnp.zeros((groups, X), f32)
        for d in range(nx - 1):
            alpha = jnp.where(d < gx, hl(d) + xtau[d] * alpha, alpha)
        gamma = jnp.zeros((groups, X), f32)
        for d in reversed(range(1, nx)):
            gamma = jnp.where(d > gx, hr(d) + xtau2[d] * gamma, gamma)
        p = xrho[gx] * alpha + xbet[gx] * gs
        q = gamma + xdlt[gx] * ge
        return xkk[0] * p + xkk[1] * q, xkk[2] * q + xkk[3] * p

    def x_first():
        await_all(xb.at[pl.ds(0, nx - 1)], sx.at[0], x_peers[0])
        cut = [[xb[d, k] for d in range(nx)] for k in range(XC + 1)]
        own = [sxb[k] for k in range(XC + 1)]
        inv = [1.0 / v for v in cut[XC]]
        ge = [cut[GE][d] * inv[d] for d in range(nx)]
        gs = cut[GS]
        xown[0] = 1.0 / own[XC]
        chain_factor(nx, gx, cut[LS], cut[LE], cut[RS], cut[RE], cut[XC], [own[LS], own[LE], own[RS], own[RE]],
                     xrho, xtau, xsig, xbet, xtau2, xsig2, xscl, xdlt, xkk)
        return x_solve(
            lambda d: ge[d] + xsig[d] * gs[d], lambda d: xscl[d] * gs[d] + xsig2[d] * ge[d], own[GS], own[GE] * xown[0]
        )

    def x_second():
        sums = [edge_sums(g) for g in range(groups)]
        gs, ge = [jnp.concatenate([v[n] for v in sums], axis=0) for n in range(2)]
        ge = ge * xown[0]
        sx1[0], sx1[1] = ge + xsig[gx] * gs, xscl[gx] * gs + xsig2[gx] * ge
        comm.send_all(
            lambda dev: sx1.at[jnp.where(dev[0] > gx, 0, 1)], xb1.at[gx], sx.at[1], x_peers, xb1.at[pl.ds(0, nx - 1)]
        )
        coarse_send(False)
        edge_columns()
        x_local()
        await_all(xb1.at[pl.ds(0, nx - 1)], sx.at[1], x_peers[0])
        return x_solve(lambda d: xb1[d], lambda d: xb1[d], gs, ge)

    def y_half(m, left, right):
        top, end = jnp.zeros((Z, X), f32), jnp.zeros((Z, X), f32)
        for g in range(groups):
            u, w = left[g:g + 1], right[g:g + 1]
            c, v = load(ct_s, (g,)), []
            for a, b, d in zip(load(gt_s, (g,)), load(lx_s, (g,)), load(rx_s, (g,))):
                v.append(a + b * u + d * w)
            edge = u + (xrho[gx][g:g + 1] - 1.0) * v[0][0:1]
            t = added(shift(scaled(c, v), 1, edge), scaled(c, shift(v, -1, w)))
            v = jnp.concatenate(v, axis=0).T.reshape(per, Z, X)
            t = jnp.concatenate(t, axis=0).T.reshape(per, Z, X)
            for n in range(per):
                j = g * per + n
                q_s[j] = v[n]
                r = fo_s[j] + t[n] + zl_s[j] * pltpu.roll(v[n], 1, 0) + zt_s[j] * pltpu.roll(v[n], Z - 1, 0)
                r_s[j] = r
                top, end = top + ly_s[j] * r, end + ry_s[j] * r
        top, end = top * ysc[0], end * ysc[1]
        if m == 0:
            shy[0, 0], shy[0, 1] = top, end
            yb0[gy] = shy[0]
            comm.send_all(lambda dev: shy.at[0], yb0.at[gy], sy.at[0], y_peers, yb0.at[pl.ds(0, ny - 1)])
        else:
            shy[1, 0] = end + ysig[gy] * top
            shy[1, 1] = top + ysig2[gy] * end
            yb1[gy] = shy[1, 0]
            comm.send_all(
                lambda dev: shy.at[1, jnp.where(dev[1] > gy, 0, 1)], yb1.at[gy], sy.at[1], y_peers, yb1.at[pl.ds(0, ny - 1)]
            )
        if m:
            sxt[0], sxt[1] = end, top
            comm.send(sxt.at[0], xtr.at[1], sw.at[1], (gx, north), has_n)
            comm.send(sxt.at[1], xtr.at[0], sw.at[1], (gx, south), has_s)
        y_local()
        if m == 0:
            coarse_send(True)
            await_all(ycb.at[pl.ds(0, ny - 1)], sy.at[2], y_peers[0])
            ls, mid, re = [[ycb[d, k] for d in range(ny)] for k in range(3)]
            interface_factor(
                ny, gy, ls, mid, mid, re, [syc[0], syc[1], syc[1], syc[2]],
                ytau, ysig, ybet, ytau2, ysig2, ydlt, ykk,
            )
            comm.finish()
            await_all(yb0.at[pl.ds(0, ny - 1)], sy.at[0], y_peers[0])
            above, below = interface_solve(
                ny, gy, lambda d: yb0[d, 1] + ysig[d] * yb0[d, 0], lambda d: yb0[d, 0] + ysig2[d] * yb0[d, 1],
                top, end, ytau, ytau2, ykk,
            )
            return above * ysc[0], below * ysc[1]
        else:
            for j in range(Y):
                r_s[j] = g_s[j] - q_s[j]
            pbuf[2:CY + 2] = gathered([
                pairs(0, lambda j: xc_s[j] * r_s[j]),
                pairs(1, lambda j: xl_s[j] * r_s[j]),
                pairs(2, lambda j: zl_s[j] * pltpu.roll(r_s[j], 1, 0) + zt_s[j] * pltpu.roll(r_s[j], Z - 1, 0)),
            ], 0).reshape(CY, CZ, X)
            edge_rows()
            comm.finish()
            coarse_wait()
            coefs = planes()
            edge_operators()
        await_all(yb1.at[pl.ds(0, ny - 1)], sy.at[1], y_peers[0])
        above, below = interface_solve(ny, gy, lambda d: yb1[d], lambda d: yb1[d], top, end, ytau, ytau2, ykk)
        await_sides(xtr, sw.at[1], (gx, north), has_n, has_s)
        alpha, gamma = jnp.zeros((Z, X), f32), jnp.zeros((Z, X), f32)
        for d in range(ny - 2):
            alpha = jnp.where(d < gy - 1, yb1[d] + ytau[d] * alpha, alpha)
        for d in reversed(range(2, ny)):
            gamma = jnp.where(d > gy + 1, yb1[d] + ytau2[d] * gamma, gamma)
        q_top = top + syc[0] * above + syc[1] * below
        q_end = end + syc[1] * above + syc[2] * below
        beta, delta = ybet[north], ydlt[south]
        over = (alpha + beta * (xtr[0] + ycb[north, 1] * q_top)) / (1.0 - beta * ycb[north, 0])
        under = (gamma + delta * (xtr[1] + ycb[south, 1] * q_end)) / (1.0 - delta * ycb[south, 2])
        return above, below, coefs, [(over, q_top), (above, below), (q_end, under)]

    centre = jnp.logical_and(lane3 >= off, lane3 < off + half)
    H = CY + 4
    row = lax.broadcasted_iota(jnp.int32, (H, 1, 1), 0)
    inside = jnp.logical_and(
        jnp.logical_or(row >= 2, has_n), jnp.logical_or(row < 2 + CY, has_s)
    )
    inside = jnp.logical_and(
        inside,
        jnp.logical_and(jnp.logical_or(lane3 >= off, has_w), jnp.logical_or(lane3 < off + half, has_e)),
    )

    def planes():
        out = []
        for m in range(2):
            w, o, e = cbuf[0, m], cbuf[1, m], cbuf[2, m]
            out.append(jnp.where(centre, o, pltpu.roll(jnp.where(lane3 >= half, w, e), half, 2)))
            out.append(jnp.where(centre, pltpu.roll(o, half, 2), jnp.where(lane3 < half, w, e)))
        cx, cy, cz, cd = out
        czl = lax.broadcasted_iota(jnp.int32, (1, CZ, 1), 1)
        cyl, cy = cy[:H], cy[1:]
        cx, cz, cd = cx[1:], cz[1:], cd[1:]
        cd = jnp.where(inside, cd, 1.0)
        ct = jnp.where(czl < CZ - 1, cz, 0.0)
        cl = pltpu.roll(ct, 1, 1)
        cxl = pltpu.roll(cx, 1, 2)
        diag = cxl + cx + cyl + cy + cl + ct + cd
        return cx, cxl, cy, cyl, cl, ct, diag, RELAX / diag

    left, right = x_first()
    above, below = y_half(0, left, right)
    p_s[...] = g_s[...] + ly_s[...] * above[None] + ry_s[...] * below[None]
    for lo in range(0, Y, 4):
        hi = lo + 4
        lower = jnp.concatenate([above[None], p_s[0:hi - 1]], axis=0) if lo == 0 else p_s[lo - 1:hi - 1]
        upper = jnp.concatenate([p_s[lo + 1:Y], below[None]], axis=0) if hi == Y else p_s[lo + 1:hi + 1]
        x_source(lo, hi, lower, upper)
    left, right = x_second()
    above, below, coefs, ghosts = y_half(1, left, right)
    cx, cxl, cy, cyl, cl, ct, diag, scale = coefs
    sides = [[], [], []]
    for at in range(H):
        a, b = ghosts[0 if at < 2 else 1 if at < CY + 2 else 2]
        w = [wbuf[at, n] for n in range(8)]
        sides[0].append(w[0] * a + w[1] * b)
        sides[1].append(w[2] * a + w[3] * b)
        a1, b1, a2, b2 = pltpu.roll(a, 1, 0), pltpu.roll(b, 1, 0), pltpu.roll(a, Z - 1, 0), pltpu.roll(b, Z - 1, 0)
        sides[2].append(w[4] * a1 + w[5] * b1 + w[6] * a2 + w[7] * b2)
    partial = gathered([level_pairs(n, v) for n, v in enumerate(sides)], 0).reshape(H, CZ, X)
    await_sides(pbuf.at[pl.ds(0, 4)].reshape(2, 2, CZ, X), sw.at[2], (gx, north), has_n, has_s)
    res = jnp.where(inside, partial + pbuf[...], 0.0)
    clane = lax.broadcasted_iota(jnp.int32, (CZ, X), 1)
    inner = clane % half

    def fringe(v):
        edge = jnp.zeros((CZ, X), f32)
        for r in range(CY):
            edge = jnp.where(inner >= SLOTS * r, pltpu.roll(v[r], half - off + 3 + SLOTS * r, 1), edge)
        return edge

    cor = scale * res
    for repeat in range(COARSE - 1):
        lo, n = 1 + repeat, H - 2 - 2 * repeat
        cut = slice(lo, lo + n)
        mid, over, under = cor[1:-1], cor[:-2], cor[2:]
        applied = (
            diag[cut] * mid
            - cxl[cut] * pltpu.roll(mid, 1, 2)
            - cx[cut] * pltpu.roll(mid, X - 1, 2)
            - cyl[cut] * over
            - cy[cut] * under
            - cl[cut] * pltpu.roll(mid, 1, 1)
            - ct[cut] * pltpu.roll(mid, CZ - 1, 1)
        )
        cor = jnp.where(inside[cut], mid + scale[cut] * (res[cut] - applied), 0.0)
    hj = CY // 2
    fown[0:hj] = jnp.where(lane3 < half, pltpu.roll(cor[:hj], X - off, 2), pltpu.roll(cor[hj:], off, 2))
    fown[hj] = fringe(cor)
    fbuf[gx] = fown[...]
    comm.send_all(lambda dev: fown, fbuf.at[gx], sx.at[0], x_peers, fbuf.at[pl.ds(0, nx - 1)])
    sedge[...] = fringe(res[2:CY + 2])
    comm.send(sedge, ebuf.at[1], sr.at[0], (west, gy), has_w)
    comm.send(sedge, ebuf.at[0], sr.at[0], (east, gy), has_e)
    above, below = above * ysc[0], below * ysc[1]
    for j in range(Y):
        op_ref[pl.ds(j, Z, stride=Y), :] = g_s[j] + ly_s[j] * above + ry_s[j] * below
    comm.finish()
    await_sides(ebuf, sr.at[0], (west, gy), has_w, has_e)
    both = jnp.where(clane < half, ebuf[0], ebuf[1])
    for r in range(CY):
        v = pltpu.roll(both, (off - 3 - SLOTS * r) % X, 1)
        v = res[2 + r] + jnp.where(jnp.logical_or(clane == off, clane == off + half - 1), v, 0.0)
        flip[pl.ds(r, CZ, stride=CY), :] = pltpu.roll(v, X - off, 1)
    or_ref[...] = flip[0:CZ * CY, :half]
    await_all(fbuf.at[pl.ds(0, nx - 1)], sx.at[0], x_peers[0])
    nothing = jnp.zeros((CZ, X), f32)
    edges = [nothing] + [fbuf[d, hj] for d in range(nx)] + [nothing]
    spill = jnp.logical_or(clane >= X - 3, jnp.logical_and(clane >= half, clane < half + 3))
    spill2 = jnp.logical_or(clane < 3, jnp.logical_and(clane >= half - 3, clane < half))
    for t in range(nx // 2):
        u, v = fbuf[2 * t, 0:hj], fbuf[2 * t + 1, 0:hj]
        top = jnp.where(lane3 < half, u, pltpu.roll(v, half, 2))
        low = jnp.where(lane3 < half, pltpu.roll(u, half, 2), v)
        one = jnp.where(clane < half, edges[2 * t + 1], edges[2 * t + 3])
        two = jnp.where(clane < half, edges[2 * t], edges[2 * t + 2])
        base = (t + 1) * CZ * CY
        for j in range(CY):
            turn = (half - 3 - SLOTS * j) % X
            v = top[j] if j < hj else low[j - hj]
            v = v + jnp.where(spill, pltpu.roll(one, turn, 1), 0.0)
            v = v + jnp.where(spill2, pltpu.roll(two, (turn + half) % X, 1), 0.0)
            flip[pl.ds(base + j, CZ, stride=CY), :] = v
        oc_ref[:, t * X:(t + 1) * X] = flip[base:base + CZ * CY, :]
    comm.finish()


def kernel(nx, ny, *refs):
    sems = [pltpu.SemaphoreType.DMA((n,)) for n in (14, 2, 2, 3, 3, 1, 3, 3)]
    pl.run_scoped(functools.partial(work, nx, ny, *refs), *sems)


def put(*refs):
    sems = refs[6]
    give = [pltpu.make_async_copy(refs[m], refs[3 + m], sems.at[m]) for m in range(3)]
    for copy in give:
        copy.start()
    for copy in give:
        copy.wait()


def body(nx, ny, *args):
    Z, Y, X = args[0].shape
    CZ, CY = Z // 2, Y // 2
    flat = [v.reshape(Z * Y, X) for v in args]
    f32 = jnp.float32

    def vm(*shape):
        return pltpu.VMEM(shape, f32)

    block, square, groups = (Y, Z, X), (Y * Z // X, X, X), Y * Z // X
    assert Y * SLOTS <= X and CY * SLOTS <= X // 2 and X % Z == 0 and Y * Z % X == 0 and X % 8 == 0
    nsx, nsy = len(strides_of(X)), len(strides_of(Y))
    assert nx > 1 and ny > 1
    dma = pltpu.SemaphoreType.DMA
    scratch = (
        [vm(*block) for _ in range(12)]
        + [vm(*square) for _ in range(6)] + [vm(nsx, 2, *square), vm(*block), vm(*block), vm(*block), vm(nsy, 2, *block)]
        + [vm(Z, X), vm(3, Z, X), vm(Z, X), vm(3, Z, X)]
        + [vm(nx, XC + 1, groups, X), vm(XC + 1, groups, X), vm(nx, groups, X), vm(2, groups, X)]
        + [vm(ny, 3, Z, X), vm(3, Z, X), vm(ny, 2, Z, X), vm(ny, Z, X), vm(2, 2, Z, X)]
        + [vm(1, groups, X)] + [vm(nx, groups, X) for _ in range(8)] + [vm(4, groups, X)]
        + [vm(ny, Z, X) for _ in range(6)] + [vm(6, Z, X), vm(2, Z, X)]
        + [vm(3, (CY + 4) * Z, X), pltpu.VMEM((4 * X, X), jnp.bfloat16), vm(2, CY, CZ, X), vm(3, 2, CY + 5, CZ, X),
           vm(CY + 4, 8, Z, X), vm(2, 2 * EDGE + 1, Z, X), vm(2, 4 * EDGE + 1, Z, X), vm(CY + 4, CZ, X), vm(2, Z, X), vm(2, Z, X),
           vm(2, CZ, X), vm(CZ, X), vm(CY // 2 + 1, CZ, X), vm(nx, CY // 2 + 1, CZ, X), vm((nx // 2 + 1) * CZ * CY, X)]
        + [vm(6, Z * Y, X)]
    )
    p, r, c = pl.pallas_call(
        functools.partial(kernel, nx, ny),
        out_shape=(
            vm(Z * Y, X),
            vm(CZ * CY, X // 2),
            vm(CZ * CY, nx * X // 2),
        ),
        in_specs=[pl.BlockSpec(memory_space=pltpu.HBM)] * 6,
        out_specs=[pl.BlockSpec(memory_space=pltpu.VMEM)] * 3,
        scratch_shapes=scratch,
        compiler_params=pltpu.CompilerParams(
            collective_id=0, has_side_effects=True, vmem_limit_bytes=60000000
        ),
    )(*flat)
    p, r, c = pl.pallas_call(
        put,
        out_shape=tuple(jax.ShapeDtypeStruct(v.shape, f32) for v in (p, r, c)),
        in_specs=[pl.BlockSpec(memory_space=pltpu.VMEM)] * 3,
        out_specs=[pl.BlockSpec(memory_space=pltpu.HBM)] * 3,
        scratch_shapes=[dma((3,))],
    )(*[pltpu.with_memory_space_constraint(v, pltpu.VMEM) for v in (p, r, c)])
    return p.reshape(Z, Y, X), r.reshape(CZ, CY, X // 2), c.reshape(CZ, CY, nx * X // 2)


def solution(mesh):
    nx, ny = mesh.shape["gx"], mesh.shape["gy"]
    split = P(None, "gy", "gx")
    return jax.shard_map(
        functools.partial(body, nx, ny),
        mesh=mesh,
        in_specs=(split,) * 6,
        out_specs=(split, split, P(None, "gy", None)),
        check_vma=False,
    )
```

```python
import functools

import jax
import jax.numpy as jnp
from jax import lax
from jax.experimental import pallas as pl
from jax.experimental.pallas import tpu as pltpu
from jax.sharding import PartitionSpec as P

COARSE = 3
RELAX = 0.8
LE, LS, RE, RS, GS, GE, XC = range(7)
SLOTS = 8
EDGE = 4
MESH = pl.DeviceIdType.MESH


def strides_of(length):
    out, s = [], 1
    while s < length:
        out.append(s)
        s *= 2
    return out


class Comm:
    def __init__(self, send_sems):
        self.sems, self.used, self.pending = send_sems, 0, []

    def copy(self, src, dst, sem, recv, dev):
        return pltpu.make_async_remote_copy(
            src_ref=src, dst_ref=dst, send_sem=sem, recv_sem=recv, device_id=dev, device_id_type=MESH
        )

    def send(self, src, dst, recv, dev, cond=None):
        copy = self.copy(src, dst, self.sems.at[self.used], recv, dev)
        self.used += 1
        self.pending.append((copy, cond))
        if cond is None:
            copy.start()
        else:
            pl.when(cond)(copy.start)

    def send_all(self, src, dst, recv, devs, received):
        sem = self.sems.at[self.used]
        self.used += 1
        for dev in devs:
            self.copy(src(dev), dst, sem, recv, dev).start()
        self.pending.append((self.copy(received, received, sem, recv, devs[0]), None))

    def finish(self):
        for copy, cond in self.pending:
            if cond is None:
                copy.wait_send()
            else:
                pl.when(cond)(copy.wait_send)
        self.used, self.pending = 0, []


def await_recv(src, dst, sems, recv, dev, cond=None):
    copy = pltpu.make_async_remote_copy(
        src_ref=src, dst_ref=dst, send_sem=sems.at[0], recv_sem=recv, device_id=dev, device_id_type=MESH
    )
    if cond is None:
        copy.wait_recv()
    else:
        pl.when(cond)(copy.wait_recv)


def await_sides(buf, recv, dev, one, two):
    both = jnp.logical_and(one, two)
    pl.when(both)(lambda: await_all(buf, recv, dev))
    pl.when(jnp.logical_and(jnp.logical_or(one, two), jnp.logical_not(both)))(lambda: await_all(buf.at[0], recv, dev))


def await_all(part, recv, dev):
    pltpu.make_async_remote_copy(
        src_ref=part, dst_ref=part, send_sem=recv, recv_sem=recv, device_id=dev, device_id_type=MESH
    ).wait_recv()


def farthest_first(me, n):
    out = []
    for k in range(n - 1):
        down = jnp.where(n - 1 - k > me, n - 1 - k, n - 2 - k)
        up = jnp.where(k < me, k, k + 1)
        out.append(jnp.where(2 * me < n, down, up))
    return out


def flipped(me, n):
    if n & (n - 1):
        return [lax.rem(me + o, n) for o in range(1, n)]
    def peer_of(mask):
        peer, bit = 0, 1
        while bit < n:
            value = lax.rem(me // bit, 2)
            peer = peer + bit * (1 - value if mask & bit else value)
            bit *= 2
        return peer

    masks = list(range(n - 1, 0, -1))
    even, odd = [m for m in masks if m % 2 == 0], [m for m in masks if m % 2]
    first = lax.rem(me, 2) == 0
    return [jnp.where(first, peer_of(a), peer_of(b)) for a, b in zip(even + odd, odd + even)]


def interface_factor(n, me, ls, le, rs, re, own, tau, sig, bet, tau2, sig2, dlt, kk):
    beta = jnp.zeros_like(ls[0])
    for d in range(n):
        bet[d] = beta
        w = 1.0 / (1.0 - ls[d] * beta)
        t = le[d] * w
        tau[d] = t
        s = t * beta
        sig[d] = s
        beta = re[d] + s * rs[d]
    delta = jnp.zeros_like(ls[0])
    for d in reversed(range(n)):
        dlt[d] = delta
        w = 1.0 / (1.0 - re[d] * delta)
        t = rs[d] * w
        tau2[d] = t
        s = t * delta
        sig2[d] = s
        delta = ls[d] + s * le[d]
    ls_m, le_m, rs_m, re_m = own
    beta, delta = bet[me], dlt[me]
    a, b = 1.0 - beta * ls_m, 1.0 - delta * re_m
    o1, o2 = beta * rs_m, delta * le_m
    inv = 1.0 / (a * b - o1 * o2)
    kk[0], kk[1], kk[2], kk[3] = b * inv, o1 * inv, a * inv, o2 * inv
    kk[4], kk[5] = beta, delta


def interface_solve(n, me, h_left, h_right, gs, ge, tau, tau2, kk):
    alpha = jnp.zeros_like(gs)
    for d in range(n - 1):
        alpha = jnp.where(d < me, h_left(d) + tau[d] * alpha, alpha)
    gamma = jnp.zeros_like(gs)
    for d in reversed(range(1, n)):
        gamma = jnp.where(d > me, h_right(d) + tau2[d] * gamma, gamma)
    p = alpha + kk[4] * gs
    q = gamma + kk[5] * ge
    return kk[0] * p + kk[1] * q, kk[2] * q + kk[3] * p


def chain_factor(n, me, ls, le, rs, re, xc, own, rho, tau, sig, bet, tau2, sig2, scl, dlt, kk):
    one, zero = jnp.ones_like(ls[0]), jnp.zeros_like(ls[0])
    beta = zero
    for d in range(n):
        r = zero if d == 0 else xc[d - 1]
        b = one if d == 0 else 1.0 - r * (1.0 - beta)
        rho[d], bet[d] = r, b
        w = 1.0 / (1.0 - ls[d] * b)
        t = le[d] * w
        tau[d] = t * r
        s = t * b
        sig[d] = s
        beta = re[d] + s * rs[d]
    delta = zero
    for d in reversed(range(n)):
        dlt[d] = delta
        t = rs[d] / (1.0 - re[d] * delta)
        s = t * delta
        q = ls[d] + s * le[d]
        if d > 0:
            v = 1.0 / (1.0 - q + q * xc[d - 1])
            scl[d], tau2[d], sig2[d] = v, v * t, v * s
            delta = v * q * xc[d - 1]
        else:
            scl[d], tau2[d], sig2[d] = zero, zero, zero
    ls_m, le_m, rs_m, re_m = own
    beta, delta = bet[me], dlt[me]
    a, b = 1.0 - beta * ls_m, 1.0 - delta * re_m
    o1, o2 = beta * rs_m, delta * le_m
    inv = 1.0 / (a * b - o1 * o2)
    kk[0], kk[1], kk[2], kk[3] = b * inv, o1 * inv, a * inv, o2 * inv


def work(nx, ny, f_hbm, p_hbm, x_hbm, y_hbm, z_hbm, d_hbm, op_ref, or_ref, oc_ref,
           xl_s, xc_s, yl_s, yc_s, zl_s, zt_s, zd_s, fo_s, p_s, r_s, g_s, q_s,
           ct_s, rt_s, gt_s, lx_s, rx_s, ix_s, wx_s, ly_s, ry_s, iy_s, wy_s,
           sx0, sy0, hx, hy, xb, sxb, xb1, sx1, ycb, syc, yb0, yb1, shy,
           xown, xrho, xtau, xsig, xbet, xtau2, xsig2, xscl, xdlt, xkk,
           ytau, ysig, ybet, ytau2, ysig2, ydlt, ykk, ysc,
           pair_s, sel_s, cown, cbuf, wbuf, elr, nbr, pbuf, sxt, xtr, ebuf, sedge, fown, fbuf, flip,
           ins, ssem, s0, sx, sy, sc, sr, sw, sin):
    Y, Z, X = xc_s.shape
    CY, CZ = Y // 2, Z // 2
    f32 = jnp.float32
    gx, gy = lax.axis_index("gx"), lax.axis_index("gy")
    has_w, has_e = gx > 0, gx < nx - 1
    has_n, has_s = gy > 0, gy < ny - 1
    west, east = jnp.maximum(gx - 1, 0), jnp.minimum(gx + 1, nx - 1)
    north, south = jnp.maximum(gy - 1, 0), jnp.minimum(gy + 1, ny - 1)
    x_peers = [(i, gy) for i in farthest_first(gx, nx)]
    y_peers = [(gx, j) for j in flipped(gy, ny)]

    barrier = pltpu.get_barrier_semaphore()
    for dev in y_peers + x_peers:
        pl.semaphore_signal(barrier, inc=1, device_id=dev, device_id_type=MESH)

    stages = ((0, 2), (2, 3), (3, 6))
    sources = (y_hbm, p_hbm, x_hbm, z_hbm, d_hbm, f_hbm)
    for n, (lo, hi) in enumerate(stages):
        for m in range(lo, hi):
            pltpu.make_async_copy(sources[m], ins.at[m], sin.at[n]).start()

    def loaded(n):
        part = ins.at[pl.ds(stages[n][0], stages[n][1] - stages[n][0])]
        pltpu.make_async_copy(part, part, sin.at[n]).wait()

    y_ref, p_ref, x_ref, z_ref, d_ref, f_ref = [ins.at[m] for m in range(6)]

    lane = lax.broadcasted_iota(jnp.int32, (Z, X), 1)
    level = lax.broadcasted_iota(jnp.int32, (Z, X), 0)
    lane3 = lax.broadcasted_iota(jnp.int32, (1, 1, X), 2)

    def rows(ref, j):
        return ref[pl.ds(j, Z, stride=Y), :]

    loaded(0)
    sy0[0] = rows(y_ref, Y - 1)
    sy0[1] = rows(p_ref, Y - 1)
    sy0[2] = rows(p_ref, 0)

    pl.semaphore_wait(barrier, (nx - 1) + (ny - 1))

    comm = Comm(ssem)
    comm.send(sy0.at[0:2], hy.at[0:2], s0.at[1], (gx, south), has_s)
    comm.send(sy0.at[2:3], hy.at[2:3], s0.at[1], (gx, north), has_n)

    loaded(1)
    packed = jnp.zeros((Z, X), f32)
    for j in range(Y):
        v = rows(x_ref, j)
        xc_s[j] = v
        packed = jnp.where(lane == SLOTS * j + XC, v[:, X - 1:], packed)
    sx0[...] = packed
    comm.send(sx0, hx, s0.at[0], (east, gy), has_e)

    for j in range(Y):
        yc_s[j] = rows(y_ref, j)
        p_s[j] = rows(p_ref, j)
    loaded(2)
    for j in range(Y):
        zv = jnp.where(level < Z - 1, rows(z_ref, j), 0.0)
        zt_s[j] = zv
        zl = pltpu.roll(zv, 1, 0)
        zl_s[j] = zl
        zd_s[j] = zv + zl + rows(d_ref, j)
        fo_s[j] = rows(f_ref, j)

    to_sides = (((gx, south), has_s, has_n), ((gx, north), has_n, has_s))
    per, groups, blocks = X // Z, Y * Z // X, X // 8
    sub = lax.broadcasted_iota(jnp.int32, (8, X), 0)

    def turned(ref, g):
        return ref[g * per:(g + 1) * per].reshape(X, X).T

    def split(v):
        return [v[8 * k:8 * k + 8] for k in range(blocks)]

    def shift(v, s, fill):
        if s % 8 == 0:
            m = s // 8
            return [v[k - m] if 0 <= k - m < blocks else fill for k in range(blocks)]
        turn = [pltpu.roll(u, s % 8, 0) for u in v]
        if s > 0:
            return [jnp.where(sub < s, fill if k == 0 else turn[k - 1], turn[k]) for k in range(blocks)]
        return [jnp.where(sub >= 8 + s, fill if k == blocks - 1 else turn[k + 1], turn[k]) for k in range(blocks)]

    def scaled(u, v):
        return [a if b is None else b if a is None else a * b for a, b in zip(u, v)]

    def added(u, v):
        return [a if b is None else a + b for a, b in zip(u, v)]

    def fill_of(s, value):
        return None if s % 8 == 0 else value

    def store(ref, at, v):
        for k in range(blocks):
            ref[at + (slice(8 * k, 8 * k + 8),)] = v[k]

    def load(ref, at):
        return [ref[at + (slice(8 * k, 8 * k + 8),)] for k in range(blocks)]

    xsteps = strides_of(X)

    def x_factor(g):
        c = load(ct_s, (g,))
        a = shift(c, 1, 1.0)
        for j in range(g * per, (g + 1) * per):
            g_s[j] = yl_s[j] + yc_s[j] + zd_s[j]
        e = split(turned(g_s, g))
        for n, s in enumerate(xsteps):
            inv = [1.0 / (u + v + w) for u, v, w in zip(a, c, e)]
            ai, ci = scaled(a, inv), scaled(c, inv)
            store(wx_s, (n, 0, g), ci)
            store(wx_s, (n, 1, g), ai)
            ae, ce = scaled(ai, e), scaled(ci, e)
            a = scaled(a, shift(ai, s, fill_of(s, 1.0)))
            c = scaled(c, shift(ci, -s, fill_of(s, 1.0)))
            e = added(added(e, shift(ce, s, fill_of(s, 0.0))), shift(ae, -s, fill_of(s, 0.0)))
        inv = [1.0 / (u + v + w) for u, v, w in zip(a, c, e)]
        a, c = scaled(a, inv), scaled(c, inv)
        store(ix_s, (g,), inv)
        store(lx_s, (g,), a)
        store(rx_s, (g,), c)
        one = slice(g, g + 1)
        sxb[LE, one], sxb[LS, one] = a[-1][7:8], a[0][0:1]
        sxb[RE, one], sxb[RS, one] = c[-1][7:8], c[0][0:1]
        sxb[XC, one] = ct_s[g, X - 1:X]

    def edge_sums(g):
        r = split(turned(r_s, g))
        store(rt_s, (g,), r)
        out = []
        for ref in (lx_s, rx_s):
            v = scaled(load(ref, (g,)), r)
            while len(v) > 1:
                v = [a + b for a, b in zip(v[0::2], v[1::2])]
            out.append(jnp.sum(v[0], axis=0, keepdims=True))
        return out

    def z_terms(v, part):
        return zl_s[part] * pltpu.roll(v, 1, 1) + zt_s[part] * pltpu.roll(v, Z - 1, 1)

    def x_source(lo, hi, lower, upper):
        part = slice(lo, hi)
        r_s[part] = fo_s[part] + yl_s[part] * lower + yc_s[part] * upper + z_terms(p_s[part], part)

    for g in range(groups):
        store(ct_s, (g,), split(turned(xc_s, g)))
    yl_s[1:Y] = yc_s[0:Y - 1]
    for g in range(1, groups):
        x_factor(g)
    x_source(1, Y - 1, p_s[0:Y - 2], p_s[2:Y])

    @pl.when(jnp.logical_not(has_w))
    def _():
        hx[...] = jnp.zeros_like(hx)
        cbuf[0] = jnp.zeros_like(cbuf[0])
        ebuf[0] = jnp.zeros_like(ebuf[0])

    @pl.when(jnp.logical_not(has_e))
    def _():
        cbuf[2] = jnp.zeros_like(cbuf[2])
        ebuf[1] = jnp.zeros_like(ebuf[1])

    @pl.when(jnp.logical_not(has_n))
    def _():
        hy[0:2] = jnp.zeros_like(hy[0:2])
        nbr[0] = jnp.zeros_like(nbr[0])
        pbuf[0:2] = jnp.zeros_like(pbuf[0:2])
        xtr[0] = jnp.zeros_like(xtr[0])
        for d in range(3):
            cbuf[d, :, 0:3] = jnp.zeros_like(cbuf[d, :, 0:3])

    @pl.when(jnp.logical_not(has_s))
    def _():
        hy[2] = jnp.zeros_like(hy[2])
        nbr[1] = jnp.zeros_like(nbr[1])
        pbuf[CY + 2:] = jnp.zeros_like(pbuf[CY + 2:])
        xtr[1] = jnp.zeros_like(xtr[1])
        for d in range(3):
            cbuf[d, :, 3 + CY:] = jnp.zeros_like(cbuf[d, :, 3 + CY:])

    for n, u in ((True, True), (True, False), (False, True)):
        cond = jnp.logical_and(has_n if n else jnp.logical_not(has_n), has_s if u else jnp.logical_not(has_s))
        part = hy.at[pl.ds(0, (2 if n else 0) + (1 if u else 0))]
        await_recv(part, part, ssem, s0.at[1], (gx, north), cond)

    yl_s[0] = hy[0]
    x_factor(0)
    x_source(0, 1, hy[1:2], p_s[1:2])
    x_source(Y - 1, Y, p_s[Y - 2:Y - 1], hy[2:3])
    for g in range(groups):
        one = slice(g, g + 1)
        sxb[GS, one], sxb[GE, one] = edge_sums(g)
    xb[gx] = sxb[...]
    comm.send_all(lambda dev: sxb, xb.at[gx], sx.at[0], x_peers, xb.at[pl.ds(0, nx - 1)])

    for n, (dev, there, _) in enumerate(to_sides):
        for k, ref in enumerate((xc_s, zt_s)):
            src = ref.at[pl.ds(0 if n else Y - EDGE, EDGE)]
            comm.send(src, nbr.at[n, pl.ds(k * EDGE, EDGE)], sw.at[0], dev, there)

    await_recv(sx0, hx, ssem, s0.at[0], (east, gy), has_w)
    for j in range(Y):
        xl_s[j] = jnp.where(lane == 0, hx[:, SLOTS * j + XC:SLOTS * j + XC + 1], pltpu.roll(xc_s[j], 1, 1))

    ysteps = strides_of(Y)
    for lo in range(0, Z, 8):
        zs = slice(lo, lo + 8)
        a = [yl_s[j, zs] for j in range(Y)]
        c = [yc_s[j, zs] for j in range(Y)]
        e = [xl_s[j, zs] + xc_s[j, zs] + zd_s[j, zs] for j in range(Y)]
        for n, s in enumerate(ysteps):
            inv = [1.0 / (a[j] + c[j] + e[j]) for j in range(Y)]
            ai, ci = [a[j] * inv[j] for j in range(Y)], [c[j] * inv[j] for j in range(Y)]
            for j in range(Y):
                if j + s < Y:
                    wy_s[n, 0, j, zs] = ci[j]
                if j >= s:
                    wy_s[n, 1, j, zs] = ai[j]
            e2 = []
            for j in range(Y):
                v = e[j]
                if j >= s:
                    v = v + ci[j - s] * e[j - s]
                if j + s < Y:
                    v = v + ai[j + s] * e[j + s]
                e2.append(v)
            a = [a[j] * ai[j - s] if j >= s else a[j] for j in range(Y)]
            c = [c[j] * ci[j + s] if j + s < Y else c[j] for j in range(Y)]
            e = e2
        for j in range(Y):
            inv = 1.0 / (a[j] + c[j] + e[j])
            iy_s[j, zs], ly_s[j, zs], ry_s[j, zs] = inv, a[j] * inv, c[j] * inv

    k_top, k_end = jnp.sqrt(yl_s[0]), jnp.sqrt(yc_s[Y - 1])
    i_top = jnp.where(has_n, 1.0 / jnp.where(has_n, k_top, 1.0), 0.0)
    ysc[0], ysc[1] = i_top, 1.0 / k_end
    syc[0], syc[1], syc[2] = ly_s[0], ly_s[Y - 1] * k_end * i_top, ry_s[Y - 1]
    ycb[gy] = syc[...]
    comm.send_all(lambda dev: syc, ycb.at[gy], sy.at[2], y_peers, ycb.at[pl.ds(0, ny - 1)])

    def x_local():
        for g in range(groups):
            r = load(rt_s, (g,))
            for n, s in enumerate(xsteps):
                low = shift(scaled(load(wx_s, (n, 0, g)), r), s, fill_of(s, 0.0))
                high = shift(scaled(load(wx_s, (n, 1, g)), r), -s, fill_of(s, 0.0))
                r = added(added(r, low), high)
            store(gt_s, (g,), scaled(r, load(ix_s, (g,))))

    def y_local():
        for lo in range(0, Z, 8):
            zs = slice(lo, lo + 8)
            r = [r_s[j, zs] for j in range(Y)]
            for n, s in enumerate(ysteps):
                low = [wy_s[n, 0, j, zs] * r[j] if j + s < Y else None for j in range(Y)]
                high = [wy_s[n, 1, j, zs] * r[j] if j >= s else None for j in range(Y)]
                r2 = []
                for j in range(Y):
                    v = r[j]
                    if j >= s:
                        v = v + low[j - s]
                    if j + s < Y:
                        v = v + high[j + s]
                    r2.append(v)
                r = r2
            for j in range(Y):
                g_s[j, zs] = r[j] * iy_s[j, zs]

    x_local()

    half = X // 2
    off = half // 2
    ii = lax.broadcasted_iota(jnp.int32, (X, X), 0)
    mm = lax.broadcasted_iota(jnp.int32, (X, X), 1)

    def selection(step, start):
        target = lax.rem((ii + (step + 2)) // 2 - 1 + start + X, X)
        return jnp.where(mm == target, 0.125, 0.0)

    def level_pairs(n, levels):
        for k, v in enumerate(levels):
            pair_s[n, k * Z:(k + 1) * Z] = v
        count = len(levels) * CZ
        return pair_s[n, pl.ds(0, count, stride=2), :] + pair_s[n, pl.ds(1, count, stride=2), :]

    def pairs(n, field):
        return level_pairs(n, [field(2 * k) + field(2 * k + 1) for k in range(CY)])

    def gathered(parts, first):
        v = jnp.concatenate(parts, axis=1)
        high = v.astype(jnp.bfloat16)
        v = v - high.astype(f32)
        mid = v.astype(jnp.bfloat16)
        low = (v - mid.astype(f32)).astype(jnp.bfloat16)
        sel = sel_s[first * X:(first + len(parts)) * X]
        return sum(jnp.dot(u, sel, preferred_element_type=f32) for u in (low, mid, high))

    for n, sel in enumerate((selection(1, off), selection(-1, off), selection(0, off), selection(0, half + off))):
        sel_s[n * X:(n + 1) * X] = sel.astype(jnp.bfloat16)
    for m, (u, v) in enumerate(((lambda j: xc_s[j], lambda j: yc_s[j]), (lambda j: rows(z_ref, j), lambda j: rows(d_ref, j)))):
        part = gathered([pairs(0, u), pairs(1, v)], 2).reshape(CY, CZ, X)
        cown[m] = part
        cbuf[1, m, 3:3 + CY] = part

    def operator(at, xc, xl, zl, zt, sides):
        for n, (u, v) in enumerate(sides):
            wbuf[at, n] = xc[0] * u + xc[1] * v
            wbuf[at, 2 + n] = xl[0] * u + xl[1] * v
            wbuf[at, 4 + n] = zl[0] * pltpu.roll(u, 1, 0) + zl[1] * pltpu.roll(v, 1, 0)
            wbuf[at, 6 + n] = zt[0] * pltpu.roll(u, Z - 1, 0) + zt[1] * pltpu.roll(v, Z - 1, 0)

    for k in range(EDGE):
        for n, j in enumerate((Y - EDGE + k, k)):
            elr[n, k], elr[n, EDGE + k] = ly_s[j] * ysc[0], ry_s[j] * ysc[1]
    for n in range(2):
        elr[n, 2 * EDGE] = hx[...]
    for k in range(CY):
        two = (2 * k, 2 * k + 1)
        operator(2 + k, *[[ref[j] for j in two] for ref in (xc_s, xl_s, zl_s, zt_s)],
                 [[ref[j] * ysc[n] for j in two] for n, ref in enumerate((ly_s, ry_s))])

    def edge_columns():
        for n, (dev, there, _) in enumerate(to_sides):
            comm.send(elr.at[n], nbr.at[n, pl.ds(2 * EDGE, 2 * EDGE + 1)], sw.at[0], dev, there)

    def edge_operators():
        await_sides(nbr, sw.at[0], (gx, north), has_n, has_s)
        for n, first in enumerate((Y - EDGE, 0)):
            for k in range(0, EDGE, 2):
                xc = [nbr[n, k + i] for i in range(2)]
                zt = [nbr[n, EDGE + k + i] for i in range(2)]
                cols = [SLOTS * (first + k + i) + XC for i in range(2)]
                xl = [jnp.where(lane == 0, nbr[n, 4 * EDGE, :, c:c + 1], pltpu.roll(v, 1, 1)) for c, v in zip(cols, xc)]
                operator(n * (CY + 2) + k // 2, xc, xl, [pltpu.roll(v, 1, 0) for v in zt], zt,
                         [[nbr[n, (2 + m) * EDGE + k + i] for i in range(2)] for m in range(2)])

    def edge_rows():
        for dev, there, src, dst in (((gx, north), has_n, 2, CY + 2), ((gx, south), has_s, CY, 0)):
            comm.send(pbuf.at[pl.ds(src, 2)], pbuf.at[pl.ds(dst, 2)], sw.at[2], dev, there)

    def coarse_send(straight):
        for i, ok, back in ((west, has_w, 2), (gx, None, 1), (east, has_e, 0)):
            both = (lambda c: c) if ok is None else (lambda c, ok=ok: jnp.logical_and(c, ok))
            if straight:
                if ok is not None:
                    comm.send(cown, cbuf.at[back, :, pl.ds(3, CY)], sc.at[back], (i, gy), ok)
            else:
                comm.send(cown.at[:, pl.ds(CY - 3, 3)], cbuf.at[back, :, pl.ds(0, 3)], sc.at[back], (i, south), both(has_s))
                comm.send(cown.at[:, pl.ds(0, 2)], cbuf.at[back, :, pl.ds(3 + CY, 2)], sc.at[back], (i, north), both(has_n))

    def coarse_wait():
        for slot, i, ok in ((0, west, has_w), (1, gx, None), (2, east, has_e)):
            kept = 0 if ok is None else CY
            for n, s in ((True, True), (True, False), (False, True)):
                cond = jnp.logical_and(has_n if n else jnp.logical_not(has_n), has_s if s else jnp.logical_not(has_s))
                cond = cond if ok is None else jnp.logical_and(cond, ok)
                part = cbuf.at[slot, :, pl.ds(0, kept + (3 if n else 0) + (2 if s else 0))]
                await_recv(part, part, ssem, sc.at[slot], (i, gy), cond)

    def x_solve(hl, hr, gs, ge):
        alpha = jnp.zeros((groups, X), f32)
        for d in range(nx - 1):
            alpha = jnp.where(d < gx, hl(d) + xtau[d] * alpha, alpha)
        gamma = jnp.zeros((groups, X), f32)
        for d in reversed(range(1, nx)):
            gamma = jnp.where(d > gx, hr(d) + xtau2[d] * gamma, gamma)
        p = xrho[gx] * alpha + xbet[gx] * gs
        q = gamma + xdlt[gx] * ge
        return xkk[0] * p + xkk[1] * q, xkk[2] * q + xkk[3] * p

    def x_first():
        await_all(xb.at[pl.ds(0, nx - 1)], sx.at[0], x_peers[0])
        cut = [[xb[d, k] for d in range(nx)] for k in range(XC + 1)]
        own = [sxb[k] for k in range(XC + 1)]
        inv = [1.0 / v for v in cut[XC]]
        ge = [cut[GE][d] * inv[d] for d in range(nx)]
        gs = cut[GS]
        xown[0] = 1.0 / own[XC]
        chain_factor(nx, gx, cut[LS], cut[LE], cut[RS], cut[RE], cut[XC], [own[LS], own[LE], own[RS], own[RE]],
                     xrho, xtau, xsig, xbet, xtau2, xsig2, xscl, xdlt, xkk)
        return x_solve(
            lambda d: ge[d] + xsig[d] * gs[d], lambda d: xscl[d] * gs[d] + xsig2[d] * ge[d], own[GS], own[GE] * xown[0]
        )

    def x_second():
        sums = [edge_sums(g) for g in range(groups)]
        gs, ge = [jnp.concatenate([v[n] for v in sums], axis=0) for n in range(2)]
        ge = ge * xown[0]
        sx1[0], sx1[1] = ge + xsig[gx] * gs, xscl[gx] * gs + xsig2[gx] * ge
        comm.send_all(
            lambda dev: sx1.at[jnp.where(dev[0] > gx, 0, 1)], xb1.at[gx], sx.at[1], x_peers, xb1.at[pl.ds(0, nx - 1)]
        )
        coarse_send(False)
        edge_columns()
        x_local()
        await_all(xb1.at[pl.ds(0, nx - 1)], sx.at[1], x_peers[0])
        return x_solve(lambda d: xb1[d], lambda d: xb1[d], gs, ge)

    def y_half(m, left, right):
        top, end = jnp.zeros((Z, X), f32), jnp.zeros((Z, X), f32)
        for g in range(groups):
            u, w = left[g:g + 1], right[g:g + 1]
            c, v = load(ct_s, (g,)), []
            for a, b, d in zip(load(gt_s, (g,)), load(lx_s, (g,)), load(rx_s, (g,))):
                v.append(a + b * u + d * w)
            edge = u + (xrho[gx][g:g + 1] - 1.0) * v[0][0:1]
            t = added(shift(scaled(c, v), 1, edge), scaled(c, shift(v, -1, w)))
            v = jnp.concatenate(v, axis=0).T.reshape(per, Z, X)
            t = jnp.concatenate(t, axis=0).T.reshape(per, Z, X)
            for n in range(per):
                j = g * per + n
                q_s[j] = v[n]
                r = fo_s[j] + t[n] + zl_s[j] * pltpu.roll(v[n], 1, 0) + zt_s[j] * pltpu.roll(v[n], Z - 1, 0)
                r_s[j] = r
                top, end = top + ly_s[j] * r, end + ry_s[j] * r
        top, end = top * ysc[0], end * ysc[1]
        if m == 0:
            shy[0, 0], shy[0, 1] = top, end
            yb0[gy] = shy[0]
            comm.send_all(lambda dev: shy.at[0], yb0.at[gy], sy.at[0], y_peers, yb0.at[pl.ds(0, ny - 1)])
        else:
            shy[1, 0] = end + ysig[gy] * top
            shy[1, 1] = top + ysig2[gy] * end
            yb1[gy] = shy[1, 0]
            comm.send_all(
                lambda dev: shy.at[1, jnp.where(dev[1] > gy, 0, 1)], yb1.at[gy], sy.at[1], y_peers, yb1.at[pl.ds(0, ny - 1)]
            )
        if m:
            sxt[0], sxt[1] = end, top
            comm.send(sxt.at[0], xtr.at[1], sw.at[1], (gx, north), has_n)
            comm.send(sxt.at[1], xtr.at[0], sw.at[1], (gx, south), has_s)
        y_local()
        if m == 0:
            coarse_send(True)
            await_all(ycb.at[pl.ds(0, ny - 1)], sy.at[2], y_peers[0])
            ls, mid, re = [[ycb[d, k] for d in range(ny)] for k in range(3)]
            interface_factor(
                ny, gy, ls, mid, mid, re, [syc[0], syc[1], syc[1], syc[2]],
                ytau, ysig, ybet, ytau2, ysig2, ydlt, ykk,
            )
            comm.finish()
            await_all(yb0.at[pl.ds(0, ny - 1)], sy.at[0], y_peers[0])
            above, below = interface_solve(
                ny, gy, lambda d: yb0[d, 1] + ysig[d] * yb0[d, 0], lambda d: yb0[d, 0] + ysig2[d] * yb0[d, 1],
                top, end, ytau, ytau2, ykk,
            )
            return above * ysc[0], below * ysc[1]
        else:
            for j in range(Y):
                r_s[j] = g_s[j] - q_s[j]
            pbuf[2:CY + 2] = gathered([
                pairs(0, lambda j: xc_s[j] * r_s[j]),
                pairs(1, lambda j: xl_s[j] * r_s[j]),
                pairs(2, lambda j: zl_s[j] * pltpu.roll(r_s[j], 1, 0) + zt_s[j] * pltpu.roll(r_s[j], Z - 1, 0)),
            ], 0).reshape(CY, CZ, X)
            edge_rows()
            comm.finish()
            coarse_wait()
            coefs = planes()
            edge_operators()
        await_all(yb1.at[pl.ds(0, ny - 1)], sy.at[1], y_peers[0])
        above, below = interface_solve(ny, gy, lambda d: yb1[d], lambda d: yb1[d], top, end, ytau, ytau2, ykk)
        await_sides(xtr, sw.at[1], (gx, north), has_n, has_s)
        alpha, gamma = jnp.zeros((Z, X), f32), jnp.zeros((Z, X), f32)
        for d in range(ny - 2):
            alpha = jnp.where(d < gy - 1, yb1[d] + ytau[d] * alpha, alpha)
        for d in reversed(range(2, ny)):
            gamma = jnp.where(d > gy + 1, yb1[d] + ytau2[d] * gamma, gamma)
        q_top = top + syc[0] * above + syc[1] * below
        q_end = end + syc[1] * above + syc[2] * below
        beta, delta = ybet[north], ydlt[south]
        over = (alpha + beta * (xtr[0] + ycb[north, 1] * q_top)) / (1.0 - beta * ycb[north, 0])
        under = (gamma + delta * (xtr[1] + ycb[south, 1] * q_end)) / (1.0 - delta * ycb[south, 2])
        return above, below, coefs, [(over, q_top), (above, below), (q_end, under)]

    centre = jnp.logical_and(lane3 >= off, lane3 < off + half)
    H = CY + 4
    row = lax.broadcasted_iota(jnp.int32, (H, 1, 1), 0)
    inside = jnp.logical_and(
        jnp.logical_or(row >= 2, has_n), jnp.logical_or(row < 2 + CY, has_s)
    )
    inside = jnp.logical_and(
        inside,
        jnp.logical_and(jnp.logical_or(lane3 >= off, has_w), jnp.logical_or(lane3 < off + half, has_e)),
    )

    def planes():
        out = []
        for m in range(2):
            w, o, e = cbuf[0, m], cbuf[1, m], cbuf[2, m]
            out.append(jnp.where(centre, o, pltpu.roll(jnp.where(lane3 >= half, w, e), half, 2)))
            out.append(jnp.where(centre, pltpu.roll(o, half, 2), jnp.where(lane3 < half, w, e)))
        cx, cy, cz, cd = out
        czl = lax.broadcasted_iota(jnp.int32, (1, CZ, 1), 1)
        cyl, cy = cy[:H], cy[1:]
        cx, cz, cd = cx[1:], cz[1:], cd[1:]
        cd = jnp.where(inside, cd, 1.0)
        ct = jnp.where(czl < CZ - 1, cz, 0.0)
        cl = pltpu.roll(ct, 1, 1)
        cxl = pltpu.roll(cx, 1, 2)
        diag = cxl + cx + cyl + cy + cl + ct + cd
        return cx, cxl, cy, cyl, cl, ct, diag, RELAX / diag

    left, right = x_first()
    above, below = y_half(0, left, right)
    p_s[...] = g_s[...] + ly_s[...] * above[None] + ry_s[...] * below[None]
    for lo in range(0, Y, 4):
        hi = lo + 4
        lower = jnp.concatenate([above[None], p_s[0:hi - 1]], axis=0) if lo == 0 else p_s[lo - 1:hi - 1]
        upper = jnp.concatenate([p_s[lo + 1:Y], below[None]], axis=0) if hi == Y else p_s[lo + 1:hi + 1]
        x_source(lo, hi, lower, upper)
    left, right = x_second()
    above, below, coefs, ghosts = y_half(1, left, right)
    cx, cxl, cy, cyl, cl, ct, diag, scale = coefs
    sides = [[], [], []]
    for at in range(H):
        a, b = ghosts[0 if at < 2 else 1 if at < CY + 2 else 2]
        w = [wbuf[at, n] for n in range(8)]
        sides[0].append(w[0] * a + w[1] * b)
        sides[1].append(w[2] * a + w[3] * b)
        a1, b1, a2, b2 = pltpu.roll(a, 1, 0), pltpu.roll(b, 1, 0), pltpu.roll(a, Z - 1, 0), pltpu.roll(b, Z - 1, 0)
        sides[2].append(w[4] * a1 + w[5] * b1 + w[6] * a2 + w[7] * b2)
    partial = gathered([level_pairs(n, v) for n, v in enumerate(sides)], 0).reshape(H, CZ, X)
    await_sides(pbuf.at[pl.ds(0, 4)].reshape(2, 2, CZ, X), sw.at[2], (gx, north), has_n, has_s)
    res = jnp.where(inside, partial + pbuf[...], 0.0)
    clane = lax.broadcasted_iota(jnp.int32, (CZ, X), 1)
    inner = clane % half

    def fringe(v):
        edge = jnp.zeros((CZ, X), f32)
        for r in range(CY):
            edge = jnp.where(inner >= SLOTS * r, pltpu.roll(v[r], half - off + 3 + SLOTS * r, 1), edge)
        return edge

    cor = scale * res
    for repeat in range(COARSE - 1):
        lo, n = 1 + repeat, H - 2 - 2 * repeat
        cut = slice(lo, lo + n)
        mid, over, under = cor[1:-1], cor[:-2], cor[2:]
        applied = (
            diag[cut] * mid
            - cxl[cut] * pltpu.roll(mid, 1, 2)
            - cx[cut] * pltpu.roll(mid, X - 1, 2)
            - cyl[cut] * over
            - cy[cut] * under
            - cl[cut] * pltpu.roll(mid, 1, 1)
            - ct[cut] * pltpu.roll(mid, CZ - 1, 1)
        )
        cor = jnp.where(inside[cut], mid + scale[cut] * (res[cut] - applied), 0.0)
    hj = CY // 2
    fown[0:hj] = jnp.where(lane3 < half, pltpu.roll(cor[:hj], X - off, 2), pltpu.roll(cor[hj:], off, 2))
    fown[hj] = fringe(cor)
    fbuf[gx] = fown[...]
    comm.send_all(lambda dev: fown, fbuf.at[gx], sx.at[0], x_peers, fbuf.at[pl.ds(0, nx - 1)])
    sedge[...] = fringe(res[2:CY + 2])
    comm.send(sedge, ebuf.at[1], sr.at[0], (west, gy), has_w)
    comm.send(sedge, ebuf.at[0], sr.at[0], (east, gy), has_e)
    above, below = above * ysc[0], below * ysc[1]
    for j in range(Y):
        op_ref[pl.ds(j, Z, stride=Y), :] = g_s[j] + ly_s[j] * above + ry_s[j] * below
    comm.finish()
    await_sides(ebuf, sr.at[0], (west, gy), has_w, has_e)
    both = jnp.where(clane < half, ebuf[0], ebuf[1])
    for r in range(CY):
        v = pltpu.roll(both, (off - 3 - SLOTS * r) % X, 1)
        v = res[2 + r] + jnp.where(jnp.logical_or(clane == off, clane == off + half - 1), v, 0.0)
        flip[pl.ds(r, CZ, stride=CY), :] = pltpu.roll(v, X - off, 1)
    or_ref[...] = flip[0:CZ * CY, :half]
    await_all(fbuf.at[pl.ds(0, nx - 1)], sx.at[0], x_peers[0])
    nothing = jnp.zeros((CZ, X), f32)
    edges = [nothing] + [fbuf[d, hj] for d in range(nx)] + [nothing]
    spill = jnp.logical_or(clane >= X - 3, jnp.logical_and(clane >= half, clane < half + 3))
    spill2 = jnp.logical_or(clane < 3, jnp.logical_and(clane >= half - 3, clane < half))
    for t in range(nx // 2):
        u, v = fbuf[2 * t, 0:hj], fbuf[2 * t + 1, 0:hj]
        top = jnp.where(lane3 < half, u, pltpu.roll(v, half, 2))
        low = jnp.where(lane3 < half, pltpu.roll(u, half, 2), v)
        one = jnp.where(clane < half, edges[2 * t + 1], edges[2 * t + 3])
        two = jnp.where(clane < half, edges[2 * t], edges[2 * t + 2])
        base = (t + 1) * CZ * CY
        for j in range(CY):
            turn = (half - 3 - SLOTS * j) % X
            v = top[j] if j < hj else low[j - hj]
            v = v + jnp.where(spill, pltpu.roll(one, turn, 1), 0.0)
            v = v + jnp.where(spill2, pltpu.roll(two, (turn + half) % X, 1), 0.0)
            flip[pl.ds(base + j, CZ, stride=CY), :] = v
        oc_ref[:, t * X:(t + 1) * X] = flip[base:base + CZ * CY, :]
    comm.finish()


def kernel(nx, ny, *refs):
    sems = [pltpu.SemaphoreType.DMA((n,)) for n in (14, 2, 2, 3, 3, 1, 3, 3)]
    pl.run_scoped(functools.partial(work, nx, ny, *refs), *sems)


def put(*refs):
    sems = refs[6]
    give = [pltpu.make_async_copy(refs[m], refs[3 + m], sems.at[m]) for m in range(3)]
    for copy in give:
        copy.start()
    for copy in give:
        copy.wait()


def body(nx, ny, *args):
    Z, Y, X = args[0].shape
    CZ, CY = Z // 2, Y // 2
    flat = [v.reshape(Z * Y, X) for v in args]
    f32 = jnp.float32

    def vm(*shape):
        return pltpu.VMEM(shape, f32)

    block, square, groups = (Y, Z, X), (Y * Z // X, X, X), Y * Z // X
    assert Y * SLOTS <= X and CY * SLOTS <= X // 2 and X % Z == 0 and Y * Z % X == 0 and X % 8 == 0
    nsx, nsy = len(strides_of(X)), len(strides_of(Y))
    assert nx > 1 and ny > 1
    dma = pltpu.SemaphoreType.DMA
    scratch = (
        [vm(*block) for _ in range(12)]
        + [vm(*square) for _ in range(6)] + [vm(nsx, 2, *square), vm(*block), vm(*block), vm(*block), vm(nsy, 2, *block)]
        + [vm(Z, X), vm(3, Z, X), vm(Z, X), vm(3, Z, X)]
        + [vm(nx, XC + 1, groups, X), vm(XC + 1, groups, X), vm(nx, groups, X), vm(2, groups, X)]
        + [vm(ny, 3, Z, X), vm(3, Z, X), vm(ny, 2, Z, X), vm(ny, Z, X), vm(2, 2, Z, X)]
        + [vm(1, groups, X)] + [vm(nx, groups, X) for _ in range(8)] + [vm(4, groups, X)]
        + [vm(ny, Z, X) for _ in range(6)] + [vm(6, Z, X), vm(2, Z, X)]
        + [vm(3, (CY + 4) * Z, X), pltpu.VMEM((4 * X, X), jnp.bfloat16), vm(2, CY, CZ, X), vm(3, 2, CY + 5, CZ, X),
           vm(CY + 4, 8, Z, X), vm(2, 2 * EDGE + 1, Z, X), vm(2, 4 * EDGE + 1, Z, X), vm(CY + 4, CZ, X), vm(2, Z, X), vm(2, Z, X),
           vm(2, CZ, X), vm(CZ, X), vm(CY // 2 + 1, CZ, X), vm(nx, CY // 2 + 1, CZ, X), vm((nx // 2 + 1) * CZ * CY, X)]
        + [vm(6, Z * Y, X)]
    )
    p, r, c = pl.pallas_call(
        functools.partial(kernel, nx, ny),
        out_shape=(
            vm(Z * Y, X),
            vm(CZ * CY, X // 2),
            vm(CZ * CY, nx * X // 2),
        ),
        in_specs=[pl.BlockSpec(memory_space=pltpu.HBM)] * 6,
        out_specs=[pl.BlockSpec(memory_space=pltpu.VMEM)] * 3,
        scratch_shapes=scratch,
        compiler_params=pltpu.CompilerParams(
            collective_id=0, has_side_effects=True, vmem_limit_bytes=60000000
        ),
    )(*flat)
    p, r, c = pl.pallas_call(
        put,
        out_shape=tuple(jax.ShapeDtypeStruct(v.shape, f32) for v in (p, r, c)),
        in_specs=[pl.BlockSpec(memory_space=pltpu.VMEM)] * 3,
        out_specs=[pl.BlockSpec(memory_space=pltpu.HBM)] * 3,
        scratch_shapes=[dma((3,))],
    )(*[pltpu.with_memory_space_constraint(v, pltpu.VMEM) for v in (p, r, c)])
    return p.reshape(Z, Y, X), r.reshape(CZ, CY, X // 2), c.reshape(CZ, CY, nx * X // 2)


def solution(mesh):
    nx, ny = mesh.shape["gx"], mesh.shape["gy"]
    split = P(None, "gy", "gx")
    return jax.shard_map(
        functools.partial(body, nx, ny),
        mesh=mesh,
        in_specs=(split,) * 6,
        out_specs=(split, split, P(None, "gy", None)),
        check_vma=False,
    )
```
